512 devices in a mesh: head: 8 (over x, core), shard: 64 (over y, z).
Axes of the slice: x: 4, y: 4, z: 16, core: 2. Of those that a mesh axis runs over, the one named last changes fastest.
Arguments:
- tokens: bfloat16 [256, 64, 1024], P('shard'), may hold values from -6 to 6
- w_query: bfloat16 [1024, 1024], P(None, 'head'), may hold values from -0.1875 to 0.1875
- w_key: bfloat16 [1024, 1024], P(None, 'head'), may hold values from -0.1875 to 0.1875
- w_value: bfloat16 [1024, 1024], P(None, 'head'), may hold values from -0.1875 to 0.1875
- w_out: bfloat16 [1024, 1024], P('head'), may hold values from -0.1875 to 0.1875
- norm1_gain: float32 [1024], replicated, may hold values from 0.1 to 1.9
- w_inner: bfloat16 [1024, 4096], P(None, 'head'), may hold values from -0.1875 to 0.1875
- w_outer: bfloat16 [4096, 1024], P('head'), may hold values from -0.09375 to 0.09375
- norm2_gain: float32 [1024], replicated, may hold values from 0.1 to 1.9
- w_project: bfloat16 [1024, 128], replicated, may hold values from -0.1875 to 0.1875
- key_pages: bfloat16 [128, 64, 1024], P('shard', None, 'head'), may hold values from -400 to 400
- value_pages: bfloat16 [128, 64, 1024], P('shard', None, 'head'), may hold values from -6 to 6
- page_table: int32 [128], replicated, may hold values from 0 to 127, as said below
- prompt_lengths: int32 [16], replicated, may hold values from 1 to 512
- request_group: int32 [256], P('shard'), may hold values from 0 to 15, as said below
- doc_vectors: bfloat16 [131072, 128], P(('head', 'shard')), may hold values from -0.29882812 to 0.29882812
- doc_lengths: int32 [512, 4], P(('head', 'shard')), may hold values from 1 to 128, 256 in all within a row
- candidates: int32 [256, 16], P('shard'), may hold values from 0 to 2047, as said below
Outputs:
- embedded: bfloat16 [256, 64, 128], P('shard')
- scores: float32 [256, 16], P('shard')
The draws below stay inside these ranges and needn't reach their ends.
Inputs may be any that keep to these rules, and one draw needn't show every extreme that they name: `page_table`: positions g * 8 to g * 8 + 7 list the pages of group g's prompt in order; they are the pages g * 8 to g * 8 + 7 in some order. `request_group`: every group has exactly 16 requests; the 4 requests of one index of shard belong to distinct groups. `candidates`: document d is held by the device of index d // 4 along head+shard. `doc_lengths`: each row holds the token counts of one holder's documents in the order they are packed; a row sums to 256.
All inputs are finite; a program needn't handle non-finite values.
Results may differ from the reference program's by a relative error of at most 0.023.
Values may be sent and summed in bfloat16 or wider, within the bound.
No kernel may reach another device: no remote copies, remote signals or barrier semaphores. Data moves between devices by JAX's collectives and lax.ppermute only.
A program may use at most 64 MiB of HBM per device.

```python
import math
import jax
import jax.numpy as jnp
import numpy as np
from jax import lax

D = 1024
H = 16
DH = 64
FF = 4096
E = 128
Q = 64
R_DEV = 4
C = 16
PAGE = 64
PPG = 8
DLMAX = 128
DTOK_DEV = 256
R = 256
NPAGE = 128
NG = 16
DOC_DEV = 4
DEVICES = 512


def draw_key_pages(key, part):
    key_base = jax.random.fold_in(key, 0)
    return jax.random.normal(key_base, (NPAGE, PAGE, D), jnp.float32).astype(jnp.bfloat16)


def group_order(key_one):
    return jax.random.permutation(key_one, PPG).astype(jnp.int32)


def draw_page_table(key, part):
    group_keys = jax.random.split(jax.random.fold_in(key, 11), NG)
    orders = jax.vmap(group_order)(group_keys)
    return (jnp.arange(NG, dtype=jnp.int32)[:, None] * PPG + orders).reshape(-1).astype(jnp.int32)


def draw_request_group(key, part):
    key_dev, key_label = jax.random.split(jax.random.fold_in(key, 23))
    device_count = R // R_DEV
    device_order = jax.random.permutation(key_dev, device_count).astype(jnp.int32)
    labels = jax.random.permutation(key_label, NG).astype(jnp.int32)
    raw = (device_order[:, None] * R_DEV + jnp.arange(R_DEV, dtype=jnp.int32)[None, :]) % NG
    return jnp.take(labels, raw.reshape(-1), axis=0).astype(jnp.int32)


def draw_candidates(key, part):
    key_rank, key_perm, key_doc = jax.random.split(jax.random.fold_in(key, 37), 3)
    rank_ids = jnp.arange(1, DEVICES + 1, dtype=jnp.int32)
    share = jnp.maximum(jnp.int32(1048576) // (rank_ids * rank_ids), 1).astype(jnp.int32)
    bounds = jnp.cumsum(share).astype(jnp.int32)
    pick = jax.random.randint(key_rank, (R, C), 0, bounds[-1], dtype=jnp.int32)
    rank = jnp.sum((pick[..., None] >= bounds[None, None, :]).astype(jnp.int32), axis=-1).astype(jnp.int32)
    holder_order = jax.random.permutation(key_perm, DEVICES).astype(jnp.int32)
    holder = jnp.take(holder_order, rank, axis=0).astype(jnp.int32)
    within = jax.random.randint(key_doc, (R, C), 0, DOC_DEV, dtype=jnp.int32)
    return (holder * DOC_DEV + within).astype(jnp.int32)


def plant(values, rng, smallest, largest):
    dims = values.shape
    spot = [jax.random.randint(jax.random.fold_in(rng, axis), (), 0, dims[axis]) for axis in range(len(dims))]
    values = values.at[tuple(spot)].set(smallest)
    longest = dims.index(max(dims))
    spot[longest] = (spot[longest] + 1) % dims[longest]
    return values.at[tuple(spot)].set(largest)


def level_of(stream_key, shape, pieces, smallest, high):
    loudness = 1.0
    for axis_at, shards_of in pieces:
        heights = jax.random.uniform(jax.random.fold_in(jax.random.fold_in(stream_key, 6), axis_at), (shards_of,), jnp.float32, smallest / len(pieces), high / len(pieces))
        loudness = loudness * jnp.repeat(jnp.exp(heights), shape[axis_at] // shards_of).reshape((-1,) + (1,) * (len(shape) - 1 - axis_at))
    return loudness


def length_profile(count, total, bound, skew):
    portions = [(1 << 20) // math.isqrt(rank ** skew) + 1 for rank in range(2, count + 1)]
    surplus, given = total - bound - (count - 1), [1] * (count - 1)
    while surplus > 0:
        movable = [i for i in range(count - 1) if given[i] < bound]
        whole, remaining = sum([portions[i] for i in movable]), surplus
        for i in movable:
            more = min(bound - given[i], max(1, remaining * portions[i] // whole), surplus)
            given[i] = given[i] + more
            surplus = surplus - more
    return np.array([bound] + given)


def ragged(key, amount, total, bound, skew):
    if amount == 2:
        one = jax.random.randint(key, (), max(1, total - bound), min(bound, total - 1) + 1)
        return jnp.stack([one, total - one])
    tallies = jnp.asarray(length_profile(amount, total, bound, skew), jnp.int32)
    pairs = (amount - 1) // 2
    donor, taker = tallies[1:1 + 2 * pairs:2], tallies[2:2 + 2 * pairs:2]
    slack = jnp.minimum(donor - 1, bound - taker)
    shifted = jax.random.randint(jax.random.fold_in(key, 1), (pairs,), 0, 1 << 20) % (slack + 1)
    tallies = tallies.at[1:1 + 2 * pairs:2].set(donor - shifted).at[2:2 + 2 * pairs:2].set(taker + shifted)
    return tallies[jax.random.permutation(jax.random.fold_in(key, 2), amount)]


def noise(stream_key, dims, width, limit, cuts=(), kind=jnp.bfloat16):
    values = jax.random.normal(stream_key, dims, jnp.float32) * width
    if len(cuts) > 0:
        values = level_of(stream_key, dims, cuts, -0.22, 0.18) * values
    return jnp.clip(values, min=-limit, max=limit).astype(kind)


def setup_inputs(seed: int = 0) -> dict:
    key_of = jax.random.split(jax.random.key(seed), 19)
    tokens = noise(key_of[0], (R, Q, D), 1.0, 6.0, ((0, 64),))
    w_query = noise(key_of[1], (D, D), D ** -0.5, 0.1875, ((1, 8),))
    w_key = noise(key_of[2], (D, D), D ** -0.5, 0.1875, ((1, 8),))
    w_value = noise(key_of[3], (D, D), D ** -0.5, 0.1875, ((1, 8),))
    w_out = noise(key_of[4], (D, D), D ** -0.5, 0.1875, ((0, 8),))
    norm1_gain = jnp.clip(1.0 + 0.18 * jax.random.normal(key_of[5], (D,), jnp.float32), 0.1, 1.9)
    w_inner = noise(key_of[6], (D, FF), D ** -0.5, 0.1875, ((1, 8),))
    w_outer = noise(key_of[7], (FF, D), FF ** -0.5, 0.09375, ((0, 8),))
    norm2_gain = jnp.clip(1.0 + 0.18 * jax.random.normal(key_of[8], (D,), jnp.float32), 0.1, 1.9)
    w_project = noise(key_of[9], (D, E), D ** -0.5, 0.1875)
    key_pages = draw_key_pages(jax.random.fold_in(key_of[18], 71), 0)
    value_pages = noise(key_of[11], (NPAGE, PAGE, D), 1.0, 6.0, ((0, 64), (2, 8)))
    page_table = draw_page_table(jax.random.fold_in(key_of[18], 71), 0)
    prompt_lengths = plant(jax.random.randint(key_of[13], (NG,), 1, PPG * PAGE + 1), jax.random.fold_in(key_of[13], 1), 1, PPG * PAGE).astype(jnp.int32)
    request_group = draw_request_group(jax.random.fold_in(key_of[18], 71), 0)
    doc_vectors = noise(key_of[15], (DEVICES * DTOK_DEV, E), 0.05, 0.29882812, ((0, 512),))
    doc_lengths = jax.vmap(lambda own: ragged(own, DOC_DEV, DTOK_DEV, DLMAX, 2))(jax.random.split(key_of[16], DEVICES)).reshape((DEVICES, DOC_DEV)).astype(jnp.int32)
    candidates = draw_candidates(jax.random.fold_in(key_of[18], 71), 0)
    return {"tokens": tokens, "w_query": w_query, "w_key": w_key, "w_value": w_value, "w_out": w_out, "norm1_gain": norm1_gain, "w_inner": w_inner, "w_outer": w_outer, "norm2_gain": norm2_gain, "w_project": w_project, "key_pages": key_pages, "value_pages": value_pages, "page_table": page_table, "prompt_lengths": prompt_lengths, "request_group": request_group, "doc_vectors": doc_vectors, "doc_lengths": doc_lengths, "candidates": candidates}


def layer_norm(values, norm_gain):
    row_mean = lax.optimization_barrier(jnp.mean(values, axis=-1, keepdims=True))
    row_var = lax.optimization_barrier(jnp.mean(jnp.square(values - row_mean), axis=-1, keepdims=True))
    return (values - row_mean) * lax.rsqrt(row_var + 1e-05) * norm_gain.astype(jnp.float32)

def reference(tokens, w_query, w_key, w_value, w_out, norm1_gain, w_inner, w_outer, norm2_gain, w_project, key_pages, value_pages, page_table, prompt_lengths, request_group, doc_vectors, doc_lengths, candidates):
    token_rows = tokens.reshape(R * Q, D)

    def project(weight):
        out = jnp.dot(token_rows, weight, preferred_element_type=jnp.float32).astype(jnp.bfloat16)
        return out.reshape(R, Q, H, DH)
    queries = project(w_query)
    keys_own = project(w_key)
    values_own = project(w_value)
    page_rows = page_table.reshape(NG, PPG)
    score_scale = 1.0 / math.sqrt(DH)

    def attend(request_data):
        query, key_own, value_own, group = request_data
        pages = page_rows[group]
        key_prompt = key_pages[pages].reshape(PPG * PAGE, H, DH)
        value_prompt = value_pages[pages].reshape(PPG * PAGE, H, DH)
        keys_all = jnp.concatenate([key_prompt, key_own], axis=0)
        values_all = jnp.concatenate([value_prompt, value_own], axis=0)
        is_valid = jnp.concatenate([jnp.arange(PPG * PAGE) < prompt_lengths[group], jnp.ones((Q,), bool)])
        score = jnp.einsum('qhd,khd->hqk', query.astype(jnp.float32), keys_all.astype(jnp.float32)) * score_scale
        score = jnp.where(is_valid[None, None, :], score, -1e+30)
        row_top = lax.optimization_barrier(jnp.max(score, axis=-1, keepdims=True))
        weight = jnp.exp(score - row_top)
        row_total = lax.optimization_barrier(jnp.sum(weight, axis=-1))
        mixed = jnp.einsum('hqk,khd->hqd', weight.astype(jnp.bfloat16).astype(jnp.float32), values_all.astype(jnp.float32))
        mixed = mixed / row_total[:, :, None]
        return jnp.transpose(mixed, (1, 0, 2)).astype(jnp.bfloat16)
    context = lax.map(attend, (queries, keys_own, values_own, request_group)).reshape(R * Q, D)
    attn_out = jnp.dot(context, w_out, preferred_element_type=jnp.float32)
    first = layer_norm(token_rows.astype(jnp.float32) + attn_out, norm1_gain).astype(jnp.bfloat16)
    inner = jnp.dot(first, w_inner, preferred_element_type=jnp.float32)
    active = jax.nn.gelu(inner, approximate=False).astype(jnp.bfloat16)
    outer = jnp.dot(active, w_outer, preferred_element_type=jnp.float32)
    second = layer_norm(first.astype(jnp.float32) + outer, norm2_gain).astype(jnp.bfloat16)
    projected = jnp.dot(second, w_project, preferred_element_type=jnp.float32)
    embedded = (projected * lax.rsqrt(lax.optimization_barrier(jnp.sum(projected * projected, axis=-1, keepdims=True)) + 1e-06)).astype(jnp.bfloat16)
    embedded = embedded.reshape(R, Q, E)
    starts = (jnp.arange(DEVICES, dtype=jnp.int32)[:, None] * DTOK_DEV + jnp.cumsum(doc_lengths, axis=1) - doc_lengths).reshape(-1).astype(jnp.int32)
    flat_lengths = doc_lengths.reshape(-1)

    def match_request(request_data):
        query_vectors, cand_ids = request_data
        tile_index = starts[cand_ids][:, None] + jnp.arange(DLMAX, dtype=jnp.int32)[None, :]
        tile_valid = jnp.arange(DLMAX)[None, :] < flat_lengths[cand_ids][:, None]
        tile_index = jnp.minimum(tile_index, DEVICES * DTOK_DEV - 1).astype(jnp.int32)
        doc_tiles = doc_vectors[tile_index]
        sims = jnp.einsum('qe,cte->qct', query_vectors.astype(jnp.float32), doc_tiles.astype(jnp.float32))
        sims = jnp.where(tile_valid[None], sims, -1e+30)
        return lax.optimization_barrier(jnp.sum(lax.optimization_barrier(jnp.max(sims, axis=-1)), axis=0))
    scores = lax.map(match_request, (embedded, candidates))
    return (embedded, scores)
```

```python
import jax
import jax.numpy as jnp
from jax import lax
from jax.experimental import pallas as pl
from jax.experimental.pallas import tpu as pltpu
from jax.sharding import Mesh, PartitionSpec as P

HEAD = ("x", "c")
SHARD = ("y", "q", "r")
RQ = 4
QL = 64
NC = 16
NROW = RQ * QL
DT = 256
DPAD = 272
XROW = 3 * NROW + 16
BF = jnp.bfloat16
F32 = jnp.float32


def layer_norm(values, norm_gain):
    row_mean = jnp.mean(values, axis=-1, keepdims=True)
    row_var = jnp.mean(jnp.square(values - row_mean), axis=-1, keepdims=True)
    return (values - row_mean) * lax.rsqrt(row_var + 1e-05) * norm_gain


def spread(block, axes, count):
    wide = jnp.broadcast_to(block[None], (count,) + block.shape)
    return lax.all_to_all(wide, axes, 0, 0, tiled=True)


def nt_dot(a, b):
    return lax.dot_general(a, b, (((1,), (1,)), ((), ())), preferred_element_type=F32)


def attend_kernel(group_ref, rows_ref, prompt_ref, bias_ref, out_ref):
    low_half = lax.broadcasted_iota(jnp.int32, (QL, 128), 1) < 64

    def one_request(i, carry):
        src = i // RQ
        row = pl.multiple_of((i % RQ) * QL, QL)
        group = group_ref[i]

        @pl.when(group >= 0)
        def _():
            query = rows_ref[src, pl.ds(row, QL), :]
            zero = jnp.zeros_like(query)
            both = jnp.concatenate(
                [jnp.where(low_half, query, zero), jnp.where(low_half, zero, query)], axis=0
            )
            own_key = rows_ref[src, pl.ds(pl.multiple_of(NROW + row, QL), QL), :]
            own_value = rows_ref[src, pl.ds(pl.multiple_of(2 * NROW + row, QL), QL), :]
            parts = [nt_dot(both, own_key)]
            values = [own_value]
            for piece in range(4):
                start = pl.multiple_of(piece * 1024 + group * 256, 256)
                key = prompt_ref[pl.ds(start, 128), :]
                values.append(prompt_ref[pl.ds(pl.multiple_of(start + 128, 128), 128), :])
                bias = bias_ref[group, :, piece * 128 : (piece + 1) * 128]
                parts.append(nt_dot(both, key) + bias)
            top = jnp.max(parts[0], axis=-1, keepdims=True)
            for part in parts[1:]:
                top = jnp.maximum(top, jnp.max(part, axis=-1, keepdims=True))
            total = jnp.zeros_like(top)
            mixed = jnp.zeros((2 * QL, 128), F32)
            for part, value in zip(parts, values):
                weight = jnp.exp(part - top)
                total = total + jnp.sum(weight, axis=-1, keepdims=True)
                mixed = mixed + jnp.dot(weight.astype(BF), value, preferred_element_type=F32)
            mixed = mixed / total
            out_ref[i] = jnp.where(low_half, mixed[:QL], mixed[QL:]).astype(BF)

        @pl.when(group < 0)
        def _():
            out_ref[i] = jnp.zeros((QL, 128), BF)

        return carry

    lax.fori_loop(0, 16, one_request, 0)


def attend(groups, rows, prompt, bias):
    return pl.pallas_call(
        attend_kernel,
        out_shape=jax.ShapeDtypeStruct((16, QL, 128), BF),
        in_specs=[
            pl.BlockSpec(memory_space=pltpu.SMEM),
            pl.BlockSpec(memory_space=pltpu.VMEM),
            pl.BlockSpec(memory_space=pltpu.VMEM),
            pl.BlockSpec(memory_space=pltpu.VMEM),
        ],
        out_specs=pl.BlockSpec(memory_space=pltpu.VMEM),
        compiler_params=pltpu.CompilerParams(vmem_limit_bytes=32 << 20),
        cost_estimate=pl.CostEstimate(flops=600_000_000, bytes_accessed=2_200_000, transcendentals=1_200_000),
        name="attend",
    )(groups, rows, prompt, bias)


def match_kernel(need_ref, first_ref, last_ref, query_ref, docs_ref, pick_ref, out_ref, sims_ref, best_ref):
    best_ref[...] = jnp.zeros_like(best_ref)
    token = lax.broadcasted_iota(jnp.int32, (DT, 128), 0)

    def one_holder(z, carry):
        base = z * 4
        any_need = need_ref[base] + need_ref[base + 1] + need_ref[base + 2] + need_ref[base + 3]

        @pl.when(any_need > 0)
        def _():
            vectors = docs_ref[pl.ds(pl.multiple_of(z * DPAD, 16), DT), :]
            sims_ref[...] = nt_dot(vectors, query_ref[...])

            def one_doc(k, inner):
                doc = base + k

                @pl.when(need_ref[doc] > 0)
                def _():
                    inside = (token >= first_ref[doc]) & (token < last_ref[doc])
                    tops = []
                    for col in range(8):
                        block = sims_ref[:, col * 128 : (col + 1) * 128]
                        tops.append(jnp.max(jnp.where(inside, block, -1e30), axis=0, keepdims=True))
                    best_ref[doc] = jnp.concatenate(tops, axis=0)

                return inner

            lax.fori_loop(0, 4, one_doc, 0)

        return carry

    lax.fori_loop(0, 16, one_holder, 0)
    lane = lax.broadcasted_iota(jnp.int32, (128, 128), 0)
    request = lax.broadcasted_iota(jnp.int32, (128, 128), 1)
    member = (lane // 32 == request // RQ).astype(F32)
    sums = jnp.dot(
        best_ref[...].reshape(512, 128), member, preferred_element_type=F32, precision=lax.Precision.HIGHEST
    ).reshape(64, 8, 128)
    head = lax.broadcasted_iota(jnp.int32, (64, 8, 128), 1)
    request = lax.broadcasted_iota(jnp.int32, (64, 8, 128), 2)
    per_doc = jnp.sum(jnp.where(head // 2 == request % RQ, sums, 0.0), axis=1)
    doc_row = lax.broadcasted_iota(jnp.int32, (64, 128), 0)
    for c in range(NC):
        hit = doc_row == pick_ref[c : c + 1, :]
        out_ref[c : c + 1, :] = jnp.sum(jnp.where(hit, per_doc, 0.0), axis=0, keepdims=True)


def match(need, first, last, queries, docs, pick):
    return pl.pallas_call(
        match_kernel,
        out_shape=jax.ShapeDtypeStruct((NC, 128), F32),
        in_specs=[pl.BlockSpec(memory_space=pltpu.SMEM)] * 3 + [pl.BlockSpec(memory_space=pltpu.VMEM)] * 3,
        out_specs=pl.BlockSpec(memory_space=pltpu.VMEM),
        scratch_shapes=[pltpu.VMEM((DT, 1024), F32), pltpu.VMEM((64, 8, 128), F32)],
        compiler_params=pltpu.CompilerParams(vmem_limit_bytes=32 << 20),
        cost_estimate=pl.CostEstimate(flops=1_000_000_000, bytes_accessed=1_500_000, transcendentals=0),
        name="match",
    )(need, first, last, queries, docs, pick)


def per_device(
    tokens,
    w_query,
    w_key,
    w_value,
    w_out,
    norm1_gain,
    w_inner,
    w_outer,
    norm2_gain,
    w_project,
    key_pages,
    value_pages,
    page_table,
    prompt_lengths,
    request_group,
    doc_vectors,
    doc_lengths,
    candidates,
):
    my_y = lax.axis_index("y")
    my_head = lax.axis_index(HEAD)
    token_rows = tokens.reshape(NROW, 1024)

    pages = jnp.concatenate([key_pages.reshape(128, 128), value_pages.reshape(128, 128)], axis=0)
    pages_q = lax.all_gather(pages, "q", axis=0, tiled=True)
    w_out_all = lax.all_gather(w_out, HEAD, axis=0, tiled=True)
    pages_q, w_out_all = lax.optimization_barrier((pages_q, w_out_all))
    prompt = lax.all_gather(pages_q, "r", axis=0, tiled=True)

    query = jnp.dot(token_rows, w_query, preferred_element_type=F32).astype(BF) * BF(0.125)
    own_key = jnp.dot(token_rows, w_key, preferred_element_type=F32).astype(BF)
    own_value = jnp.dot(token_rows, w_value, preferred_element_type=F32).astype(BF)
    ids = jnp.concatenate([candidates // 64, candidates % 64, request_group[:, None]], axis=1)
    ids = jnp.pad(ids.astype(BF), ((0, 12), (0, 128 - 33)))
    rows = spread(jnp.concatenate([query, own_key, own_value, ids], axis=0), "y", 4)
    rows = rows.reshape(4, XROW, 128)
    got = rows[:, 3 * NROW : 3 * NROW + RQ, :33].reshape(16, 33).astype(jnp.int32)
    groups = jnp.where(got[:, 32] // 4 == my_y, got[:, 32] % 4, -1)
    pick = jnp.where(got[:, :16] == my_head * 4 + my_y, got[:, 16:32], -1)

    table = lax.dynamic_slice(page_table, (my_y * 32,), (32,)).reshape(4, 8)
    lengths = lax.dynamic_slice(prompt_lengths, (my_y * 4,), (4,))
    page_ids = (my_y * 32 + jnp.arange(32, dtype=jnp.int32)).reshape(4, 8)
    slot = jnp.sum(
        jnp.where(table[:, None, :] == page_ids[:, :, None], jnp.arange(8, dtype=jnp.int32), 0), axis=-1
    )
    position = slot[:, :, None] * 64 + jnp.arange(64, dtype=jnp.int32)
    bias = jnp.where(position < lengths[:, None, None], 0.0, -1e30).astype(F32).reshape(4, 1, 512)

    doc_rows = jnp.pad(doc_lengths.astype(BF), ((0, 15), (0, 124)))
    doc_block = jnp.concatenate([doc_vectors, doc_rows], axis=0)
    doc_block, prompt = lax.optimization_barrier((doc_block, prompt))
    docs = lax.all_gather(doc_block, ("q", "r"), axis=0, tiled=True)

    mixed = attend(groups, rows, prompt, bias)
    back = lax.all_to_all(mixed.reshape(4, NROW, 128), "y", 0, 0, tiled=True)
    context = jnp.sum(back.astype(F32), axis=0).astype(BF)
    context = lax.all_gather(context, HEAD, axis=0, tiled=False)
    context = jnp.transpose(context, (1, 0, 2)).reshape(NROW, 1024)
    attn = jnp.dot(context, w_out_all, preferred_element_type=F32)
    first = layer_norm(token_rows.astype(F32) + attn, norm1_gain).astype(BF)
    inner = jnp.dot(first, w_inner, preferred_element_type=F32)
    active = jax.nn.gelu(inner, approximate=False).astype(BF)
    outer = jnp.dot(active, w_outer, preferred_element_type=F32).astype(BF)
    outer = lax.all_to_all(outer.reshape(8, 32, 1024), HEAD, 0, 0, tiled=True)
    mine = lax.dynamic_slice(first, (my_head * 32, 0), (32, 1024))
    second = layer_norm(mine.astype(F32) + jnp.sum(outer.astype(F32), axis=0), norm2_gain).astype(BF)
    projected = jnp.dot(second, w_project, preferred_element_type=F32)
    embed = (projected * lax.rsqrt(jnp.sum(projected * projected, axis=-1, keepdims=True) + 1e-06)).astype(BF)

    queries = spread(embed, HEAD + ("y",), 32)
    own = lax.dynamic_slice(queries.reshape(8, 4, 32, 128), (0, my_y, 0, 0), (8, 1, 32, 128))
    embedded = own.reshape(RQ, QL, 128)

    doc_len = docs.reshape(16, DPAD, 128)[:, DT, :4].astype(jnp.int32)
    doc_last = jnp.cumsum(doc_len, axis=1)
    doc_first = doc_last - doc_len
    need = jnp.any(
        pick.reshape(1, 256) == jnp.arange(64, dtype=jnp.int32)[:, None], axis=1
    ).astype(jnp.int32)
    pick_lanes = jnp.pad(pick.T, ((0, 0), (0, 112)), constant_values=-1)
    terms = match(
        need, doc_first.reshape(64), doc_last.reshape(64), queries.reshape(1024, 128), docs, pick_lanes
    )
    terms = spread(terms, HEAD + ("y",), 32).reshape(32, NC, 128)
    total = jnp.sum(terms, axis=0)
    scores = lax.dynamic_slice(total, (0, my_y * RQ), (NC, RQ)).T
    return (embedded, scores)


def solution(mesh):
    fine = Mesh(mesh.devices.reshape(4, 2, 4, 4, 4), HEAD + SHARD)
    in_specs = (
        P(SHARD, None, None),
        P(None, HEAD),
        P(None, HEAD),
        P(None, HEAD),
        P(HEAD, None),
        P(),
        P(None, HEAD),
        P(HEAD, None),
        P(),
        P(),
        P(SHARD, None, HEAD),
        P(SHARD, None, HEAD),
        P(),
        P(),
        P(SHARD),
        P(HEAD + SHARD, None),
        P(HEAD + SHARD, None),
        P(SHARD, None),
    )
    out_specs = (P(SHARD, None, None), P(SHARD, None))
    return jax.shard_map(per_device, mesh=fine, in_specs=in_specs, out_specs=out_specs, check_vma=False)
```

```python
import jax
import jax.numpy as jnp
from jax import lax
from jax.experimental import pallas as pl
from jax.experimental.pallas import tpu as pltpu
from jax.sharding import Mesh, PartitionSpec as P

HEAD = ("x", "c")
SHARD = ("y", "q", "r")
RQ = 4
QL = 64
NC = 16
NROW = RQ * QL
DT = 256
DPAD = 640
XROW = 3 * NROW + 16
BF = jnp.bfloat16
F32 = jnp.float32


def layer_norm(values, norm_gain):
    row_mean = jnp.mean(values, axis=-1, keepdims=True)
    row_var = jnp.mean(jnp.square(values - row_mean), axis=-1, keepdims=True)
    return (values - row_mean) * lax.rsqrt(row_var + 1e-05) * norm_gain


def spread(block, axes, count):
    wide = jnp.broadcast_to(block[None], (count,) + block.shape)
    return lax.all_to_all(wide, axes, 0, 0, tiled=True).reshape((-1,) + block.shape[1:])


def nt_dot(a, b):
    return lax.dot_general(a, b, (((1,), (1,)), ((), ())), preferred_element_type=F32)


def attend_kernel(group_ref, rows_ref, prompt_ref, bias_ref, out_ref):
    low_half = lax.broadcasted_iota(jnp.int32, (QL, 128), 1) < 64

    def one_request(i, carry):
        src = i // RQ
        row = pl.multiple_of((i % RQ) * QL, QL)
        group = group_ref[i]

        @pl.when(group >= 0)
        def _():
            query = rows_ref[src, pl.ds(row, QL), :]
            zero = jnp.zeros_like(query)
            both = jnp.concatenate(
                [jnp.where(low_half, query, zero), jnp.where(low_half, zero, query)], axis=0
            )
            own_key = rows_ref[src, pl.ds(pl.multiple_of(NROW + row, QL), QL), :]
            own_value = rows_ref[src, pl.ds(pl.multiple_of(2 * NROW + row, QL), QL), :]
            parts = [nt_dot(both, own_key)]
            values = [own_value]
            for piece in range(4):
                start = pl.multiple_of(piece * 1024 + group * 256, 256)
                key = prompt_ref[pl.ds(start, 128), :]
                values.append(prompt_ref[pl.ds(pl.multiple_of(start + 128, 128), 128), :])
                bias = bias_ref[group, :, piece * 128 : (piece + 1) * 128]
                parts.append(nt_dot(both, key) + bias)
            top = jnp.max(parts[0], axis=-1, keepdims=True)
            for part in parts[1:]:
                top = jnp.maximum(top, jnp.max(part, axis=-1, keepdims=True))
            total = jnp.zeros_like(top)
            mixed = jnp.zeros((2 * QL, 128), F32)
            for part, value in zip(parts, values):
                weight = jnp.exp(part - top)
                total = total + jnp.sum(weight, axis=-1, keepdims=True)
                mixed = mixed + jnp.dot(weight.astype(BF), value, preferred_element_type=F32)
            mixed = mixed / total
            out_ref[i] = jnp.where(low_half, mixed[:QL], mixed[QL:]).astype(BF)

        @pl.when(group < 0)
        def _():
            out_ref[i] = jnp.zeros((QL, 128), BF)

        return carry

    lax.fori_loop(0, 16, one_request, 0)


def attend(groups, rows, prompt, bias):
    return pl.pallas_call(
        attend_kernel,
        out_shape=jax.ShapeDtypeStruct((16, QL, 128), BF),
        in_specs=[
            pl.BlockSpec(memory_space=pltpu.SMEM),
            pl.BlockSpec(memory_space=pltpu.VMEM),
            pl.BlockSpec(memory_space=pltpu.VMEM),
            pl.BlockSpec(memory_space=pltpu.VMEM),
        ],
        out_specs=pl.BlockSpec(memory_space=pltpu.VMEM),
        compiler_params=pltpu.CompilerParams(vmem_limit_bytes=32 << 20),
        cost_estimate=pl.CostEstimate(flops=1000, bytes_accessed=1000, transcendentals=0),
        name="attend",
    )(groups, rows, prompt, bias)


def match_kernel(need_ref, first_ref, last_ref, query_ref, docs_ref, pick_ref, out_ref, sims_ref, best_ref):
    best_ref[...] = jnp.zeros_like(best_ref)
    token = lax.broadcasted_iota(jnp.int32, (DT, 128), 0)

    def one_holder(z, carry):
        base = z * 4
        any_need = need_ref[base] + need_ref[base + 1] + need_ref[base + 2] + need_ref[base + 3]

        @pl.when(any_need > 0)
        def _():
            vectors = docs_ref[pl.ds(pl.multiple_of(z * DT, DT), DT), :]
            sims_ref[...] = nt_dot(vectors, query_ref[...])

            def one_doc(k, inner):
                doc = base + k

                @pl.when(need_ref[doc] > 0)
                def _():
                    inside = (token >= first_ref[doc]) & (token < last_ref[doc])
                    tops = []
                    for col in range(8):
                        block = sims_ref[:, col * 128 : (col + 1) * 128]
                        tops.append(jnp.max(jnp.where(inside, block, -1e30), axis=0, keepdims=True))
                    best_ref[doc] = jnp.concatenate(tops, axis=0)

                return inner

            lax.fori_loop(0, 4, one_doc, 0)

        return carry

    lax.fori_loop(0, 16, one_holder, 0)
    lane = lax.broadcasted_iota(jnp.int32, (128, 128), 0)
    request = lax.broadcasted_iota(jnp.int32, (128, 128), 1)
    member = (lane // 32 == request // RQ).astype(F32)
    sums = jnp.dot(
        best_ref[...].reshape(512, 128), member, preferred_element_type=F32, precision=lax.Precision.HIGHEST
    ).reshape(64, 8, 128)
    head = lax.broadcasted_iota(jnp.int32, (64, 8, 128), 1)
    request = lax.broadcasted_iota(jnp.int32, (64, 8, 128), 2)
    per_doc = jnp.sum(jnp.where(head // 2 == request % RQ, sums, 0.0), axis=1)
    doc_row = lax.broadcasted_iota(jnp.int32, (64, 128), 0)
    for c in range(NC):
        hit = doc_row == pick_ref[c : c + 1, :]
        out_ref[c : c + 1, :] = jnp.sum(jnp.where(hit, per_doc, 0.0), axis=0, keepdims=True)


def match(need, first, last, queries, docs, pick):
    return pl.pallas_call(
        match_kernel,
        out_shape=jax.ShapeDtypeStruct((NC, 128), F32),
        in_specs=[pl.BlockSpec(memory_space=pltpu.SMEM)] * 3 + [pl.BlockSpec(memory_space=pltpu.VMEM)] * 3,
        out_specs=pl.BlockSpec(memory_space=pltpu.VMEM),
        scratch_shapes=[pltpu.VMEM((DT, 1024), F32), pltpu.VMEM((64, 8, 128), F32)],
        compiler_params=pltpu.CompilerParams(vmem_limit_bytes=32 << 20),
        cost_estimate=pl.CostEstimate(flops=1_000_000_000, bytes_accessed=1_500_000, transcendentals=0),
        name="match",
    )(need, first, last, queries, docs, pick)


def per_device(
    tokens,
    w_query,
    w_key,
    w_value,
    w_out,
    norm1_gain,
    w_inner,
    w_outer,
    norm2_gain,
    w_project,
    key_pages,
    value_pages,
    page_table,
    prompt_lengths,
    request_group,
    doc_vectors,
    doc_lengths,
    candidates,
):
    my_y = lax.axis_index("y")
    my_head = lax.axis_index(HEAD)
    token_rows = tokens.reshape(NROW, 1024)

    pages = jnp.concatenate([key_pages.reshape(128, 128), value_pages.reshape(128, 128)], axis=0)
    pages_q = spread(pages, "q", 4)
    prompt = spread(pages_q.reshape(1024, 128), "r", 4)

    w_out_all = lax.all_gather(w_out, HEAD, axis=0, tiled=True)
    doc_rows = jnp.pad(doc_lengths.astype(BF), ((0, DPAD - DT - 1), (0, 124)))
    doc_block = jnp.concatenate([doc_vectors, doc_rows], axis=0)
    docs = lax.all_gather(doc_block, ("q", "r"), axis=0, tiled=True)

    query = jnp.dot(token_rows, w_query, preferred_element_type=F32).astype(BF) * BF(0.125)
    own_key = jnp.dot(token_rows, w_key, preferred_element_type=F32).astype(BF)
    own_value = jnp.dot(token_rows, w_value, preferred_element_type=F32).astype(BF)
    ids = jnp.concatenate([candidates // 64, candidates % 64, request_group[:, None]], axis=1)
    ids = jnp.pad(ids.astype(BF), ((0, 12), (0, 128 - 33)))
    rows = lax.all_gather(jnp.concatenate([query, own_key, own_value, ids], axis=0), "y", axis=0, tiled=True)
    rows = rows.reshape(4, XROW, 128)
    got = rows[:, 3 * NROW : 3 * NROW + RQ, :33].reshape(16, 33).astype(jnp.int32)
    groups = jnp.where(got[:, 32] // 4 == my_y, got[:, 32] % 4, -1)
    pick = jnp.where(got[:, :16] == my_head * 4 + my_y, got[:, 16:32], -1)

    table = lax.dynamic_slice(page_table, (my_y * 32,), (32,)).reshape(4, 8)
    lengths = lax.dynamic_slice(prompt_lengths, (my_y * 4,), (4,))
    page_ids = (my_y * 32 + jnp.arange(32, dtype=jnp.int32)).reshape(4, 8)
    slot = jnp.sum(
        jnp.where(table[:, None, :] == page_ids[:, :, None], jnp.arange(8, dtype=jnp.int32), 0), axis=-1
    )
    position = slot[:, :, None] * 64 + jnp.arange(64, dtype=jnp.int32)
    bias = jnp.where(position < lengths[:, None, None], 0.0, -1e30).astype(F32).reshape(4, 1, 512)

    mixed = attend(groups, rows, prompt, bias)
    back = lax.all_to_all(mixed.reshape(4, NROW, 128), "y", 0, 0, tiled=True)
    context = jnp.sum(back.astype(F32), axis=0).astype(BF)
    context = lax.all_gather(context, HEAD, axis=0, tiled=False)
    context = jnp.transpose(context, (1, 0, 2)).reshape(NROW, 1024)
    attn = jnp.dot(context, w_out_all, preferred_element_type=F32)
    first = layer_norm(token_rows.astype(F32) + attn, norm1_gain).astype(BF)
    inner = jnp.dot(first, w_inner, preferred_element_type=F32)
    active = jax.nn.gelu(inner, approximate=False).astype(BF)
    outer = jnp.dot(active, w_outer, preferred_element_type=F32).astype(BF)
    outer = lax.all_to_all(outer.reshape(8, 32, 1024), HEAD, 0, 0, tiled=True)
    mine = lax.dynamic_slice(first, (my_head * 32, 0), (32, 1024))
    second = layer_norm(mine.astype(F32) + jnp.sum(outer.astype(F32), axis=0), norm2_gain).astype(BF)
    projected = jnp.dot(second, w_project, preferred_element_type=F32)
    embed = (projected * lax.rsqrt(jnp.sum(projected * projected, axis=-1, keepdims=True) + 1e-06)).astype(BF)

    queries = spread(embed, HEAD + ("y",), 32)
    own = lax.dynamic_slice(queries.reshape(8, 4, 32, 128), (0, my_y, 0, 0), (8, 1, 32, 128))
    embedded = own.reshape(RQ, QL, 128)

    docs = docs.reshape(16, DPAD, 128)
    doc_len = docs[:, DT, :4].astype(jnp.int32)
    docs = docs[:, :DT].reshape(16 * DT, 128)
    doc_last = jnp.cumsum(doc_len, axis=1)
    doc_first = doc_last - doc_len
    need = jnp.any(
        pick.reshape(1, 256) == jnp.arange(64, dtype=jnp.int32)[:, None], axis=1
    ).astype(jnp.int32)
    pick_lanes = jnp.pad(pick.T, ((0, 0), (0, 112)), constant_values=-1)
    terms = match(
        need, doc_first.reshape(64), doc_last.reshape(64), queries.reshape(1024, 128), docs, pick_lanes
    )
    terms = spread(terms, HEAD + ("y",), 32).reshape(32, NC, 128)
    total = jnp.sum(terms, axis=0)
    scores = lax.dynamic_slice(total, (0, my_y * RQ), (NC, RQ)).T
    return (embedded, scores)


def solution(mesh):
    fine = Mesh(mesh.devices.reshape(4, 2, 4, 4, 4), HEAD + SHARD)
    in_specs = (
        P(SHARD, None, None),
        P(None, HEAD),
        P(None, HEAD),
        P(None, HEAD),
        P(HEAD, None),
        P(),
        P(None, HEAD),
        P(HEAD, None),
        P(),
        P(),
        P(SHARD, None, HEAD),
        P(SHARD, None, HEAD),
        P(),
        P(),
        P(SHARD),
        P(HEAD + SHARD, None),
        P(HEAD + SHARD, None),
        P(SHARD, None),
    )
    out_specs = (P(SHARD, None, None), P(SHARD, None))
    return jax.shard_map(per_device, mesh=fine, in_specs=in_specs, out_specs=out_specs, check_vma=False)
```

```python
import jax
import jax.numpy as jnp
from jax import lax
from jax.experimental import pallas as pl
from jax.experimental.pallas import tpu as pltpu
from jax.sharding import Mesh, PartitionSpec as P

HEAD = ("x", "c")
SHARD = ("y", "q", "r")
RQ = 4
QL = 64
NC = 16
NROW = RQ * QL
DT = 256
DPAD = 272
XROW = 3 * NROW + 16
BF = jnp.bfloat16
F32 = jnp.float32


def layer_norm(values, norm_gain):
    row_mean = jnp.mean(values, axis=-1, keepdims=True)
    row_var = jnp.mean(jnp.square(values - row_mean), axis=-1, keepdims=True)
    return (values - row_mean) * lax.rsqrt(row_var + 1e-05) * norm_gain


def spread(block, axes, count):
    wide = jnp.broadcast_to(block[None], (count,) + block.shape)
    return lax.all_to_all(wide, axes, 0, 0, tiled=True).reshape((-1,) + block.shape[1:])


def nt_dot(a, b):
    return lax.dot_general(a, b, (((1,), (1,)), ((), ())), preferred_element_type=F32)


def attend_kernel(group_ref, rows_ref, prompt_ref, bias_ref, out_ref):
    low_half = lax.broadcasted_iota(jnp.int32, (QL, 128), 1) < 64

    def one_request(i, carry):
        src = i // RQ
        row = pl.multiple_of((i % RQ) * QL, QL)
        half = (i % RQ) // 2
        place = pl.multiple_of((i % 2) * QL, QL)
        group = group_ref[i]

        @pl.when(group >= 0)
        def _():
            query = rows_ref[src, pl.ds(row, QL), :]
            zero = jnp.zeros_like(query)
            both = jnp.concatenate(
                [jnp.where(low_half, query, zero), jnp.where(low_half, zero, query)], axis=0
            )
            own_key = rows_ref[src, pl.ds(pl.multiple_of(NROW + row, QL), QL), :]
            own_value = rows_ref[src, pl.ds(pl.multiple_of(2 * NROW + row, QL), QL), :]
            parts = [nt_dot(both, own_key)]
            values = [own_value]
            for piece in range(4):
                start = pl.multiple_of(piece * 1024 + group * 256, 256)
                key = prompt_ref[pl.ds(start, 128), :]
                values.append(prompt_ref[pl.ds(pl.multiple_of(start + 128, 128), 128), :])
                bias = bias_ref[group, :, piece * 128 : (piece + 1) * 128]
                parts.append(nt_dot(both, key) + bias)
            top = jnp.max(parts[0], axis=-1, keepdims=True)
            for part in parts[1:]:
                top = jnp.maximum(top, jnp.max(part, axis=-1, keepdims=True))
            total = jnp.zeros_like(top)
            mixed = jnp.zeros((2 * QL, 128), F32)
            for part, value in zip(parts, values):
                weight = jnp.exp(part - top)
                total = total + jnp.sum(weight, axis=-1, keepdims=True)
                mixed = mixed + jnp.dot(weight.astype(BF), value, preferred_element_type=F32)
            mixed = mixed / total
            out_ref[half, src, pl.ds(place, QL), :] = jnp.where(low_half, mixed[:QL], mixed[QL:]).astype(BF)

        @pl.when(group < 0)
        def _():
            out_ref[half, src, pl.ds(place, QL), :] = jnp.zeros((QL, 128), BF)

        return carry

    lax.fori_loop(0, 16, one_request, 0)


def attend(groups, rows, prompt, bias):
    return pl.pallas_call(
        attend_kernel,
        out_shape=jax.ShapeDtypeStruct((2, 4, 2 * QL, 128), BF),
        in_specs=[
            pl.BlockSpec(memory_space=pltpu.SMEM),
            pl.BlockSpec(memory_space=pltpu.VMEM),
            pl.BlockSpec(memory_space=pltpu.VMEM),
            pl.BlockSpec(memory_space=pltpu.VMEM),
        ],
        out_specs=pl.BlockSpec(memory_space=pltpu.VMEM),
        compiler_params=pltpu.CompilerParams(vmem_limit_bytes=16 << 20),
        cost_estimate=pl.CostEstimate(flops=1000, bytes_accessed=1000, transcendentals=0),
        name="attend",
    )(groups, rows, prompt, bias)


def match_kernel(need_ref, first_ref, last_ref, query_ref, docs_ref, pick_ref, out_ref, sims_ref, best_ref, term_ref):
    best_ref[...] = jnp.zeros_like(best_ref)
    token = lax.broadcasted_iota(jnp.int32, (DT, 128), 0)

    def one_holder(z, carry):
        base = z * 4
        any_need = need_ref[base] + need_ref[base + 1] + need_ref[base + 2] + need_ref[base + 3]

        @pl.when(any_need > 0)
        def _():
            vectors = docs_ref[pl.ds(pl.multiple_of(z * DT, DT), DT), :]
            sims_ref[...] = nt_dot(vectors, query_ref[...])

            def one_doc(k, inner):
                doc = base + k

                @pl.when(need_ref[doc] > 0)
                def _():
                    inside = (token >= first_ref[doc]) & (token < last_ref[doc])
                    tops = []
                    for col in range(8):
                        block = sims_ref[:, col * 128 : (col + 1) * 128]
                        tops.append(jnp.max(jnp.where(inside, block, -1e30), axis=0, keepdims=True))
                    best_ref[doc] = jnp.concatenate(tops, axis=0)

                return inner

            lax.fori_loop(0, 4, one_doc, 0)

        return carry

    lax.fori_loop(0, 16, one_holder, 0)
    lane = lax.broadcasted_iota(jnp.int32, (128, 128), 0)
    request = lax.broadcasted_iota(jnp.int32, (128, 128), 1)
    member = (lane // 32 == request // RQ).astype(F32)
    sums = jnp.dot(
        best_ref[...].reshape(512, 128), member, preferred_element_type=F32, precision=lax.Precision.HIGHEST
    ).reshape(64, 8, 128)
    head = lax.broadcasted_iota(jnp.int32, (64, 8, 128), 1)
    request = lax.broadcasted_iota(jnp.int32, (64, 8, 128), 2)
    per_doc = jnp.sum(jnp.where((head % 2) * 2 + head // 4 == request % RQ, sums, 0.0), axis=1)
    doc_row = lax.broadcasted_iota(jnp.int32, (64, 128), 0)
    for c in range(NC):
        hit = doc_row == pick_ref[c : c + 1, :]
        term_ref[c : c + 1, :] = jnp.sum(jnp.where(hit, per_doc, 0.0), axis=0, keepdims=True)
    for i in range(32):
        out_ref[i] = term_ref[...]


def match(need, first, last, queries, docs, pick):
    return pl.pallas_call(
        match_kernel,
        out_shape=jax.ShapeDtypeStruct((32, NC, 128), F32),
        in_specs=[pl.BlockSpec(memory_space=pltpu.SMEM)] * 3 + [pl.BlockSpec(memory_space=pltpu.VMEM)] * 3,
        out_specs=pl.BlockSpec(memory_space=pltpu.VMEM),
        scratch_shapes=[pltpu.VMEM((DT, 1024), F32), pltpu.VMEM((64, 8, 128), F32), pltpu.VMEM((NC, 128), F32)],
        compiler_params=pltpu.CompilerParams(vmem_limit_bytes=16 << 20),
        cost_estimate=pl.CostEstimate(flops=1000, bytes_accessed=1000, transcendentals=0),
        name="match",
    )(need, first, last, queries, docs, pick)


def vmem_call(body, out_shape, name, smem=0):
    def call(*args):
        spaces = [pltpu.SMEM] * smem + [pltpu.VMEM] * (len(args) - smem)
        return pl.pallas_call(
            body,
            out_shape=out_shape,
            in_specs=[pl.BlockSpec(memory_space=space) for space in spaces],
            out_specs=jax.tree.map(lambda _: pl.BlockSpec(memory_space=pltpu.VMEM), out_shape),
            compiler_params=pltpu.CompilerParams(vmem_limit_bytes=16 << 20),
            cost_estimate=pl.CostEstimate(flops=1000, bytes_accessed=1000, transcendentals=0),
            name=name,
        )(*args)

    return call


def dense_kernel(place_ref, context_ref, token_ref, gain_ref, *refs):
    held, first_ref, terms_ref, scratch, sems = refs[:9], refs[9], refs[10], refs[11:20], refs[20]
    copies = [pltpu.make_async_copy(held[i], scratch[i], sems.at[i]) for i in range(9)]
    for copy in copies:
        copy.start()
    w_out_ref, inner_refs, outer_refs = scratch[0], scratch[1:5], scratch[5:9]
    start = pl.multiple_of(place_ref[0] * 128, 128)
    attn = token_ref[pl.ds(start, 128), :].astype(F32)
    copies[0].wait()
    for h in range(8):
        attn = attn + jnp.dot(
            context_ref[h], w_out_ref[h * 128 : (h + 1) * 128, :], preferred_element_type=F32
        )
    first = layer_norm(attn, gain_ref[...]).astype(BF)
    first_ref[...] = first
    for copy in copies[1:]:
        copy.wait()
    total = jnp.zeros((128, 1024), F32)
    for core in range(2):
        inner = jnp.zeros((128, 512), F32)
        for part in range(4):
            inner = inner + jnp.dot(
                first[:, part * 256 : (part + 1) * 256], inner_refs[part][core], preferred_element_type=F32
            )
        active = (0.5 * inner * (1.0 + lax.erf(inner * (0.5**0.5)))).astype(BF)
        for part in range(4):
            total = total + jnp.dot(
                active[:, part * 128 : (part + 1) * 128], outer_refs[part][core], preferred_element_type=F32
            )
    terms_ref[...] = total.astype(BF).reshape(4, 32, 1024)


def dense(place, context, tokens, gain, weights):
    return pl.pallas_call(
        dense_kernel,
        out_shape=(jax.ShapeDtypeStruct((128, 1024), BF), jax.ShapeDtypeStruct((4, 32, 1024), BF)),
        in_specs=[pl.BlockSpec(memory_space=pltpu.SMEM)]
        + [pl.BlockSpec(memory_space=pltpu.VMEM)] * 3
        + [pl.BlockSpec(memory_space=pl.ANY)] * 9,
        out_specs=(pl.BlockSpec(memory_space=pltpu.VMEM), pl.BlockSpec(memory_space=pltpu.VMEM)),
        scratch_shapes=[pltpu.VMEM(w.shape, w.dtype) for w in weights] + [pltpu.SemaphoreType.DMA((9,))],
        compiler_params=pltpu.CompilerParams(vmem_limit_bytes=20 << 20),
        cost_estimate=pl.CostEstimate(flops=1000, bytes_accessed=1000, transcendentals=0),
        name="dense",
    )(place, context, tokens, gain, *weights)


def embed_kernel(place_ref, first_ref, terms_ref, gain_ref, w_project_ref, out_ref):
    start = pl.multiple_of(place_ref[0] * 32, 32)
    total = first_ref[pl.ds(start, 32), :].astype(F32)
    for x in range(4):
        total = total + terms_ref[x].astype(F32)
    second = layer_norm(total, gain_ref[...]).astype(BF)
    projected = jnp.dot(second, w_project_ref[...], preferred_element_type=F32)
    scale = lax.rsqrt(jnp.sum(projected * projected, axis=-1, keepdims=True) + 1e-06)
    embed = (projected * scale).astype(BF)
    for i in range(32):
        out_ref[i] = embed


def per_device(
    tokens,
    w_query,
    w_key,
    w_value,
    w_out,
    norm1_gain,
    w_inner,
    w_outer,
    norm2_gain,
    w_project,
    key_pages,
    value_pages,
    page_table,
    prompt_lengths,
    request_group,
    doc_vectors,
    doc_lengths,
    candidates,
):
    my_y = lax.axis_index("y")
    my_head = lax.axis_index(HEAD)
    my_core = lax.axis_index("c").reshape(1)
    my_x = lax.axis_index("x").reshape(1)
    token_rows = tokens.reshape(NROW, 1024)

    pages = jnp.concatenate([key_pages.reshape(128, 128), value_pages.reshape(128, 128)], axis=0)
    pages_q = spread(pages, "q", 4)
    inner_parts = [
        lax.all_gather(w_inner[i * 256 : (i + 1) * 256], "c", axis=0, tiled=False) for i in range(4)
    ]
    outer_parts = [
        lax.all_gather(w_outer[i * 128 : (i + 1) * 128], "c", axis=0, tiled=False) for i in range(4)
    ]

    pages_q, inner_parts, outer_parts = lax.optimization_barrier((pages_q, inner_parts, outer_parts))
    prompt = spread(pages_q.reshape(1024, 128), "r", 4)

    w_out_all = lax.all_gather(w_out, HEAD, axis=0, tiled=True)
    doc_rows = jnp.pad(doc_lengths.astype(BF), ((0, DPAD - DT - 1), (0, 124)))
    doc_block = jnp.concatenate([doc_vectors, doc_rows], axis=0)
    docs = lax.all_gather(doc_block, ("q", "r"), axis=0, tiled=True)

    query = jnp.dot(token_rows, w_query, preferred_element_type=F32).astype(BF) * BF(0.125)
    own_key = jnp.dot(token_rows, w_key, preferred_element_type=F32).astype(BF)
    own_value = jnp.dot(token_rows, w_value, preferred_element_type=F32).astype(BF)
    ids = jnp.concatenate([candidates // 64, candidates % 64, request_group[:, None]], axis=1)
    ids = jnp.pad(ids.astype(BF), ((0, 12), (0, 128 - 33)))
    rows = lax.all_gather(jnp.concatenate([query, own_key, own_value, ids], axis=0), "y", axis=0, tiled=True)
    rows = rows.reshape(4, XROW, 128)
    got = rows[:, 3 * NROW : 3 * NROW + RQ, :33].reshape(16, 33).astype(jnp.int32)
    groups = jnp.where(got[:, 32] // 4 == my_y, got[:, 32] % 4, -1)
    pick = jnp.where(got[:, :16] == my_head * 4 + my_y, got[:, 16:32], -1)

    table = lax.dynamic_slice(page_table, (my_y * 32,), (32,)).reshape(4, 8)
    lengths = lax.dynamic_slice(prompt_lengths, (my_y * 4,), (4,))
    page_ids = (my_y * 32 + jnp.arange(32, dtype=jnp.int32)).reshape(4, 8)
    slot = jnp.sum(
        jnp.where(table[:, None, :] == page_ids[:, :, None], jnp.arange(8, dtype=jnp.int32), 0), axis=-1
    )
    position = slot[:, :, None] * 64 + jnp.arange(64, dtype=jnp.int32)
    bias = jnp.where(position < lengths[:, None, None], 0.0, -1e30).astype(F32).reshape(4, 1, 512)

    mixed = attend(groups, rows, prompt, bias)
    back = lax.all_to_all(mixed.reshape(8, 128, 128), ("c", "y"), 0, 0, tiled=True)
    context = jnp.sum(back.reshape(2, 4, 128, 128).astype(F32), axis=1).astype(BF)
    context = lax.all_gather(context, "x", axis=0, tiled=True)
    weights = [w_out_all] + inner_parts + outer_parts
    first, terms = dense(my_core, context, token_rows, norm1_gain[None], weights)
    terms = lax.all_to_all(terms, "x", 0, 0, tiled=True)
    embed = vmem_call(embed_kernel, jax.ShapeDtypeStruct((32, 32, 128), BF), "embed", 1)(
        my_x, first, terms, norm2_gain[None], w_project
    )

    queries = lax.all_to_all(embed, HEAD + ("y",), 0, 0, tiled=True)
    own = lax.dynamic_slice(queries.reshape(4, 2, 4, 32, 128), (0, 0, my_y, 0, 0), (4, 2, 1, 32, 128))
    embedded = jnp.transpose(own, (1, 0, 2, 3, 4)).reshape(RQ, QL, 128)

    docs = docs.reshape(16, DPAD, 128)
    doc_len = docs[:, DT, :4].astype(jnp.int32)
    docs = docs[:, :DT].reshape(16 * DT, 128)
    doc_last = jnp.cumsum(doc_len, axis=1)
    doc_first = doc_last - doc_len
    need = jnp.any(
        pick.reshape(1, 256) == jnp.arange(64, dtype=jnp.int32)[:, None], axis=1
    ).astype(jnp.int32)
    pick_lanes = jnp.pad(pick.T, ((0, 0), (0, 112)), constant_values=-1)
    terms = match(
        need, doc_first.reshape(64), doc_last.reshape(64), queries.reshape(1024, 128), docs, pick_lanes
    )
    terms = lax.all_to_all(terms, HEAD + ("y",), 0, 0, tiled=True)
    total = jnp.sum(terms, axis=0)
    scores = lax.dynamic_slice(total, (0, my_y * RQ), (NC, RQ)).T
    return (embedded, scores)


def solution(mesh):
    fine = Mesh(mesh.devices.reshape(4, 2, 4, 4, 4), HEAD + SHARD)
    in_specs = (
        P(SHARD, None, None),
        P(None, HEAD),
        P(None, HEAD),
        P(None, HEAD),
        P(HEAD, None),
        P(),
        P(None, HEAD),
        P(HEAD, None),
        P(),
        P(),
        P(SHARD, None, HEAD),
        P(SHARD, None, HEAD),
        P(),
        P(),
        P(SHARD),
        P(HEAD + SHARD, None),
        P(HEAD + SHARD, None),
        P(SHARD, None),
    )
    out_specs = (P(SHARD, None, None), P(SHARD, None))
    return jax.shard_map(per_device, mesh=fine, in_specs=in_specs, out_specs=out_specs, check_vma=False)
```

```python
import jax
import jax.numpy as jnp
from jax import lax
from jax.experimental import pallas as pl
from jax.experimental.pallas import tpu as pltpu
from jax.sharding import Mesh, PartitionSpec as P

HEAD = ("x", "c")
SHARD = ("y", "q", "r")
RQ = 4
QL = 64
NC = 16
NROW = RQ * QL
DT = 256
DPAD = 272
XROW = 3 * NROW + 16
BF = jnp.bfloat16
F32 = jnp.float32


def layer_norm(values, norm_gain):
    row_mean = jnp.mean(values, axis=-1, keepdims=True)
    row_var = jnp.mean(jnp.square(values - row_mean), axis=-1, keepdims=True)
    return (values - row_mean) * lax.rsqrt(row_var + 1e-05) * norm_gain


def spread(block, axes, count):
    wide = jnp.broadcast_to(block[None], (count,) + block.shape)
    return lax.all_to_all(wide, axes, 0, 0, tiled=True).reshape((-1,) + block.shape[1:])


def nt_dot(a, b):
    return lax.dot_general(a, b, (((1,), (1,)), ((), ())), preferred_element_type=F32)


def attend_kernel(group_ref, rows_ref, prompt_ref, bias_ref, out_ref):
    low_half = lax.broadcasted_iota(jnp.int32, (QL, 128), 1) < 64

    def one_request(i, carry):
        src = i // RQ
        row = pl.multiple_of((i % RQ) * QL, QL)
        half = (i % RQ) // 2
        place = pl.multiple_of((i % 2) * QL, QL)
        group = group_ref[i]

        @pl.when(group >= 0)
        def _():
            query = rows_ref[src, pl.ds(row, QL), :]
            zero = jnp.zeros_like(query)
            both = jnp.concatenate(
                [jnp.where(low_half, query, zero), jnp.where(low_half, zero, query)], axis=0
            )
            own_key = rows_ref[src, pl.ds(pl.multiple_of(NROW + row, QL), QL), :]
            own_value = rows_ref[src, pl.ds(pl.multiple_of(2 * NROW + row, QL), QL), :]
            parts = [nt_dot(both, own_key)]
            values = [own_value]
            for piece in range(4):
                start = pl.multiple_of(piece * 1024 + group * 256, 256)
                key = prompt_ref[pl.ds(start, 128), :]
                values.append(prompt_ref[pl.ds(pl.multiple_of(start + 128, 128), 128), :])
                bias = bias_ref[group, :, piece * 128 : (piece + 1) * 128]
                parts.append(nt_dot(both, key) + bias)
            top = jnp.max(parts[0], axis=-1, keepdims=True)
            for part in parts[1:]:
                top = jnp.maximum(top, jnp.max(part, axis=-1, keepdims=True))
            total = jnp.zeros_like(top)
            mixed = jnp.zeros((2 * QL, 128), F32)
            for part, value in zip(parts, values):
                weight = jnp.exp(part - top)
                total = total + jnp.sum(weight, axis=-1, keepdims=True)
                mixed = mixed + jnp.dot(weight.astype(BF), value, preferred_element_type=F32)
            mixed = mixed / total
            out_ref[half, src, pl.ds(place, QL), :] = jnp.where(low_half, mixed[:QL], mixed[QL:]).astype(BF)

        @pl.when(group < 0)
        def _():
            out_ref[half, src, pl.ds(place, QL), :] = jnp.zeros((QL, 128), BF)

        return carry

    lax.fori_loop(0, 16, one_request, 0)


def attend(groups, rows, prompt, bias):
    return pl.pallas_call(
        attend_kernel,
        out_shape=jax.ShapeDtypeStruct((2, 4, 2 * QL, 128), BF),
        in_specs=[
            pl.BlockSpec(memory_space=pltpu.SMEM),
            pl.BlockSpec(memory_space=pltpu.VMEM),
            pl.BlockSpec(memory_space=pltpu.VMEM),
            pl.BlockSpec(memory_space=pltpu.VMEM),
        ],
        out_specs=pl.BlockSpec(memory_space=pltpu.VMEM),
        compiler_params=pltpu.CompilerParams(vmem_limit_bytes=16 << 20),
        cost_estimate=pl.CostEstimate(flops=1000, bytes_accessed=1000, transcendentals=0),
        name="attend",
    )(groups, rows, prompt, bias)


def match_kernel(need_ref, first_ref, last_ref, query_ref, docs_ref, pick_ref, out_ref, sims_ref, best_ref, term_ref):
    best_ref[...] = jnp.zeros_like(best_ref)
    token = lax.broadcasted_iota(jnp.int32, (DT, 128), 0)

    def one_holder(z, carry):
        base = z * 4
        any_need = need_ref[base] + need_ref[base + 1] + need_ref[base + 2] + need_ref[base + 3]

        @pl.when(any_need > 0)
        def _():
            vectors = docs_ref[pl.ds(pl.multiple_of(z * DT, DT), DT), :]
            sims_ref[...] = nt_dot(vectors, query_ref[...])

            def one_doc(k, inner):
                doc = base + k

                @pl.when(need_ref[doc] > 0)
                def _():
                    inside = (token >= first_ref[doc]) & (token < last_ref[doc])
                    tops = []
                    for col in range(8):
                        block = sims_ref[:, col * 128 : (col + 1) * 128]
                        tops.append(jnp.max(jnp.where(inside, block, -1e30), axis=0, keepdims=True))
                    best_ref[doc] = jnp.concatenate(tops, axis=0)

                return inner

            lax.fori_loop(0, 4, one_doc, 0)

        return carry

    lax.fori_loop(0, 16, one_holder, 0)
    lane = lax.broadcasted_iota(jnp.int32, (128, 128), 0)
    request = lax.broadcasted_iota(jnp.int32, (128, 128), 1)
    member = (lane // 32 == request // RQ).astype(F32)
    sums = jnp.dot(
        best_ref[...].reshape(512, 128), member, preferred_element_type=F32, precision=lax.Precision.HIGHEST
    ).reshape(64, 8, 128)
    head = lax.broadcasted_iota(jnp.int32, (64, 8, 128), 1)
    request = lax.broadcasted_iota(jnp.int32, (64, 8, 128), 2)
    per_doc = jnp.sum(jnp.where((head % 2) * 2 + head // 4 == request % RQ, sums, 0.0), axis=1)
    doc_row = lax.broadcasted_iota(jnp.int32, (64, 128), 0)
    for c in range(NC):
        hit = doc_row == pick_ref[c : c + 1, :]
        term_ref[c : c + 1, :] = jnp.sum(jnp.where(hit, per_doc, 0.0), axis=0, keepdims=True)
    for i in range(32):
        out_ref[i] = term_ref[...]


def match(need, first, last, queries, docs, pick):
    return pl.pallas_call(
        match_kernel,
        out_shape=jax.ShapeDtypeStruct((32, NC, 128), F32),
        in_specs=[pl.BlockSpec(memory_space=pltpu.SMEM)] * 3 + [pl.BlockSpec(memory_space=pltpu.VMEM)] * 3,
        out_specs=pl.BlockSpec(memory_space=pltpu.VMEM),
        scratch_shapes=[pltpu.VMEM((DT, 1024), F32), pltpu.VMEM((64, 8, 128), F32), pltpu.VMEM((NC, 128), F32)],
        compiler_params=pltpu.CompilerParams(vmem_limit_bytes=16 << 20),
        cost_estimate=pl.CostEstimate(flops=1000, bytes_accessed=1000, transcendentals=0),
        name="match",
    )(need, first, last, queries, docs, pick)


def vmem_call(body, out_shape, name, smem=0):
    def call(*args):
        spaces = [pltpu.SMEM] * smem + [pltpu.VMEM] * (len(args) - smem)
        return pl.pallas_call(
            body,
            out_shape=out_shape,
            in_specs=[pl.BlockSpec(memory_space=space) for space in spaces],
            out_specs=jax.tree.map(lambda _: pl.BlockSpec(memory_space=pltpu.VMEM), out_shape),
            compiler_params=pltpu.CompilerParams(vmem_limit_bytes=16 << 20),
            cost_estimate=pl.CostEstimate(flops=1000, bytes_accessed=1000, transcendentals=0),
            name=name,
        )(*args)

    return call


def dense_kernel(place_ref, context_ref, token_ref, gain_ref, *refs):
    held, first_ref, terms_ref, scratch, sems = refs[:9], refs[9], refs[10], refs[11:20], refs[20]
    copies = [pltpu.make_async_copy(held[i], scratch[i], sems.at[i]) for i in range(9)]
    for copy in copies:
        copy.start()
    w_out_ref, inner_refs, outer_refs = scratch[0], scratch[1:5], scratch[5:9]
    start = pl.multiple_of(place_ref[0] * 128, 128)
    attn = token_ref[pl.ds(start, 128), :].astype(F32)
    copies[0].wait()
    for h in range(8):
        attn = attn + jnp.dot(
            context_ref[h], w_out_ref[h * 128 : (h + 1) * 128, :], preferred_element_type=F32
        )
    first = layer_norm(attn, gain_ref[...]).astype(BF)
    first_ref[...] = first
    for copy in copies[1:]:
        copy.wait()
    total = jnp.zeros((128, 1024), F32)
    for core in range(2):
        inner = jnp.zeros((128, 512), F32)
        for part in range(4):
            inner = inner + jnp.dot(
                first[:, part * 256 : (part + 1) * 256], inner_refs[part][core], preferred_element_type=F32
            )
        active = (0.5 * inner * (1.0 + lax.erf(inner * (0.5**0.5)))).astype(BF)
        for part in range(4):
            total = total + jnp.dot(
                active[:, part * 128 : (part + 1) * 128], outer_refs[part][core], preferred_element_type=F32
            )
    terms_ref[...] = total.astype(BF).reshape(4, 32, 1024)


def dense(place, context, tokens, gain, weights):
    return pl.pallas_call(
        dense_kernel,
        out_shape=(jax.ShapeDtypeStruct((128, 1024), BF), jax.ShapeDtypeStruct((4, 32, 1024), BF)),
        in_specs=[pl.BlockSpec(memory_space=pltpu.SMEM)]
        + [pl.BlockSpec(memory_space=pltpu.VMEM)] * 3
        + [pl.BlockSpec(memory_space=pl.ANY)] * 9,
        out_specs=(pl.BlockSpec(memory_space=pltpu.VMEM), pl.BlockSpec(memory_space=pltpu.VMEM)),
        scratch_shapes=[pltpu.VMEM(w.shape, w.dtype) for w in weights] + [pltpu.SemaphoreType.DMA((9,))],
        compiler_params=pltpu.CompilerParams(vmem_limit_bytes=52 << 20),
        cost_estimate=pl.CostEstimate(flops=1000, bytes_accessed=1000, transcendentals=0),
        name="dense",
    )(place, context, tokens, gain, *weights)


def embed_kernel(place_ref, first_ref, terms_ref, gain_ref, w_project_ref, out_ref):
    start = pl.multiple_of(place_ref[0] * 32, 32)
    total = first_ref[pl.ds(start, 32), :].astype(F32)
    for x in range(4):
        total = total + terms_ref[x].astype(F32)
    second = layer_norm(total, gain_ref[...]).astype(BF)
    projected = jnp.dot(second, w_project_ref[...], preferred_element_type=F32)
    scale = lax.rsqrt(jnp.sum(projected * projected, axis=-1, keepdims=True) + 1e-06)
    embed = (projected * scale).astype(BF)
    for i in range(32):
        out_ref[i] = embed


def per_device(
    tokens,
    w_query,
    w_key,
    w_value,
    w_out,
    norm1_gain,
    w_inner,
    w_outer,
    norm2_gain,
    w_project,
    key_pages,
    value_pages,
    page_table,
    prompt_lengths,
    request_group,
    doc_vectors,
    doc_lengths,
    candidates,
):
    my_y = lax.axis_index("y")
    my_head = lax.axis_index(HEAD)
    my_core = lax.axis_index("c").reshape(1)
    my_x = lax.axis_index("x").reshape(1)
    token_rows = tokens.reshape(NROW, 1024)

    pages = jnp.concatenate([key_pages.reshape(128, 128), value_pages.reshape(128, 128)], axis=0)
    pages_q = spread(pages, "q", 4)
    w_out_all = lax.all_gather(w_out, HEAD, axis=0, tiled=True)
    doc_rows = jnp.pad(doc_lengths.astype(BF), ((0, DPAD - DT - 1), (0, 124)))
    doc_block = jnp.concatenate([doc_vectors, doc_rows], axis=0)
    docs = lax.all_gather(doc_block, ("q", "r"), axis=0, tiled=True)

    query = jnp.dot(token_rows, w_query, preferred_element_type=F32).astype(BF) * BF(0.125)
    own_key = jnp.dot(token_rows, w_key, preferred_element_type=F32).astype(BF)
    own_value = jnp.dot(token_rows, w_value, preferred_element_type=F32).astype(BF)
    ids = jnp.concatenate([candidates // 64, candidates % 64, request_group[:, None]], axis=1)
    ids = jnp.pad(ids.astype(BF), ((0, 12), (0, 128 - 33)))
    rows = lax.all_gather(jnp.concatenate([query, own_key, own_value, ids], axis=0), "y", axis=0, tiled=True)
    pages_q, rows = lax.optimization_barrier((pages_q, rows))
    prompt = spread(pages_q.reshape(1024, 128), "r", 4)

    w_inner, w_outer, pages_q = lax.optimization_barrier((w_inner, w_outer, pages_q))
    inner_parts = [
        lax.all_gather(w_inner[i * 256 : (i + 1) * 256], "c", axis=0, tiled=False) for i in range(4)
    ]
    outer_parts = [
        lax.all_gather(w_outer[i * 128 : (i + 1) * 128], "c", axis=0, tiled=False) for i in range(4)
    ]

    rows = rows.reshape(4, XROW, 128)
    got = rows[:, 3 * NROW : 3 * NROW + RQ, :33].reshape(16, 33).astype(jnp.int32)
    groups = jnp.where(got[:, 32] // 4 == my_y, got[:, 32] % 4, -1)
    pick = jnp.where(got[:, :16] == my_head * 4 + my_y, got[:, 16:32], -1)

    table = lax.dynamic_slice(page_table, (my_y * 32,), (32,)).reshape(4, 8)
    lengths = lax.dynamic_slice(prompt_lengths, (my_y * 4,), (4,))
    page_ids = (my_y * 32 + jnp.arange(32, dtype=jnp.int32)).reshape(4, 8)
    slot = jnp.sum(
        jnp.where(table[:, None, :] == page_ids[:, :, None], jnp.arange(8, dtype=jnp.int32), 0), axis=-1
    )
    position = slot[:, :, None] * 64 + jnp.arange(64, dtype=jnp.int32)
    bias = jnp.where(position < lengths[:, None, None], 0.0, -1e30).astype(F32).reshape(4, 1, 512)

    rows, inner_parts, outer_parts = lax.optimization_barrier((rows, inner_parts, outer_parts))
    mixed = attend(groups, rows, prompt, bias)
    back = lax.all_to_all(mixed.reshape(8, 128, 128), ("c", "y"), 0, 0, tiled=True)
    context = jnp.sum(back.reshape(2, 4, 128, 128).astype(F32), axis=1).astype(BF)
    context = lax.all_gather(context, "x", axis=0, tiled=True)
    weights = [w_out_all] + inner_parts + outer_parts
    first, terms = dense(my_core, context, token_rows, norm1_gain[None], weights)
    terms = lax.all_to_all(terms, "x", 0, 0, tiled=True)
    embed = vmem_call(embed_kernel, jax.ShapeDtypeStruct((32, 32, 128), BF), "embed", 1)(
        my_x, first, terms, norm2_gain[None], w_project
    )

    queries = lax.all_to_all(embed, HEAD + ("y",), 0, 0, tiled=True)
    own = lax.dynamic_slice(queries.reshape(4, 2, 4, 32, 128), (0, 0, my_y, 0, 0), (4, 2, 1, 32, 128))
    embedded = jnp.transpose(own, (1, 0, 2, 3, 4)).reshape(RQ, QL, 128)

    docs = docs.reshape(16, DPAD, 128)
    doc_len = docs[:, DT, :4].astype(jnp.int32)
    docs = docs[:, :DT].reshape(16 * DT, 128)
    doc_last = jnp.cumsum(doc_len, axis=1)
    doc_first = doc_last - doc_len
    need = jnp.any(
        pick.reshape(1, 256) == jnp.arange(64, dtype=jnp.int32)[:, None], axis=1
    ).astype(jnp.int32)
    pick_lanes = jnp.pad(pick.T, ((0, 0), (0, 112)), constant_values=-1)
    terms = match(
        need, doc_first.reshape(64), doc_last.reshape(64), queries.reshape(1024, 128), docs, pick_lanes
    )
    terms = lax.all_to_all(terms, HEAD + ("y",), 0, 0, tiled=True)
    total = jnp.sum(terms, axis=0)
    scores = lax.dynamic_slice(total, (0, my_y * RQ), (NC, RQ)).T
    return (embedded, scores)


def solution(mesh):
    fine = Mesh(mesh.devices.reshape(4, 2, 4, 4, 4), HEAD + SHARD)
    in_specs = (
        P(SHARD, None, None),
        P(None, HEAD),
        P(None, HEAD),
        P(None, HEAD),
        P(HEAD, None),
        P(),
        P(None, HEAD),
        P(HEAD, None),
        P(),
        P(),
        P(SHARD, None, HEAD),
        P(SHARD, None, HEAD),
        P(),
        P(),
        P(SHARD),
        P(HEAD + SHARD, None),
        P(HEAD + SHARD, None),
        P(SHARD, None),
    )
    out_specs = (P(SHARD, None, None), P(SHARD, None))
    return jax.shard_map(per_device, mesh=fine, in_specs=in_specs, out_specs=out_specs, check_vma=False)
```

```python
import jax
import jax.numpy as jnp
from jax import lax
from jax.experimental import pallas as pl
from jax.experimental.pallas import tpu as pltpu
from jax.sharding import Mesh, PartitionSpec as P

HEAD = ("x", "c")
SHARD = ("y", "q", "r")
RQ = 4
QL = 64
NC = 16
NROW = RQ * QL
DT = 256
DPAD = 272
XROW = 3 * NROW + 16
BF = jnp.bfloat16
F32 = jnp.float32


def layer_norm(values, norm_gain):
    row_mean = jnp.mean(values, axis=-1, keepdims=True)
    row_var = jnp.mean(jnp.square(values - row_mean), axis=-1, keepdims=True)
    return (values - row_mean) * lax.rsqrt(row_var + 1e-05) * norm_gain


def spread(block, axes, count):
    wide = jnp.broadcast_to(block[None], (count,) + block.shape)
    return lax.all_to_all(wide, axes, 0, 0, tiled=True).reshape((-1,) + block.shape[1:])


def nt_dot(a, b):
    return lax.dot_general(a, b, (((1,), (1,)), ((), ())), preferred_element_type=F32)


def attend_kernel(group_ref, rows_ref, prompt_ref, bias_ref, out_ref, order_ref):
    low_half = lax.broadcasted_iota(jnp.int32, (QL, 128), 1) < 64
    out_ref[...] = jnp.zeros_like(out_ref)
    count = jnp.int32(0)
    for i in range(16):
        order_ref[count] = jnp.int32(i)
        count = count + (group_ref[i] >= 0).astype(jnp.int32)

    def one_request(i):
        src = i // RQ
        row = pl.multiple_of((i % RQ) * QL, QL)
        group = group_ref[i]
        query = rows_ref[src, pl.ds(row, QL), :]
        zero = jnp.zeros_like(query)
        both = jnp.concatenate(
            [jnp.where(low_half, query, zero), jnp.where(low_half, zero, query)], axis=0
        )
        own_key = rows_ref[src, pl.ds(pl.multiple_of(NROW + row, QL), QL), :]
        own_value = rows_ref[src, pl.ds(pl.multiple_of(2 * NROW + row, QL), QL), :]
        parts = [nt_dot(both, own_key)]
        values = [own_value]
        for piece in range(4):
            start = pl.multiple_of(piece * 1024 + group * 256, 256)
            key = prompt_ref[pl.ds(start, 128), :]
            values.append(prompt_ref[pl.ds(pl.multiple_of(start + 128, 128), 128), :])
            bias = bias_ref[group, :, piece * 128 : (piece + 1) * 128]
            parts.append(nt_dot(both, key) + bias)
        top = jnp.max(parts[0], axis=-1, keepdims=True)
        wide = jnp.maximum(jnp.maximum(parts[1], parts[2]), jnp.maximum(parts[3], parts[4]))
        top = jnp.maximum(top, jnp.max(wide, axis=-1, keepdims=True))
        weights = [jnp.exp(part - top) for part in parts]
        wide = (weights[1] + weights[2]) + (weights[3] + weights[4])
        total = jnp.sum(weights[0], axis=-1, keepdims=True) + jnp.sum(wide, axis=-1, keepdims=True)
        mixed = jnp.zeros((2 * QL, 128), F32)
        for weight, value in zip(weights, values):
            mixed = mixed + jnp.dot(weight.astype(BF), value, preferred_element_type=F32)
        mixed = mixed / total
        return jnp.where(low_half, mixed[:QL], mixed[QL:]).astype(BF)

    def two_requests(step, carry):
        i = order_ref[2 * step]
        k = order_ref[jnp.where(2 * step + 1 < count, 2 * step + 1, 2 * step)]
        results = [one_request(i), one_request(k)]
        for j, result in zip((i, k), results):
            place = pl.multiple_of((j % 2) * QL, QL)
            out_ref[(j % RQ) // 2, j // RQ, pl.ds(place, QL), :] = result
        return carry

    lax.fori_loop(0, (count + 1) // 2, two_requests, 0)


def attend(groups, rows, prompt, bias):
    return pl.pallas_call(
        attend_kernel,
        out_shape=jax.ShapeDtypeStruct((2, 4, 2 * QL, 128), BF),
        in_specs=[
            pl.BlockSpec(memory_space=pltpu.SMEM),
            pl.BlockSpec(memory_space=pltpu.VMEM),
            pl.BlockSpec(memory_space=pltpu.VMEM),
            pl.BlockSpec(memory_space=pltpu.VMEM),
        ],
        out_specs=pl.BlockSpec(memory_space=pltpu.VMEM),
        scratch_shapes=[pltpu.SMEM((17,), jnp.int32)],
        compiler_params=pltpu.CompilerParams(vmem_limit_bytes=16 << 20),
        cost_estimate=pl.CostEstimate(flops=1000, bytes_accessed=1000, transcendentals=0),
        name="attend",
    )(groups, rows, prompt, bias)


def match_kernel(need_ref, first_ref, last_ref, query_ref, docs_ref, pick_ref, out_ref, sims_ref, best_ref, term_ref):
    best_ref[...] = jnp.zeros_like(best_ref)
    token = lax.broadcasted_iota(jnp.int32, (DT, 128), 0)

    def one_holder(z, carry):
        base = z * 4
        any_need = need_ref[base] + need_ref[base + 1] + need_ref[base + 2] + need_ref[base + 3]

        @pl.when(any_need > 0)
        def _():
            vectors = docs_ref[pl.ds(pl.multiple_of(z * DT, DT), DT), :]
            sims_ref[...] = nt_dot(vectors, query_ref[...])

            def one_doc(k, inner):
                doc = base + k

                @pl.when(need_ref[doc] > 0)
                def _():
                    inside = (token >= first_ref[doc]) & (token < last_ref[doc])
                    tops = []
                    for col in range(8):
                        block = sims_ref[:, col * 128 : (col + 1) * 128]
                        tops.append(jnp.max(jnp.where(inside, block, -1e30), axis=0, keepdims=True))
                    best_ref[doc] = jnp.concatenate(tops, axis=0)

                return inner

            lax.fori_loop(0, 4, one_doc, 0)

        return carry

    lax.fori_loop(0, 16, one_holder, 0)
    lane = lax.broadcasted_iota(jnp.int32, (128, 128), 0)
    request = lax.broadcasted_iota(jnp.int32, (128, 128), 1)
    member = (lane // 32 == request // RQ).astype(F32)
    sums = jnp.dot(
        best_ref[...].reshape(512, 128), member, preferred_element_type=F32, precision=lax.Precision.HIGHEST
    ).reshape(64, 8, 128)
    head = lax.broadcasted_iota(jnp.int32, (64, 8, 128), 1)
    request = lax.broadcasted_iota(jnp.int32, (64, 8, 128), 2)
    per_doc = jnp.sum(jnp.where((head % 2) * 2 + head // 4 == request % RQ, sums, 0.0), axis=1)
    doc_row = lax.broadcasted_iota(jnp.int32, (64, 128), 0)
    for c in range(NC):
        hit = doc_row == pick_ref[c : c + 1, :]
        term_ref[c : c + 1, :] = jnp.sum(jnp.where(hit, per_doc, 0.0), axis=0, keepdims=True)
    for i in range(32):
        out_ref[i] = term_ref[...]


def match(need, first, last, queries, docs, pick):
    return pl.pallas_call(
        match_kernel,
        out_shape=jax.ShapeDtypeStruct((32, NC, 128), F32),
        in_specs=[pl.BlockSpec(memory_space=pltpu.SMEM)] * 3 + [pl.BlockSpec(memory_space=pltpu.VMEM)] * 3,
        out_specs=pl.BlockSpec(memory_space=pltpu.VMEM),
        scratch_shapes=[pltpu.VMEM((DT, 1024), F32), pltpu.VMEM((64, 8, 128), F32), pltpu.VMEM((NC, 128), F32)],
        compiler_params=pltpu.CompilerParams(vmem_limit_bytes=16 << 20),
        cost_estimate=pl.CostEstimate(flops=1000, bytes_accessed=1000, transcendentals=0),
        name="match",
    )(need, first, last, queries, docs, pick)


def vmem_call(body, out_shape, name, smem=0):
    def call(*args):
        spaces = [pltpu.SMEM] * smem + [pltpu.VMEM] * (len(args) - smem)
        return pl.pallas_call(
            body,
            out_shape=out_shape,
            in_specs=[pl.BlockSpec(memory_space=space) for space in spaces],
            out_specs=jax.tree.map(lambda _: pl.BlockSpec(memory_space=pltpu.VMEM), out_shape),
            compiler_params=pltpu.CompilerParams(vmem_limit_bytes=16 << 20),
            cost_estimate=pl.CostEstimate(flops=1000, bytes_accessed=1000, transcendentals=0),
            name=name,
        )(*args)

    return call


def pages_kernel(key_ref, value_ref, out_ref, sems):
    copies = []
    for i in range(4):
        for j, ref in enumerate((key_ref, value_ref)):
            target = out_ref.at[i, pl.ds(j * 128, 128), :]
            copies.append(pltpu.make_async_copy(ref, target, sems.at[2 * i + j]))
    for copy in copies:
        copy.start()
    for copy in copies:
        copy.wait()


def repeat_pages(keys, values):
    return pl.pallas_call(
        pages_kernel,
        out_shape=jax.ShapeDtypeStruct((4, 256, 128), BF),
        in_specs=[pl.BlockSpec(memory_space=pl.ANY)] * 2,
        out_specs=pl.BlockSpec(memory_space=pl.ANY),
        scratch_shapes=[pltpu.SemaphoreType.DMA((8,))],
        compiler_params=pltpu.CompilerParams(vmem_limit_bytes=52 << 20),
        cost_estimate=pl.CostEstimate(flops=1000, bytes_accessed=1000, transcendentals=0),
        name="pages",
    )(keys, values)


def total_kernel(place_ref, terms_ref, out_ref):
    total = terms_ref[0]
    for i in range(1, 32):
        total = total + terms_ref[i]
    lane = lax.broadcasted_iota(jnp.int32, (8, 128), 1)
    row = lax.broadcasted_iota(jnp.int32, (8, 128), 0)
    wanted = (lane == place_ref[0] * RQ + row).astype(F32)
    picked = lax.dot_general(
        wanted, total, (((1,), (1,)), ((), ())), preferred_element_type=F32, precision=lax.Precision.HIGHEST
    )
    out_ref[...] = picked[:RQ]


def dense_kernel(place_ref, context_ref, token_ref, gain_ref, *refs):
    held, first_ref, terms_ref, scratch, sems = refs[:9], refs[9], refs[10], refs[11:20], refs[20]
    copies = [pltpu.make_async_copy(held[i], scratch[i], sems.at[i]) for i in range(9)]
    for copy in copies:
        copy.start()
    w_out_ref, inner_refs, outer_refs = scratch[0], scratch[1:5], scratch[5:9]
    start = pl.multiple_of(place_ref[0] * 128, 128)
    attn = token_ref[pl.ds(start, 128), :].astype(F32)
    copies[0].wait()
    for h in range(8):
        attn = attn + jnp.dot(
            context_ref[h], w_out_ref[h * 128 : (h + 1) * 128, :], preferred_element_type=F32
        )
    first = layer_norm(attn, gain_ref[...]).astype(BF)
    first_ref[...] = first
    for copy in copies[1:]:
        copy.wait()
    total = jnp.zeros((128, 1024), F32)
    for core in range(2):
        inner = jnp.zeros((128, 512), F32)
        for part in range(4):
            inner = inner + jnp.dot(
                first[:, part * 256 : (part + 1) * 256], inner_refs[part][core], preferred_element_type=F32
            )
        active = (0.5 * inner * (1.0 + lax.erf(inner * (0.5**0.5)))).astype(BF)
        for part in range(4):
            total = total + jnp.dot(
                active[:, part * 128 : (part + 1) * 128], outer_refs[part][core], preferred_element_type=F32
            )
    terms_ref[...] = total.astype(BF).reshape(4, 32, 1024)


def dense(place, context, tokens, gain, weights):
    return pl.pallas_call(
        dense_kernel,
        out_shape=(jax.ShapeDtypeStruct((128, 1024), BF), jax.ShapeDtypeStruct((4, 32, 1024), BF)),
        in_specs=[pl.BlockSpec(memory_space=pltpu.SMEM)]
        + [pl.BlockSpec(memory_space=pltpu.VMEM)] * 3
        + [pl.BlockSpec(memory_space=pl.ANY)] * 9,
        out_specs=(pl.BlockSpec(memory_space=pltpu.VMEM), pl.BlockSpec(memory_space=pltpu.VMEM)),
        scratch_shapes=[pltpu.VMEM(w.shape, w.dtype) for w in weights] + [pltpu.SemaphoreType.DMA((9,))],
        compiler_params=pltpu.CompilerParams(vmem_limit_bytes=52 << 20),
        cost_estimate=pl.CostEstimate(flops=1000, bytes_accessed=1000, transcendentals=0),
        name="dense",
    )(place, context, tokens, gain, *weights)


def embed_kernel(place_ref, first_ref, terms_ref, gain_ref, w_project_ref, out_ref):
    start = pl.multiple_of(place_ref[0] * 32, 32)
    total = first_ref[pl.ds(start, 32), :].astype(F32)
    for x in range(4):
        total = total + terms_ref[x].astype(F32)
    second = layer_norm(total, gain_ref[...]).astype(BF)
    projected = jnp.dot(second, w_project_ref[...], preferred_element_type=F32)
    scale = lax.rsqrt(jnp.sum(projected * projected, axis=-1, keepdims=True) + 1e-06)
    embed = (projected * scale).astype(BF)
    for i in range(32):
        out_ref[i] = embed


def per_device(
    tokens,
    w_query,
    w_key,
    w_value,
    w_out,
    norm1_gain,
    w_inner,
    w_outer,
    norm2_gain,
    w_project,
    key_pages,
    value_pages,
    page_table,
    prompt_lengths,
    request_group,
    doc_vectors,
    doc_lengths,
    candidates,
):
    my_y = lax.axis_index("y")
    my_head = lax.axis_index(HEAD)
    my_core = lax.axis_index("c").reshape(1)
    my_x = lax.axis_index("x").reshape(1)
    token_rows = tokens.reshape(NROW, 1024)

    pages = repeat_pages(key_pages.reshape(128, 128), value_pages.reshape(128, 128))
    pages_q = lax.all_to_all(pages, "q", 0, 0, tiled=True)

    def both_cores(block, size, parts):
        return [
            lax.all_gather(block[i * size : (i + 1) * size], "c", axis=0, tiled=False) for i in parts
        ]

    inner_parts = both_cores(w_inner, 256, range(4))
    pages_q, inner_parts, w_outer = lax.optimization_barrier((pages_q, inner_parts, w_outer))
    prompt = spread(pages_q.reshape(1024, 128), "r", 4)
    outer_parts = both_cores(w_outer, 128, range(2))

    w_out_all = lax.all_gather(w_out, HEAD, axis=0, tiled=True)
    doc_rows = jnp.pad(doc_lengths.astype(BF), ((0, DPAD - DT - 1), (0, 124)))
    doc_block = jnp.concatenate([doc_vectors, doc_rows], axis=0)
    docs = lax.all_gather(doc_block, ("q", "r"), axis=0, tiled=True)

    query = jnp.dot(token_rows, w_query, preferred_element_type=F32).astype(BF) * BF(0.125)
    own_key = jnp.dot(token_rows, w_key, preferred_element_type=F32).astype(BF)
    own_value = jnp.dot(token_rows, w_value, preferred_element_type=F32).astype(BF)
    ids = jnp.concatenate([candidates // 64, candidates % 64, request_group[:, None]], axis=1)
    ids = jnp.pad(ids.astype(BF), ((0, 12), (0, 128 - 33)))
    rows = jnp.concatenate([query, own_key, own_value, ids], axis=0)
    rows, pages_q = lax.optimization_barrier((rows, pages_q))
    rows = lax.all_gather(rows, "y", axis=0, tiled=True)
    rows = rows.reshape(4, XROW, 128)
    got = rows[:, 3 * NROW : 3 * NROW + RQ, :33].reshape(16, 33).astype(jnp.int32)
    groups = jnp.where(got[:, 32] // 4 == my_y, got[:, 32] % 4, -1)
    pick = jnp.where(got[:, :16] == my_head * 4 + my_y, got[:, 16:32], -1)

    table = lax.dynamic_slice(page_table, (my_y * 32,), (32,)).reshape(4, 8)
    lengths = lax.dynamic_slice(prompt_lengths, (my_y * 4,), (4,))
    page_ids = (my_y * 32 + jnp.arange(32, dtype=jnp.int32)).reshape(4, 8)
    slot = jnp.sum(
        jnp.where(table[:, None, :] == page_ids[:, :, None], jnp.arange(8, dtype=jnp.int32), 0), axis=-1
    )
    position = slot[:, :, None] * 64 + jnp.arange(64, dtype=jnp.int32)
    bias = jnp.where(position < lengths[:, None, None], 0.0, -1e30).astype(F32).reshape(4, 1, 512)

    rows, outer_parts = lax.optimization_barrier((rows, outer_parts))
    mixed = attend(groups, rows, prompt, bias)
    w_outer, mixed = lax.optimization_barrier((w_outer, mixed))
    outer_parts = outer_parts + both_cores(w_outer, 128, range(2, 4))
    back = lax.all_to_all(mixed.reshape(8, 128, 128), ("c", "y"), 0, 0, tiled=True)
    context = jnp.sum(back.reshape(2, 4, 128, 128).astype(F32), axis=1).astype(BF)
    context = lax.all_gather(context, "x", axis=0, tiled=True)
    weights = [w_out_all] + inner_parts + outer_parts
    first, terms = dense(my_core, context, token_rows, norm1_gain[None], weights)
    terms = lax.all_to_all(terms, "x", 0, 0, tiled=True)
    embed = vmem_call(embed_kernel, jax.ShapeDtypeStruct((32, 32, 128), BF), "embed", 1)(
        my_x, first, terms, norm2_gain[None], w_project
    )

    queries = lax.all_to_all(embed, HEAD + ("y",), 0, 0, tiled=True)
    own = lax.dynamic_slice(queries.reshape(4, 2, 4, 32, 128), (0, 0, my_y, 0, 0), (4, 2, 1, 32, 128))
    embedded = jnp.transpose(own, (1, 0, 2, 3, 4)).reshape(RQ, QL, 128)

    docs = docs.reshape(16, DPAD, 128)
    doc_len = docs[:, DT, :4].astype(jnp.int32)
    docs = docs[:, :DT].reshape(16 * DT, 128)
    doc_last = jnp.cumsum(doc_len, axis=1)
    doc_first = doc_last - doc_len
    need = jnp.any(
        pick.reshape(1, 256) == jnp.arange(64, dtype=jnp.int32)[:, None], axis=1
    ).astype(jnp.int32)
    pick_lanes = jnp.pad(pick.T, ((0, 0), (0, 112)), constant_values=-1)
    terms = match(
        need, doc_first.reshape(64), doc_last.reshape(64), queries.reshape(1024, 128), docs, pick_lanes
    )
    terms = lax.all_to_all(terms, HEAD + ("y",), 0, 0, tiled=True)
    scores = vmem_call(total_kernel, jax.ShapeDtypeStruct((RQ, NC), F32), "total", 1)(my_y.reshape(1), terms)
    return (embedded, scores)


def solution(mesh):
    fine = Mesh(mesh.devices.reshape(4, 2, 4, 4, 4), HEAD + SHARD)
    in_specs = (
        P(SHARD, None, None),
        P(None, HEAD),
        P(None, HEAD),
        P(None, HEAD),
        P(HEAD, None),
        P(),
        P(None, HEAD),
        P(HEAD, None),
        P(),
        P(),
        P(SHARD, None, HEAD),
        P(SHARD, None, HEAD),
        P(),
        P(),
        P(SHARD),
        P(HEAD + SHARD, None),
        P(HEAD + SHARD, None),
        P(SHARD, None),
    )
    out_specs = (P(SHARD, None, None), P(SHARD, None))
    return jax.shard_map(per_device, mesh=fine, in_specs=in_specs, out_specs=out_specs, check_vma=False)
```

```python
import jax
import jax.numpy as jnp
from jax import lax
from jax.experimental import pallas as pl
from jax.experimental.pallas import tpu as pltpu
from jax.sharding import Mesh, PartitionSpec as P

HEAD = ("x", "c")
SHARD = ("y", "q", "r")
RQ = 4
QL = 64
NC = 16
NROW = RQ * QL
DT = 256
DPAD = 272
XROW = 3 * NROW + 16
BF = jnp.bfloat16
F32 = jnp.float32


def layer_norm(values, norm_gain):
    row_mean = jnp.mean(values, axis=-1, keepdims=True)
    row_var = jnp.mean(jnp.square(values - row_mean), axis=-1, keepdims=True)
    return (values - row_mean) * lax.rsqrt(row_var + 1e-05) * norm_gain


def spread(block, axes, count):
    wide = jnp.broadcast_to(block[None], (count,) + block.shape)
    return lax.all_to_all(wide, axes, 0, 0, tiled=True).reshape((-1,) + block.shape[1:])


def nt_dot(a, b):
    return lax.dot_general(a, b, (((1,), (1,)), ((), ())), preferred_element_type=F32)


def attend_kernel(group_ref, rows_ref, prompt_ref, bias_ref, out_ref, order_ref):
    low_half = lax.broadcasted_iota(jnp.int32, (QL, 128), 1) < 64
    out_ref[...] = jnp.zeros_like(out_ref)
    count = jnp.int32(0)
    for i in range(16):
        order_ref[count] = jnp.int32(i)
        count = count + (group_ref[i] >= 0).astype(jnp.int32)

    def one_request(i):
        src = i // RQ
        row = pl.multiple_of((i % RQ) * QL, QL)
        group = group_ref[i]
        query = rows_ref[src, pl.ds(row, QL), :]
        zero = jnp.zeros_like(query)
        both = jnp.concatenate(
            [jnp.where(low_half, query, zero), jnp.where(low_half, zero, query)], axis=0
        )
        own_key = rows_ref[src, pl.ds(pl.multiple_of(NROW + row, QL), QL), :]
        own_value = rows_ref[src, pl.ds(pl.multiple_of(2 * NROW + row, QL), QL), :]
        parts = [nt_dot(both, own_key)]
        values = [own_value]
        for piece in range(4):
            start = pl.multiple_of(piece * 1024 + group * 256, 256)
            key = prompt_ref[pl.ds(start, 128), :]
            values.append(prompt_ref[pl.ds(pl.multiple_of(start + 128, 128), 128), :])
            bias = bias_ref[group, :, piece * 128 : (piece + 1) * 128]
            parts.append(nt_dot(both, key) + bias)
        top = jnp.max(parts[0], axis=-1, keepdims=True)
        wide = jnp.maximum(jnp.maximum(parts[1], parts[2]), jnp.maximum(parts[3], parts[4]))
        top = jnp.maximum(top, jnp.max(wide, axis=-1, keepdims=True))
        weights = [jnp.exp(part - top) for part in parts]
        wide = (weights[1] + weights[2]) + (weights[3] + weights[4])
        total = jnp.sum(weights[0], axis=-1, keepdims=True) + jnp.sum(wide, axis=-1, keepdims=True)
        mixed = jnp.zeros((2 * QL, 128), F32)
        for weight, value in zip(weights, values):
            mixed = mixed + jnp.dot(weight.astype(BF), value, preferred_element_type=F32)
        mixed = mixed / total
        return jnp.where(low_half, mixed[:QL], mixed[QL:]).astype(BF)

    def two_requests(step, carry):
        i = order_ref[2 * step]
        k = order_ref[jnp.where(2 * step + 1 < count, 2 * step + 1, 2 * step)]
        results = [one_request(i), one_request(k)]
        for j, result in zip((i, k), results):
            place = pl.multiple_of((j % 2) * QL, QL)
            out_ref[(j % RQ) // 2, j // RQ, pl.ds(place, QL), :] = result
        return carry

    lax.fori_loop(0, (count + 1) // 2, two_requests, 0)


def attend(groups, rows, prompt, bias):
    return pl.pallas_call(
        attend_kernel,
        out_shape=jax.ShapeDtypeStruct((2, 4, 2 * QL, 128), BF),
        in_specs=[
            pl.BlockSpec(memory_space=pltpu.SMEM),
            pl.BlockSpec(memory_space=pltpu.VMEM),
            pl.BlockSpec(memory_space=pltpu.VMEM),
            pl.BlockSpec(memory_space=pltpu.VMEM),
        ],
        out_specs=pl.BlockSpec(memory_space=pltpu.VMEM),
        scratch_shapes=[pltpu.SMEM((17,), jnp.int32)],
        compiler_params=pltpu.CompilerParams(vmem_limit_bytes=16 << 20),
        cost_estimate=pl.CostEstimate(flops=1000, bytes_accessed=1000, transcendentals=0),
        name="attend",
    )(groups, rows, prompt, bias)


def match_kernel(need_ref, first_ref, last_ref, query_ref, docs_ref, pick_ref, out_ref, sims_ref, best_ref, term_ref):
    best_ref[...] = jnp.zeros_like(best_ref)
    token = lax.broadcasted_iota(jnp.int32, (DT, 128), 0)

    def one_holder(z, carry):
        base = z * 4
        any_need = need_ref[base] + need_ref[base + 1] + need_ref[base + 2] + need_ref[base + 3]

        @pl.when(any_need > 0)
        def _():
            vectors = docs_ref[pl.ds(pl.multiple_of(z * DT, DT), DT), :]
            sims_ref[...] = nt_dot(vectors, query_ref[...])

            def one_doc(k, inner):
                doc = base + k

                @pl.when(need_ref[doc] > 0)
                def _():
                    inside = (token >= first_ref[doc]) & (token < last_ref[doc])
                    tops = []
                    for col in range(8):
                        block = sims_ref[:, col * 128 : (col + 1) * 128]
                        tops.append(jnp.max(jnp.where(inside, block, -1e30), axis=0, keepdims=True))
                    best_ref[doc] = jnp.concatenate(tops, axis=0)

                return inner

            lax.fori_loop(0, 4, one_doc, 0)

        return carry

    lax.fori_loop(0, 16, one_holder, 0)
    lane = lax.broadcasted_iota(jnp.int32, (128, 128), 0)
    request = lax.broadcasted_iota(jnp.int32, (128, 128), 1)
    member = (lane // 32 == request // RQ).astype(F32)
    sums = jnp.dot(
        best_ref[...].reshape(512, 128), member, preferred_element_type=F32, precision=lax.Precision.HIGHEST
    ).reshape(64, 8, 128)
    head = lax.broadcasted_iota(jnp.int32, (64, 8, 128), 1)
    request = lax.broadcasted_iota(jnp.int32, (64, 8, 128), 2)
    per_doc = jnp.sum(jnp.where((head % 2) * 2 + head // 4 == request % RQ, sums, 0.0), axis=1)
    doc_row = lax.broadcasted_iota(jnp.int32, (64, 128), 0)
    for c in range(NC):
        hit = doc_row == pick_ref[c : c + 1, :]
        term_ref[c : c + 1, :] = jnp.sum(jnp.where(hit, per_doc, 0.0), axis=0, keepdims=True)
    for i in range(32):
        out_ref[i] = term_ref[...]


def match(need, first, last, queries, docs, pick):
    return pl.pallas_call(
        match_kernel,
        out_shape=jax.ShapeDtypeStruct((32, NC, 128), F32),
        in_specs=[pl.BlockSpec(memory_space=pltpu.SMEM)] * 3 + [pl.BlockSpec(memory_space=pltpu.VMEM)] * 3,
        out_specs=pl.BlockSpec(memory_space=pltpu.VMEM),
        scratch_shapes=[pltpu.VMEM((DT, 1024), F32), pltpu.VMEM((64, 8, 128), F32), pltpu.VMEM((NC, 128), F32)],
        compiler_params=pltpu.CompilerParams(vmem_limit_bytes=16 << 20),
        cost_estimate=pl.CostEstimate(flops=1000, bytes_accessed=1000, transcendentals=0),
        name="match",
    )(need, first, last, queries, docs, pick)


def vmem_call(body, out_shape, name, smem=0):
    def call(*args):
        spaces = [pltpu.SMEM] * smem + [pltpu.VMEM] * (len(args) - smem)
        return pl.pallas_call(
            body,
            out_shape=out_shape,
            in_specs=[pl.BlockSpec(memory_space=space) for space in spaces],
            out_specs=jax.tree.map(lambda _: pl.BlockSpec(memory_space=pltpu.VMEM), out_shape),
            compiler_params=pltpu.CompilerParams(vmem_limit_bytes=16 << 20),
            cost_estimate=pl.CostEstimate(flops=1000, bytes_accessed=1000, transcendentals=0),
            name=name,
        )(*args)

    return call


def total_kernel(place_ref, terms_ref, out_ref):
    total = terms_ref[0]
    for i in range(1, 32):
        total = total + terms_ref[i]
    lane = lax.broadcasted_iota(jnp.int32, (8, 128), 1)
    row = lax.broadcasted_iota(jnp.int32, (8, 128), 0)
    wanted = (lane == place_ref[0] * RQ + row).astype(F32)
    picked = lax.dot_general(
        wanted, total, (((1,), (1,)), ((), ())), preferred_element_type=F32, precision=lax.Precision.HIGHEST
    )
    out_ref[...] = picked[:RQ]


def dense_kernel(place_ref, context_ref, token_ref, gain_ref, *refs):
    held, first_ref, terms_ref, scratch, sems = refs[:9], refs[9], refs[10], refs[11:20], refs[20]
    copies = [pltpu.make_async_copy(held[i], scratch[i], sems.at[i]) for i in range(9)]
    for copy in copies:
        copy.start()
    w_out_ref, inner_refs, outer_refs = scratch[0], scratch[1:5], scratch[5:9]
    start = pl.multiple_of(place_ref[0] * 128, 128)
    attn = token_ref[pl.ds(start, 128), :].astype(F32)
    copies[0].wait()
    for h in range(8):
        attn = attn + jnp.dot(
            context_ref[h], w_out_ref[h * 128 : (h + 1) * 128, :], preferred_element_type=F32
        )
    first = layer_norm(attn, gain_ref[...]).astype(BF)
    first_ref[...] = first
    for copy in copies[1:]:
        copy.wait()
    total = jnp.zeros((128, 1024), F32)
    for core in range(2):
        inner = jnp.zeros((128, 512), F32)
        for part in range(4):
            inner = inner + jnp.dot(
                first[:, part * 256 : (part + 1) * 256], inner_refs[part][core], preferred_element_type=F32
            )
        active = (0.5 * inner * (1.0 + lax.erf(inner * (0.5**0.5)))).astype(BF)
        for part in range(4):
            total = total + jnp.dot(
                active[:, part * 128 : (part + 1) * 128], outer_refs[part][core], preferred_element_type=F32
            )
    terms_ref[...] = total.astype(BF).reshape(4, 32, 1024)


def dense(place, context, tokens, gain, weights):
    return pl.pallas_call(
        dense_kernel,
        out_shape=(jax.ShapeDtypeStruct((128, 1024), BF), jax.ShapeDtypeStruct((4, 32, 1024), BF)),
        in_specs=[pl.BlockSpec(memory_space=pltpu.SMEM)]
        + [pl.BlockSpec(memory_space=pltpu.VMEM)] * 3
        + [pl.BlockSpec(memory_space=pl.ANY)] * 9,
        out_specs=(pl.BlockSpec(memory_space=pltpu.VMEM), pl.BlockSpec(memory_space=pltpu.VMEM)),
        scratch_shapes=[pltpu.VMEM(w.shape, w.dtype) for w in weights] + [pltpu.SemaphoreType.DMA((9,))],
        compiler_params=pltpu.CompilerParams(vmem_limit_bytes=52 << 20),
        cost_estimate=pl.CostEstimate(flops=1000, bytes_accessed=1000, transcendentals=0),
        name="dense",
    )(place, context, tokens, gain, *weights)


def embed_kernel(place_ref, first_ref, terms_ref, gain_ref, w_project_ref, out_ref):
    start = pl.multiple_of(place_ref[0] * 32, 32)
    total = first_ref[pl.ds(start, 32), :].astype(F32)
    for x in range(4):
        total = total + terms_ref[x].astype(F32)
    second = layer_norm(total, gain_ref[...]).astype(BF)
    projected = jnp.dot(second, w_project_ref[...], preferred_element_type=F32)
    scale = lax.rsqrt(jnp.sum(projected * projected, axis=-1, keepdims=True) + 1e-06)
    embed = (projected * scale).astype(BF)
    for i in range(32):
        out_ref[i] = embed


def per_device(
    tokens,
    w_query,
    w_key,
    w_value,
    w_out,
    norm1_gain,
    w_inner,
    w_outer,
    norm2_gain,
    w_project,
    key_pages,
    value_pages,
    page_table,
    prompt_lengths,
    request_group,
    doc_vectors,
    doc_lengths,
    candidates,
):
    my_y = lax.axis_index("y")
    my_head = lax.axis_index(HEAD)
    my_core = lax.axis_index("c").reshape(1)
    my_x = lax.axis_index("x").reshape(1)
    token_rows = tokens.reshape(NROW, 1024)

    pages = jnp.concatenate([key_pages.reshape(128, 128), value_pages.reshape(128, 128)], axis=0)
    pages_q = spread(pages, "q", 4)

    w_out_all = lax.all_gather(w_out, HEAD, axis=0, tiled=True)
    doc_rows = jnp.pad(doc_lengths.astype(BF), ((0, DPAD - DT - 1), (0, 124)))
    doc_block = jnp.concatenate([doc_vectors, doc_rows], axis=0)
    docs = lax.all_gather(doc_block, ("q", "r"), axis=0, tiled=True)

    query = jnp.dot(token_rows, w_query, preferred_element_type=F32).astype(BF) * BF(0.125)
    own_key = jnp.dot(token_rows, w_key, preferred_element_type=F32).astype(BF)
    own_value = jnp.dot(token_rows, w_value, preferred_element_type=F32).astype(BF)
    ids = jnp.concatenate([candidates // 64, candidates % 64, request_group[:, None]], axis=1)
    ids = jnp.pad(ids.astype(BF), ((0, 12), (0, 128 - 33)))
    rows = jnp.concatenate([query, own_key, own_value, ids], axis=0)
    rows = lax.all_gather(rows, "y", axis=0, tiled=True)
    pages_q, rows = lax.optimization_barrier((pages_q, rows))
    prompt = spread(pages_q.reshape(1024, 128), "r", 4)

    w_inner, w_outer, pages_q = lax.optimization_barrier((w_inner, w_outer, pages_q))
    inner_parts = [
        lax.all_gather(w_inner[i * 256 : (i + 1) * 256], "c", axis=0, tiled=False) for i in range(4)
    ]
    outer_parts = [
        lax.all_gather(w_outer[i * 128 : (i + 1) * 128], "c", axis=0, tiled=False) for i in range(4)
    ]

    rows = rows.reshape(4, XROW, 128)
    got = rows[:, 3 * NROW : 3 * NROW + RQ, :33].reshape(16, 33).astype(jnp.int32)
    groups = jnp.where(got[:, 32] // 4 == my_y, got[:, 32] % 4, -1)
    pick = jnp.where(got[:, :16] == my_head * 4 + my_y, got[:, 16:32], -1)

    table = lax.dynamic_slice(page_table, (my_y * 32,), (32,)).reshape(4, 8)
    lengths = lax.dynamic_slice(prompt_lengths, (my_y * 4,), (4,))
    page_ids = (my_y * 32 + jnp.arange(32, dtype=jnp.int32)).reshape(4, 8)
    slot = jnp.sum(
        jnp.where(table[:, None, :] == page_ids[:, :, None], jnp.arange(8, dtype=jnp.int32), 0), axis=-1
    )
    position = slot[:, :, None] * 64 + jnp.arange(64, dtype=jnp.int32)
    bias = jnp.where(position < lengths[:, None, None], 0.0, -1e30).astype(F32).reshape(4, 1, 512)

    rows, inner_parts, outer_parts = lax.optimization_barrier((rows, inner_parts, outer_parts))
    mixed = attend(groups, rows, prompt, bias)
    back = lax.all_to_all(mixed.reshape(8, 128, 128), ("c", "y"), 0, 0, tiled=True)
    context = jnp.sum(back.reshape(2, 4, 128, 128).astype(F32), axis=1).astype(BF)
    context = lax.all_gather(context, "x", axis=0, tiled=True)
    weights = [w_out_all] + inner_parts + outer_parts
    first, terms = dense(my_core, context, token_rows, norm1_gain[None], weights)
    terms = lax.all_to_all(terms, "x", 0, 0, tiled=True)
    embed = vmem_call(embed_kernel, jax.ShapeDtypeStruct((32, 32, 128), BF), "embed", 1)(
        my_x, first, terms, norm2_gain[None], w_project
    )

    queries = lax.all_to_all(embed, HEAD + ("y",), 0, 0, tiled=True)
    own = lax.dynamic_slice(queries.reshape(4, 2, 4, 32, 128), (0, 0, my_y, 0, 0), (4, 2, 1, 32, 128))
    embedded = jnp.transpose(own, (1, 0, 2, 3, 4)).reshape(RQ, QL, 128)

    docs = docs.reshape(16, DPAD, 128)
    doc_len = docs[:, DT, :4].astype(jnp.int32)
    docs = docs[:, :DT].reshape(16 * DT, 128)
    doc_last = jnp.cumsum(doc_len, axis=1)
    doc_first = doc_last - doc_len
    need = jnp.any(
        pick.reshape(1, 256) == jnp.arange(64, dtype=jnp.int32)[:, None], axis=1
    ).astype(jnp.int32)
    pick_lanes = jnp.pad(pick.T, ((0, 0), (0, 112)), constant_values=-1)
    terms = match(
        need, doc_first.reshape(64), doc_last.reshape(64), queries.reshape(1024, 128), docs, pick_lanes
    )
    terms = lax.all_to_all(terms, HEAD + ("y",), 0, 0, tiled=True)
    scores = vmem_call(total_kernel, jax.ShapeDtypeStruct((RQ, NC), F32), "total", 1)(my_y.reshape(1), terms)
    return (embedded, scores)


def solution(mesh):
    fine = Mesh(mesh.devices.reshape(4, 2, 4, 4, 4), HEAD + SHARD)
    in_specs = (
        P(SHARD, None, None),
        P(None, HEAD),
        P(None, HEAD),
        P(None, HEAD),
        P(HEAD, None),
        P(),
        P(None, HEAD),
        P(HEAD, None),
        P(),
        P(),
        P(SHARD, None, HEAD),
        P(SHARD, None, HEAD),
        P(),
        P(),
        P(SHARD),
        P(HEAD + SHARD, None),
        P(HEAD + SHARD, None),
        P(SHARD, None),
    )
    out_specs = (P(SHARD, None, None), P(SHARD, None))
    return jax.shard_map(per_device, mesh=fine, in_specs=in_specs, out_specs=out_specs, check_vma=False)
```

```python
import jax
import jax.numpy as jnp
from jax import lax
from jax.experimental import pallas as pl
from jax.experimental.pallas import tpu as pltpu
from jax.sharding import Mesh, PartitionSpec as P

HEAD = ("x", "c")
SHARD = ("y", "q", "r")
RQ = 4
QL = 64
NC = 16
NROW = RQ * QL
DT = 256
DPAD = 272
XROW = 3 * NROW + 16
BF = jnp.bfloat16
F32 = jnp.float32


def layer_norm(values, norm_gain):
    row_mean = jnp.mean(values, axis=-1, keepdims=True)
    row_var = jnp.mean(jnp.square(values - row_mean), axis=-1, keepdims=True)
    return (values - row_mean) * lax.rsqrt(row_var + 1e-05) * norm_gain


def spread(block, axes, count):
    wide = jnp.broadcast_to(block[None], (count,) + block.shape)
    return lax.all_to_all(wide, axes, 0, 0, tiled=True).reshape((-1,) + block.shape[1:])


def from_ahead(block, step):
    return lax.ppermute(block, ("q", "r"), [((i + step) % 16, i) for i in range(16)])


def nt_dot(a, b):
    return lax.dot_general(a, b, (((1,), (1,)), ((), ())), preferred_element_type=F32)


def attend_kernel(group_ref, rows_ref, bias_ref, *refs):
    prompt_refs, out_ref, order_ref = refs[:4], refs[4], refs[5]
    low_half = lax.broadcasted_iota(jnp.int32, (QL, 128), 1) < 64
    out_ref[...] = jnp.zeros_like(out_ref)
    count = jnp.int32(0)
    for i in range(16):
        order_ref[count] = jnp.int32(i)
        count = count + (group_ref[i] >= 0).astype(jnp.int32)

    def one_request(i):
        src = i // RQ
        row = pl.multiple_of((i % RQ) * QL, QL)
        group = group_ref[i]
        query = rows_ref[src, pl.ds(row, QL), :]
        zero = jnp.zeros_like(query)
        both = jnp.concatenate(
            [jnp.where(low_half, query, zero), jnp.where(low_half, zero, query)], axis=0
        )
        own_key = rows_ref[src, pl.ds(pl.multiple_of(NROW + row, QL), QL), :]
        own_value = rows_ref[src, pl.ds(pl.multiple_of(2 * NROW + row, QL), QL), :]
        parts = [nt_dot(both, own_key)]
        values = [own_value]
        for piece in range(4):
            start = pl.multiple_of(group * 256, 256)
            key = prompt_refs[piece][pl.ds(start, 128), :]
            values.append(prompt_refs[piece][pl.ds(pl.multiple_of(start + 128, 128), 128), :])
            bias = bias_ref[group, :, piece * 128 : (piece + 1) * 128]
            parts.append(nt_dot(both, key) + bias)
        top = jnp.max(parts[0], axis=-1, keepdims=True)
        wide = jnp.maximum(jnp.maximum(parts[1], parts[2]), jnp.maximum(parts[3], parts[4]))
        top = jnp.maximum(top, jnp.max(wide, axis=-1, keepdims=True))
        weights = [jnp.exp(part - top) for part in parts]
        wide = (weights[1] + weights[2]) + (weights[3] + weights[4])
        total = jnp.sum(weights[0], axis=-1, keepdims=True) + jnp.sum(wide, axis=-1, keepdims=True)
        mixed = jnp.zeros((2 * QL, 128), F32)
        for weight, value in zip(weights, values):
            mixed = mixed + jnp.dot(weight.astype(BF), value, preferred_element_type=F32)
        mixed = mixed / total
        return jnp.where(low_half, mixed[:QL], mixed[QL:]).astype(BF)

    def two_requests(step, carry):
        i = order_ref[2 * step]
        k = order_ref[jnp.where(2 * step + 1 < count, 2 * step + 1, 2 * step)]
        results = [one_request(i), one_request(k)]
        for j, result in zip((i, k), results):
            out_ref[j // RQ, pl.ds(pl.multiple_of((j % RQ) * QL, QL), QL), :] = result
        return carry

    lax.fori_loop(0, (count + 1) // 2, two_requests, 0)


def attend(groups, rows, prompt, bias):
    return pl.pallas_call(
        attend_kernel,
        out_shape=jax.ShapeDtypeStruct((4, NROW, 128), BF),
        in_specs=[
            pl.BlockSpec(memory_space=pltpu.SMEM),
        ]
        + [pl.BlockSpec(memory_space=pltpu.VMEM)] * 6,
        out_specs=pl.BlockSpec(memory_space=pltpu.VMEM),
        scratch_shapes=[pltpu.SMEM((17,), jnp.int32)],
        compiler_params=pltpu.CompilerParams(vmem_limit_bytes=16 << 20),
        cost_estimate=pl.CostEstimate(flops=1000, bytes_accessed=1000, transcendentals=0),
        name="attend",
    )(groups, rows, bias, *prompt)


def match_kernel(need_ref, first_ref, last_ref, query_ref, docs_ref, pick_ref, out_ref, sims_ref, best_ref, term_ref):
    best_ref[...] = jnp.zeros_like(best_ref)
    token = lax.broadcasted_iota(jnp.int32, (DT, 128), 0)

    def one_holder(z, carry):
        base = z * 4
        any_need = need_ref[base] + need_ref[base + 1] + need_ref[base + 2] + need_ref[base + 3]

        @pl.when(any_need > 0)
        def _():
            vectors = docs_ref[pl.ds(pl.multiple_of(z * DT, DT), DT), :]
            sims_ref[...] = nt_dot(vectors, query_ref[...])

            def one_doc(k, inner):
                doc = base + k

                @pl.when(need_ref[doc] > 0)
                def _():
                    inside = (token >= first_ref[doc]) & (token < last_ref[doc])
                    tops = []
                    for col in range(8):
                        block = sims_ref[:, col * 128 : (col + 1) * 128]
                        tops.append(jnp.max(jnp.where(inside, block, -1e30), axis=0, keepdims=True))
                    best_ref[doc] = jnp.concatenate(tops, axis=0)

                return inner

            lax.fori_loop(0, 4, one_doc, 0)

        return carry

    lax.fori_loop(0, 16, one_holder, 0)
    lane = lax.broadcasted_iota(jnp.int32, (128, 128), 0)
    request = lax.broadcasted_iota(jnp.int32, (128, 128), 1)
    member = (lane // 32 == request // RQ).astype(F32)
    sums = jnp.dot(
        best_ref[...].reshape(512, 128), member, preferred_element_type=F32, precision=lax.Precision.HIGHEST
    ).reshape(64, 8, 128)
    head = lax.broadcasted_iota(jnp.int32, (64, 8, 128), 1)
    request = lax.broadcasted_iota(jnp.int32, (64, 8, 128), 2)
    per_doc = jnp.sum(jnp.where(head // 2 == request % RQ, sums, 0.0), axis=1)
    doc_row = lax.broadcasted_iota(jnp.int32, (64, 128), 0)
    for c in range(NC):
        hit = doc_row == pick_ref[c : c + 1, :]
        term_ref[c : c + 1, :] = jnp.sum(jnp.where(hit, per_doc, 0.0), axis=0, keepdims=True)
    for i in range(32):
        out_ref[i] = term_ref[...]


def match(need, first, last, queries, docs, pick):
    return pl.pallas_call(
        match_kernel,
        out_shape=jax.ShapeDtypeStruct((32, NC, 128), F32),
        in_specs=[pl.BlockSpec(memory_space=pltpu.SMEM)] * 3 + [pl.BlockSpec(memory_space=pltpu.VMEM)] * 3,
        out_specs=pl.BlockSpec(memory_space=pltpu.VMEM),
        scratch_shapes=[pltpu.VMEM((DT, 1024), F32), pltpu.VMEM((64, 8, 128), F32), pltpu.VMEM((NC, 128), F32)],
        compiler_params=pltpu.CompilerParams(vmem_limit_bytes=16 << 20),
        cost_estimate=pl.CostEstimate(flops=1000, bytes_accessed=1000, transcendentals=0),
        name="match",
    )(need, first, last, queries, docs, pick)


def vmem_call(body, out_shape, name, smem=0):
    def call(*args):
        spaces = [pltpu.SMEM] * smem + [pltpu.VMEM] * (len(args) - smem)
        return pl.pallas_call(
            body,
            out_shape=out_shape,
            in_specs=[pl.BlockSpec(memory_space=space) for space in spaces],
            out_specs=jax.tree.map(lambda _: pl.BlockSpec(memory_space=pltpu.VMEM), out_shape),
            compiler_params=pltpu.CompilerParams(vmem_limit_bytes=16 << 20),
            cost_estimate=pl.CostEstimate(flops=1000, bytes_accessed=1000, transcendentals=0),
            name=name,
        )(*args)

    return call


def total_kernel(place_ref, terms_ref, out_ref):
    total = terms_ref[0]
    for i in range(1, 32):
        total = total + terms_ref[i]
    lane = lax.broadcasted_iota(jnp.int32, (8, 128), 1)
    row = lax.broadcasted_iota(jnp.int32, (8, 128), 0)
    wanted = (lane == place_ref[0] * RQ + row).astype(F32)
    picked = lax.dot_general(
        wanted, total, (((1,), (1,)), ((), ())), preferred_element_type=F32, precision=lax.Precision.HIGHEST
    )
    out_ref[...] = picked[:RQ]


def dense_kernel(context_ref, token_ref, gain_ref, *refs):
    held, first_ref, terms_ref, scratch, sems = refs[:3], refs[3], refs[4], refs[5:8], refs[8]
    copies = [pltpu.make_async_copy(held[i], scratch[i], sems.at[i]) for i in range(3)]
    for copy in copies:
        copy.start()
    w_out_ref, inner_ref, outer_ref = scratch
    attn = token_ref[...].astype(F32)
    copies[0].wait()
    for h in range(8):
        attn = attn + jnp.dot(
            context_ref[h], w_out_ref[h * 128 : (h + 1) * 128, :], preferred_element_type=F32
        )
    first = layer_norm(attn, gain_ref[...]).astype(BF)
    first_ref[...] = first
    copies[1].wait()
    inner = jnp.dot(first, inner_ref[...], preferred_element_type=F32)
    active = (0.5 * inner * (1.0 + lax.erf(inner * (0.5**0.5)))).astype(BF)
    copies[2].wait()
    total = jnp.dot(active, outer_ref[...], preferred_element_type=F32)
    terms_ref[...] = total.astype(BF).reshape(8, 32, 1024)


def dense(context, tokens, gain, weights):
    return pl.pallas_call(
        dense_kernel,
        out_shape=(jax.ShapeDtypeStruct((NROW, 1024), BF), jax.ShapeDtypeStruct((8, 32, 1024), BF)),
        in_specs=[pl.BlockSpec(memory_space=pltpu.VMEM)] * 3 + [pl.BlockSpec(memory_space=pl.ANY)] * 3,
        out_specs=(pl.BlockSpec(memory_space=pltpu.VMEM), pl.BlockSpec(memory_space=pltpu.VMEM)),
        scratch_shapes=[pltpu.VMEM(w.shape, w.dtype) for w in weights] + [pltpu.SemaphoreType.DMA((3,))],
        compiler_params=pltpu.CompilerParams(vmem_limit_bytes=52 << 20),
        cost_estimate=pl.CostEstimate(flops=1000, bytes_accessed=1000, transcendentals=0),
        name="dense",
    )(context, tokens, gain, *weights)


def embed_kernel(place_ref, first_ref, terms_ref, gain_ref, w_project_ref, out_ref):
    start = pl.multiple_of(place_ref[0] * 32, 32)
    total = first_ref[pl.ds(start, 32), :].astype(F32)
    for h in range(8):
        total = total + terms_ref[h].astype(F32)
    second = layer_norm(total, gain_ref[...]).astype(BF)
    projected = jnp.dot(second, w_project_ref[...], preferred_element_type=F32)
    scale = lax.rsqrt(jnp.sum(projected * projected, axis=-1, keepdims=True) + 1e-06)
    embed = (projected * scale).astype(BF)
    for i in range(32):
        out_ref[i] = embed


def per_device(
    tokens,
    w_query,
    w_key,
    w_value,
    w_out,
    norm1_gain,
    w_inner,
    w_outer,
    norm2_gain,
    w_project,
    key_pages,
    value_pages,
    page_table,
    prompt_lengths,
    request_group,
    doc_vectors,
    doc_lengths,
    candidates,
):
    my_y = lax.axis_index("y")
    my_head = lax.axis_index(HEAD)
    token_rows = tokens.reshape(NROW, 1024)

    pages = jnp.concatenate([key_pages.reshape(128, 128), value_pages.reshape(128, 128)], axis=0)
    pages_q = spread(pages, "q", 4)

    w_out_all = lax.all_gather(w_out, HEAD, axis=0, tiled=True)
    doc_rows = jnp.pad(doc_lengths.astype(BF), ((0, DPAD - DT - 1), (0, 124)))
    doc_block = jnp.concatenate([doc_vectors, doc_rows], axis=0)
    docs = lax.all_gather(doc_block, ("q", "r"), axis=0, tiled=True)

    query = jnp.dot(token_rows, w_query, preferred_element_type=F32).astype(BF) * BF(0.125)
    own_key = jnp.dot(token_rows, w_key, preferred_element_type=F32).astype(BF)
    own_value = jnp.dot(token_rows, w_value, preferred_element_type=F32).astype(BF)
    ids = jnp.concatenate([candidates // 64, candidates % 64, request_group[:, None]], axis=1)
    ids = jnp.pad(ids.astype(BF), ((0, 12), (0, 128 - 33)))
    rows = jnp.concatenate([query, own_key, own_value, ids], axis=0)
    rows = lax.all_gather(rows, "y", axis=0, tiled=True)
    pages_q, rows = lax.optimization_barrier((pages_q, rows))
    pages_q = pages_q.reshape(1024, 128)
    ahead_two = jnp.concatenate([from_ahead(pages_q[:512], 2), from_ahead(pages_q[512:], -2)], axis=0)
    prompt = [pages_q, from_ahead(pages_q, 1), ahead_two, from_ahead(pages_q, -1)]

    rows = rows.reshape(4, XROW, 128)
    got = rows[:, 3 * NROW : 3 * NROW + RQ, :33].reshape(16, 33).astype(jnp.int32)
    groups = jnp.where(got[:, 32] // 4 == my_y, got[:, 32] % 4, -1)
    pick = jnp.where(got[:, :16] == my_head * 4 + my_y, got[:, 16:32], -1)

    table = lax.dynamic_slice(page_table, (my_y * 32,), (32,)).reshape(4, 8)
    lengths = lax.dynamic_slice(prompt_lengths, (my_y * 4,), (4,))
    page_ids = (my_y * 32 + jnp.arange(32, dtype=jnp.int32)).reshape(4, 8)
    slot = jnp.sum(
        jnp.where(table[:, None, :] == page_ids[:, :, None], jnp.arange(8, dtype=jnp.int32), 0), axis=-1
    )
    position = slot[:, :, None] * 64 + jnp.arange(64, dtype=jnp.int32)
    bias = jnp.where(position < lengths[:, None, None], 0.0, -1e30).astype(F32).reshape(4, 4, 128)
    ahead = (lax.axis_index("r") + jnp.arange(4, dtype=jnp.int32)) % 4
    turn = ahead[:, None] == jnp.arange(4, dtype=jnp.int32)
    bias = jnp.sum(jnp.where(turn[None, :, :, None], bias[:, None], 0.0), axis=2).reshape(4, 1, 512)

    mixed = attend(groups, rows, prompt, bias)
    back = lax.all_to_all(mixed, "y", 0, 0, tiled=True)
    context = jnp.sum(back.astype(F32), axis=0).astype(BF)
    context = lax.all_gather(context, HEAD, axis=0, tiled=False)
    first, terms = dense(context, token_rows, norm1_gain[None], [w_out_all, w_inner, w_outer])
    terms = lax.all_to_all(terms, HEAD, 0, 0, tiled=True)
    embed = vmem_call(embed_kernel, jax.ShapeDtypeStruct((32, 32, 128), BF), "embed", 1)(
        my_head.reshape(1), first, terms, norm2_gain[None], w_project
    )

    queries = lax.all_to_all(embed, HEAD + ("y",), 0, 0, tiled=True)
    own = lax.dynamic_slice(queries.reshape(8, 4, 32, 128), (0, my_y, 0, 0), (8, 1, 32, 128))
    embedded = own.reshape(RQ, QL, 128)

    docs = lax.optimization_barrier((docs, embed))[0].reshape(16, DPAD, 128)
    doc_len = docs[:, DT, :4].astype(jnp.int32)
    docs = docs[:, :DT].reshape(16 * DT, 128)
    doc_last = jnp.cumsum(doc_len, axis=1)
    doc_first = doc_last - doc_len
    need = jnp.any(
        pick.reshape(1, 256) == jnp.arange(64, dtype=jnp.int32)[:, None], axis=1
    ).astype(jnp.int32)
    pick_lanes = jnp.pad(pick.T, ((0, 0), (0, 112)), constant_values=-1)
    terms = match(
        need, doc_first.reshape(64), doc_last.reshape(64), queries.reshape(1024, 128), docs, pick_lanes
    )
    terms = lax.all_to_all(terms, HEAD + ("y",), 0, 0, tiled=True)
    scores = vmem_call(total_kernel, jax.ShapeDtypeStruct((RQ, NC), F32), "total", 1)(my_y.reshape(1), terms)
    return (embedded, scores)


def solution(mesh):
    fine = Mesh(mesh.devices.reshape(4, 2, 4, 4, 4), HEAD + SHARD)
    in_specs = (
        P(SHARD, None, None),
        P(None, HEAD),
        P(None, HEAD),
        P(None, HEAD),
        P(HEAD, None),
        P(),
        P(None, HEAD),
        P(HEAD, None),
        P(),
        P(),
        P(SHARD, None, HEAD),
        P(SHARD, None, HEAD),
        P(),
        P(),
        P(SHARD),
        P(HEAD + SHARD, None),
        P(HEAD + SHARD, None),
        P(SHARD, None),
    )
    out_specs = (P(SHARD, None, None), P(SHARD, None))
    return jax.shard_map(per_device, mesh=fine, in_specs=in_specs, out_specs=out_specs, check_vma=False)
```

```python
import jax
import jax.numpy as jnp
from jax import lax
from jax.experimental import pallas as pl
from jax.experimental.pallas import tpu as pltpu
from jax.sharding import Mesh, PartitionSpec as P

HEAD = ("x", "c")
SHARD = ("y", "q", "r")
RQ = 4
QL = 64
NC = 16
NROW = RQ * QL
DT = 256
DPAD = 272
XROW = 3 * NROW + 16
BF = jnp.bfloat16
F32 = jnp.float32


def layer_norm(values, norm_gain):
    row_mean = jnp.mean(values, axis=-1, keepdims=True)
    row_var = jnp.mean(jnp.square(values - row_mean), axis=-1, keepdims=True)
    return (values - row_mean) * lax.rsqrt(row_var + 1e-05) * norm_gain


def spread(block, axes, count):
    wide = jnp.broadcast_to(block[None], (count,) + block.shape)
    return lax.all_to_all(wide, axes, 0, 0, tiled=True).reshape((-1,) + block.shape[1:])


def from_ahead(block, step):
    return lax.ppermute(block, ("q", "r"), [((i + step) % 16, i) for i in range(16)])


def nt_dot(a, b):
    return lax.dot_general(a, b, (((1,), (1,)), ((), ())), preferred_element_type=F32)


def attend_kernel(group_ref, rows_ref, bias_ref, *refs):
    prompt_refs, out_ref, order_ref = refs[:4], refs[4], refs[5]
    low_half = lax.broadcasted_iota(jnp.int32, (QL, 128), 1) < 64
    out_ref[...] = jnp.zeros_like(out_ref)
    count = jnp.int32(0)
    for i in range(16):
        order_ref[count] = jnp.int32(i)
        count = count + (group_ref[i] >= 0).astype(jnp.int32)

    def one_request(i):
        src = i // RQ
        row = pl.multiple_of((i % RQ) * QL, QL)
        group = group_ref[i]
        query = rows_ref[src, pl.ds(row, QL), :]
        zero = jnp.zeros_like(query)
        both = jnp.concatenate(
            [jnp.where(low_half, query, zero), jnp.where(low_half, zero, query)], axis=0
        )
        own_key = rows_ref[src, pl.ds(pl.multiple_of(NROW + row, QL), QL), :]
        own_value = rows_ref[src, pl.ds(pl.multiple_of(2 * NROW + row, QL), QL), :]
        parts = [nt_dot(both, own_key)]
        values = [own_value]
        for piece in range(4):
            start = pl.multiple_of(group * 256, 256)
            key = prompt_refs[piece][pl.ds(start, 128), :]
            values.append(prompt_refs[piece][pl.ds(pl.multiple_of(start + 128, 128), 128), :])
            bias = bias_ref[group, :, piece * 128 : (piece + 1) * 128]
            parts.append(nt_dot(both, key) + bias)
        top = jnp.max(parts[0], axis=-1, keepdims=True)
        wide = jnp.maximum(jnp.maximum(parts[1], parts[2]), jnp.maximum(parts[3], parts[4]))
        top = jnp.maximum(top, jnp.max(wide, axis=-1, keepdims=True))
        weights = [jnp.exp(part - top) for part in parts]
        wide = (weights[1] + weights[2]) + (weights[3] + weights[4])
        total = jnp.sum(weights[0], axis=-1, keepdims=True) + jnp.sum(wide, axis=-1, keepdims=True)
        mixed = jnp.zeros((2 * QL, 128), F32)
        for weight, value in zip(weights, values):
            mixed = mixed + jnp.dot(weight.astype(BF), value, preferred_element_type=F32)
        mixed = mixed / total
        return jnp.where(low_half, mixed[:QL], mixed[QL:]).astype(BF)

    def two_requests(step, carry):
        i = order_ref[2 * step]
        k = order_ref[jnp.where(2 * step + 1 < count, 2 * step + 1, 2 * step)]
        results = [one_request(i), one_request(k)]
        for j, result in zip((i, k), results):
            out_ref[j // RQ, pl.ds(pl.multiple_of((j % RQ) * QL, QL), QL), :] = result
        return carry

    lax.fori_loop(0, (count + 1) // 2, two_requests, 0)


def attend(groups, rows, prompt, bias):
    return pl.pallas_call(
        attend_kernel,
        out_shape=jax.ShapeDtypeStruct((4, NROW, 128), BF),
        in_specs=[
            pl.BlockSpec(memory_space=pltpu.SMEM),
        ]
        + [pl.BlockSpec(memory_space=pltpu.VMEM)] * 6,
        out_specs=pl.BlockSpec(memory_space=pltpu.VMEM),
        scratch_shapes=[pltpu.SMEM((17,), jnp.int32)],
        compiler_params=pltpu.CompilerParams(vmem_limit_bytes=16 << 20),
        cost_estimate=pl.CostEstimate(flops=1000, bytes_accessed=1000, transcendentals=0),
        name="attend",
    )(groups, rows, bias, *prompt)


def match_kernel(need_ref, first_ref, last_ref, query_ref, docs_ref, pick_ref, out_ref, sims_ref, best_ref, term_ref):
    best_ref[...] = jnp.zeros_like(best_ref)
    token = lax.broadcasted_iota(jnp.int32, (DT, 128), 0)

    def one_holder(z, carry):
        base = z * 4
        any_need = need_ref[base] + need_ref[base + 1] + need_ref[base + 2] + need_ref[base + 3]

        @pl.when(any_need > 0)
        def _():
            vectors = docs_ref[pl.ds(pl.multiple_of(z * DT, DT), DT), :]
            sims_ref[...] = nt_dot(vectors, query_ref[...])

            def one_doc(k, inner):
                doc = base + k

                @pl.when(need_ref[doc] > 0)
                def _():
                    inside = (token >= first_ref[doc]) & (token < last_ref[doc])
                    tops = []
                    for col in range(8):
                        block = sims_ref[:, col * 128 : (col + 1) * 128]
                        tops.append(jnp.max(jnp.where(inside, block, -1e30), axis=0, keepdims=True))
                    best_ref[doc] = jnp.concatenate(tops, axis=0)

                return inner

            lax.fori_loop(0, 4, one_doc, 0)

        return carry

    lax.fori_loop(0, 16, one_holder, 0)
    lane = lax.broadcasted_iota(jnp.int32, (128, 128), 0)
    request = lax.broadcasted_iota(jnp.int32, (128, 128), 1)
    member = (lane // 32 == request // RQ).astype(F32)
    sums = jnp.dot(
        best_ref[...].reshape(512, 128), member, preferred_element_type=F32, precision=lax.Precision.HIGHEST
    ).reshape(64, 8, 128)
    head = lax.broadcasted_iota(jnp.int32, (64, 8, 128), 1)
    request = lax.broadcasted_iota(jnp.int32, (64, 8, 128), 2)
    per_doc = jnp.sum(jnp.where(head // 2 == request % RQ, sums, 0.0), axis=1)
    doc_row = lax.broadcasted_iota(jnp.int32, (64, 128), 0)
    for c in range(NC):
        hit = doc_row == pick_ref[c : c + 1, :]
        term_ref[c : c + 1, :] = jnp.sum(jnp.where(hit, per_doc, 0.0), axis=0, keepdims=True)
    for i in range(32):
        out_ref[i] = term_ref[...]


def match(need, first, last, queries, docs, pick):
    return pl.pallas_call(
        match_kernel,
        out_shape=jax.ShapeDtypeStruct((32, NC, 128), F32),
        in_specs=[pl.BlockSpec(memory_space=pltpu.SMEM)] * 3 + [pl.BlockSpec(memory_space=pltpu.VMEM)] * 3,
        out_specs=pl.BlockSpec(memory_space=pltpu.VMEM),
        scratch_shapes=[pltpu.VMEM((DT, 1024), F32), pltpu.VMEM((64, 8, 128), F32), pltpu.VMEM((NC, 128), F32)],
        compiler_params=pltpu.CompilerParams(vmem_limit_bytes=16 << 20),
        cost_estimate=pl.CostEstimate(flops=1000, bytes_accessed=1000, transcendentals=0),
        name="match",
    )(need, first, last, queries, docs, pick)


def vmem_call(body, out_shape, name, smem=0):
    def call(*args):
        spaces = [pltpu.SMEM] * smem + [pltpu.VMEM] * (len(args) - smem)
        return pl.pallas_call(
            body,
            out_shape=out_shape,
            in_specs=[pl.BlockSpec(memory_space=space) for space in spaces],
            out_specs=jax.tree.map(lambda _: pl.BlockSpec(memory_space=pltpu.VMEM), out_shape),
            compiler_params=pltpu.CompilerParams(vmem_limit_bytes=16 << 20),
            cost_estimate=pl.CostEstimate(flops=1000, bytes_accessed=1000, transcendentals=0),
            name=name,
        )(*args)

    return call


def total_kernel(place_ref, terms_ref, out_ref):
    total = terms_ref[0]
    for i in range(1, 32):
        total = total + terms_ref[i]
    lane = lax.broadcasted_iota(jnp.int32, (8, 128), 1)
    row = lax.broadcasted_iota(jnp.int32, (8, 128), 0)
    wanted = (lane == place_ref[0] * RQ + row).astype(F32)
    picked = lax.dot_general(
        wanted, total, (((1,), (1,)), ((), ())), preferred_element_type=F32, precision=lax.Precision.HIGHEST
    )
    out_ref[...] = picked[:RQ]


def dense_kernel(context_ref, token_ref, gain_ref, *refs):
    held, first_ref, terms_ref, scratch, sems = refs[:3], refs[3], refs[4], refs[5:8], refs[8]
    copies = [pltpu.make_async_copy(held[i], scratch[i], sems.at[i]) for i in range(3)]
    for copy in copies:
        copy.start()
    w_out_ref, inner_ref, outer_ref = scratch
    context = jnp.concatenate([context_ref[h] for h in range(8)], axis=1)
    copies[0].wait()
    attn = token_ref[...].astype(F32) + jnp.dot(context, w_out_ref[...], preferred_element_type=F32)
    first = layer_norm(attn, gain_ref[...]).astype(BF)
    first_ref[...] = first
    copies[1].wait()
    inner = jnp.dot(first, inner_ref[...], preferred_element_type=F32)
    active = (0.5 * inner * (1.0 + lax.erf(inner * (0.5**0.5)))).astype(BF)
    copies[2].wait()
    total = jnp.dot(active, outer_ref[...], preferred_element_type=F32)
    terms_ref[...] = total.astype(BF).reshape(8, 32, 1024)


def dense(context, tokens, gain, weights):
    return pl.pallas_call(
        dense_kernel,
        out_shape=(jax.ShapeDtypeStruct((NROW, 1024), BF), jax.ShapeDtypeStruct((8, 32, 1024), BF)),
        in_specs=[pl.BlockSpec(memory_space=pltpu.VMEM)] * 3 + [pl.BlockSpec(memory_space=pl.ANY)] * 3,
        out_specs=(pl.BlockSpec(memory_space=pltpu.VMEM), pl.BlockSpec(memory_space=pltpu.VMEM)),
        scratch_shapes=[pltpu.VMEM(w.shape, w.dtype) for w in weights] + [pltpu.SemaphoreType.DMA((3,))],
        compiler_params=pltpu.CompilerParams(vmem_limit_bytes=52 << 20),
        cost_estimate=pl.CostEstimate(flops=1000, bytes_accessed=1000, transcendentals=0),
        name="dense",
    )(context, tokens, gain, *weights)


def embed_kernel(place_ref, first_ref, terms_ref, gain_ref, w_project_ref, out_ref):
    start = pl.multiple_of(place_ref[0] * 32, 32)
    total = first_ref[pl.ds(start, 32), :].astype(F32)
    for h in range(8):
        total = total + terms_ref[h].astype(F32)
    second = layer_norm(total, gain_ref[...]).astype(BF)
    projected = jnp.dot(second, w_project_ref[...], preferred_element_type=F32)
    scale = lax.rsqrt(jnp.sum(projected * projected, axis=-1, keepdims=True) + 1e-06)
    embed = (projected * scale).astype(BF)
    for i in range(32):
        out_ref[i] = embed


def per_device(
    tokens,
    w_query,
    w_key,
    w_value,
    w_out,
    norm1_gain,
    w_inner,
    w_outer,
    norm2_gain,
    w_project,
    key_pages,
    value_pages,
    page_table,
    prompt_lengths,
    request_group,
    doc_vectors,
    doc_lengths,
    candidates,
):
    my_y = lax.axis_index("y")
    my_head = lax.axis_index(HEAD)
    token_rows = tokens.reshape(NROW, 1024)

    pages = jnp.concatenate([key_pages.reshape(128, 128), value_pages.reshape(128, 128)], axis=0)
    pages_q = spread(pages, "q", 4)

    w_out_all = lax.all_gather(w_out, HEAD, axis=0, tiled=True)
    doc_rows = jnp.pad(doc_lengths.astype(BF), ((0, DPAD - DT - 1), (0, 124)))
    doc_block = jnp.concatenate([doc_vectors, doc_rows], axis=0)
    docs = lax.all_gather(doc_block, ("q", "r"), axis=0, tiled=True)

    query = jnp.dot(token_rows, w_query, preferred_element_type=F32).astype(BF) * BF(0.125)
    own_key = jnp.dot(token_rows, w_key, preferred_element_type=F32).astype(BF)
    own_value = jnp.dot(token_rows, w_value, preferred_element_type=F32).astype(BF)
    ids = jnp.concatenate([candidates // 64, candidates % 64, request_group[:, None]], axis=1)
    ids = jnp.pad(ids.astype(BF), ((0, 12), (0, 128 - 33)))
    rows = jnp.concatenate([query, own_key, own_value, ids], axis=0)
    rows = lax.all_gather(rows, "y", axis=0, tiled=True)
    pages_q, rows = lax.optimization_barrier((pages_q, rows))
    pages_q = pages_q.reshape(1024, 128)
    ahead_two = jnp.concatenate([from_ahead(pages_q[:512], 2), from_ahead(pages_q[512:], -2)], axis=0)
    prompt = [pages_q, from_ahead(pages_q, 1), ahead_two, from_ahead(pages_q, -1)]

    rows = rows.reshape(4, XROW, 128)
    got = rows[:, 3 * NROW : 3 * NROW + RQ, :33].reshape(16, 33).astype(jnp.int32)
    groups = jnp.where(got[:, 32] // 4 == my_y, got[:, 32] % 4, -1)
    pick = jnp.where(got[:, :16] == my_head * 4 + my_y, got[:, 16:32], -1)

    table = lax.dynamic_slice(page_table, (my_y * 32,), (32,)).reshape(4, 8)
    lengths = lax.dynamic_slice(prompt_lengths, (my_y * 4,), (4,))
    page_ids = (my_y * 32 + jnp.arange(32, dtype=jnp.int32)).reshape(4, 8)
    slot = jnp.sum(
        jnp.where(table[:, None, :] == page_ids[:, :, None], jnp.arange(8, dtype=jnp.int32), 0), axis=-1
    )
    position = slot[:, :, None] * 64 + jnp.arange(64, dtype=jnp.int32)
    bias = jnp.where(position < lengths[:, None, None], 0.0, -1e30).astype(F32).reshape(4, 4, 128)
    ahead = (lax.axis_index("r") + jnp.arange(4, dtype=jnp.int32)) % 4
    turn = ahead[:, None] == jnp.arange(4, dtype=jnp.int32)
    bias = jnp.sum(jnp.where(turn[None, :, :, None], bias[:, None], 0.0), axis=2).reshape(4, 1, 512)

    mixed = attend(groups, rows, prompt, bias)
    back = lax.all_to_all(mixed, "y", 0, 0, tiled=True)
    context = jnp.sum(back.astype(F32), axis=0).astype(BF)
    context = lax.all_gather(context, HEAD, axis=0, tiled=False)
    first, terms = dense(context, token_rows, norm1_gain[None], [w_out_all, w_inner, w_outer])
    terms = lax.all_to_all(terms, HEAD, 0, 0, tiled=True)
    embed = vmem_call(embed_kernel, jax.ShapeDtypeStruct((32, 32, 128), BF), "embed", 1)(
        my_head.reshape(1), first, terms, norm2_gain[None], w_project
    )

    queries = lax.all_to_all(embed, HEAD + ("y",), 0, 0, tiled=True)
    own = lax.dynamic_slice(queries.reshape(8, 4, 32, 128), (0, my_y, 0, 0), (8, 1, 32, 128))
    embedded = own.reshape(RQ, QL, 128)

    docs = lax.optimization_barrier((docs, embed))[0].reshape(16, DPAD, 128)
    doc_len = docs[:, DT, :4].astype(jnp.int32)
    docs = docs[:, :DT].reshape(16 * DT, 128)
    doc_last = jnp.cumsum(doc_len, axis=1)
    doc_first = doc_last - doc_len
    need = jnp.any(
        pick.reshape(1, 256) == jnp.arange(64, dtype=jnp.int32)[:, None], axis=1
    ).astype(jnp.int32)
    pick_lanes = jnp.pad(pick.T, ((0, 0), (0, 112)), constant_values=-1)
    terms = match(
        need, doc_first.reshape(64), doc_last.reshape(64), queries.reshape(1024, 128), docs, pick_lanes
    )
    terms = lax.all_to_all(terms, HEAD + ("y",), 0, 0, tiled=True)
    scores = vmem_call(total_kernel, jax.ShapeDtypeStruct((RQ, NC), F32), "total", 1)(my_y.reshape(1), terms)
    return (embedded, scores)


def solution(mesh):
    fine = Mesh(mesh.devices.reshape(4, 2, 4, 4, 4), HEAD + SHARD)
    in_specs = (
        P(SHARD, None, None),
        P(None, HEAD),
        P(None, HEAD),
        P(None, HEAD),
        P(HEAD, None),
        P(),
        P(None, HEAD),
        P(HEAD, None),
        P(),
        P(),
        P(SHARD, None, HEAD),
        P(SHARD, None, HEAD),
        P(),
        P(),
        P(SHARD),
        P(HEAD + SHARD, None),
        P(HEAD + SHARD, None),
        P(SHARD, None),
    )
    out_specs = (P(SHARD, None, None), P(SHARD, None))
    return jax.shard_map(per_device, mesh=fine, in_specs=in_specs, out_specs=out_specs, check_vma=False)
```

```python
import jax
import jax.numpy as jnp
from jax import lax
from jax.experimental import pallas as pl
from jax.experimental.pallas import tpu as pltpu
from jax.sharding import Mesh, PartitionSpec as P

HEAD = ("x", "c")
SHARD = ("y", "q", "r")
RQ = 4
QL = 64
NC = 16
NROW = RQ * QL
DT = 256
DPAD = 272
XROW = 3 * NROW + 16
BF = jnp.bfloat16
F32 = jnp.float32


def layer_norm(values, norm_gain):
    row_mean = jnp.mean(values, axis=-1, keepdims=True)
    row_var = jnp.mean(jnp.square(values - row_mean), axis=-1, keepdims=True)
    return (values - row_mean) * lax.rsqrt(row_var + 1e-05) * norm_gain


def spread(block, axes, count):
    wide = jnp.broadcast_to(block[None], (count,) + block.shape)
    return lax.all_to_all(wide, axes, 0, 0, tiled=True).reshape((-1,) + block.shape[1:])


def from_ahead(block, step):
    return lax.ppermute(block, ("q", "r"), [((i + step) % 16, i) for i in range(16)])


def nt_dot(a, b):
    return lax.dot_general(a, b, (((1,), (1,)), ((), ())), preferred_element_type=F32)


def attend_kernel(group_ref, rows_ref, bias_ref, *refs):
    prompt_refs, out_ref, order_ref = refs[:4], refs[4], refs[5]
    low_half = lax.broadcasted_iota(jnp.int32, (QL, 128), 1) < 64
    out_ref[...] = jnp.zeros_like(out_ref)
    count = jnp.int32(0)
    for i in range(16):
        order_ref[count] = jnp.int32(i)
        count = count + (group_ref[i] >= 0).astype(jnp.int32)

    def one_request(i):
        src = i // RQ
        row = pl.multiple_of((i % RQ) * QL, QL)
        group = group_ref[i]
        query = rows_ref[src, pl.ds(row, QL), :]
        zero = jnp.zeros_like(query)
        both = jnp.concatenate(
            [jnp.where(low_half, query, zero), jnp.where(low_half, zero, query)], axis=0
        )
        own_key = rows_ref[src, pl.ds(pl.multiple_of(NROW + row, QL), QL), :]
        own_value = rows_ref[src, pl.ds(pl.multiple_of(2 * NROW + row, QL), QL), :]
        parts = [nt_dot(both, own_key)]
        values = [own_value]
        for piece in range(4):
            start = pl.multiple_of(group * 256, 256)
            key = prompt_refs[piece][pl.ds(start, 128), :]
            values.append(prompt_refs[piece][pl.ds(pl.multiple_of(start + 128, 128), 128), :])
            bias = bias_ref[group, :, piece * 128 : (piece + 1) * 128]
            parts.append(nt_dot(both, key) + bias)
        top = jnp.max(parts[0], axis=-1, keepdims=True)
        wide = jnp.maximum(jnp.maximum(parts[1], parts[2]), jnp.maximum(parts[3], parts[4]))
        top = jnp.maximum(top, jnp.max(wide, axis=-1, keepdims=True))
        weights = [jnp.exp(part - top) for part in parts]
        wide = (weights[1] + weights[2]) + (weights[3] + weights[4])
        total = jnp.sum(weights[0], axis=-1, keepdims=True) + jnp.sum(wide, axis=-1, keepdims=True)
        mixed = jnp.zeros((2 * QL, 128), F32)
        for weight, value in zip(weights, values):
            mixed = mixed + jnp.dot(weight.astype(BF), value, preferred_element_type=F32)
        mixed = mixed / total
        return jnp.where(low_half, mixed[:QL], mixed[QL:]).astype(BF)

    def two_requests(step, carry):
        i = order_ref[2 * step]
        k = order_ref[jnp.where(2 * step + 1 < count, 2 * step + 1, 2 * step)]
        results = [one_request(i), one_request(k)]
        for j, result in zip((i, k), results):
            out_ref[j // RQ, pl.ds(pl.multiple_of((j % RQ) * QL, QL), QL), :] = result
        return carry

    lax.fori_loop(0, (count + 1) // 2, two_requests, 0)


def attend(groups, rows, prompt, bias):
    return pl.pallas_call(
        attend_kernel,
        out_shape=jax.ShapeDtypeStruct((4, NROW, 128), BF),
        in_specs=[
            pl.BlockSpec(memory_space=pltpu.SMEM),
        ]
        + [pl.BlockSpec(memory_space=pltpu.VMEM)] * 6,
        out_specs=pl.BlockSpec(memory_space=pltpu.VMEM),
        scratch_shapes=[pltpu.SMEM((17,), jnp.int32)],
        compiler_params=pltpu.CompilerParams(vmem_limit_bytes=16 << 20),
        cost_estimate=pl.CostEstimate(flops=1000, bytes_accessed=1000, transcendentals=0),
        name="attend",
    )(groups, rows, bias, *prompt)


def match_kernel(need_ref, first_ref, last_ref, query_ref, docs_ref, pick_ref, out_ref, sims_ref, best_ref, term_ref):
    best_ref[...] = jnp.zeros_like(best_ref)
    token = lax.broadcasted_iota(jnp.int32, (DT, 128), 0)

    def one_holder(z, carry):
        base = z * 4
        any_need = need_ref[base] + need_ref[base + 1] + need_ref[base + 2] + need_ref[base + 3]

        @pl.when(any_need > 0)
        def _():
            vectors = docs_ref[pl.ds(pl.multiple_of(z * DT, DT), DT), :]
            sims_ref[...] = nt_dot(vectors, query_ref[...])

            def one_doc(k, inner):
                doc = base + k

                @pl.when(need_ref[doc] > 0)
                def _():
                    inside = (token >= first_ref[doc]) & (token < last_ref[doc])
                    tops = []
                    for col in range(8):
                        block = sims_ref[:, col * 128 : (col + 1) * 128]
                        tops.append(jnp.max(jnp.where(inside, block, -1e30), axis=0, keepdims=True))
                    best_ref[doc] = jnp.concatenate(tops, axis=0)

                return inner

            lax.fori_loop(0, 4, one_doc, 0)

        return carry

    lax.fori_loop(0, 16, one_holder, 0)
    lane = lax.broadcasted_iota(jnp.int32, (128, 128), 0)
    request = lax.broadcasted_iota(jnp.int32, (128, 128), 1)
    member = (lane // 32 == request // RQ).astype(F32)
    sums = jnp.dot(
        best_ref[...].reshape(512, 128), member, preferred_element_type=F32, precision=lax.Precision.HIGHEST
    ).reshape(64, 8, 128)
    head = lax.broadcasted_iota(jnp.int32, (64, 8, 128), 1)
    request = lax.broadcasted_iota(jnp.int32, (64, 8, 128), 2)
    per_doc = jnp.sum(jnp.where(head // 2 == request % RQ, sums, 0.0), axis=1)
    doc_row = lax.broadcasted_iota(jnp.int32, (64, 128), 0)
    for c in range(NC):
        hit = doc_row == pick_ref[c : c + 1, :]
        term_ref[c : c + 1, :] = jnp.sum(jnp.where(hit, per_doc, 0.0), axis=0, keepdims=True)
    for i in range(32):
        out_ref[i] = term_ref[...]


def match(need, first, last, queries, docs, pick):
    return pl.pallas_call(
        match_kernel,
        out_shape=jax.ShapeDtypeStruct((32, NC, 128), F32),
        in_specs=[pl.BlockSpec(memory_space=pltpu.SMEM)] * 3 + [pl.BlockSpec(memory_space=pltpu.VMEM)] * 3,
        out_specs=pl.BlockSpec(memory_space=pltpu.VMEM),
        scratch_shapes=[pltpu.VMEM((DT, 1024), F32), pltpu.VMEM((64, 8, 128), F32), pltpu.VMEM((NC, 128), F32)],
        compiler_params=pltpu.CompilerParams(vmem_limit_bytes=16 << 20),
        cost_estimate=pl.CostEstimate(flops=1000, bytes_accessed=1000, transcendentals=0),
        name="match",
    )(need, first, last, queries, docs, pick)


def vmem_call(body, out_shape, name, smem=0):
    def call(*args):
        spaces = [pltpu.SMEM] * smem + [pltpu.VMEM] * (len(args) - smem)
        return pl.pallas_call(
            body,
            out_shape=out_shape,
            in_specs=[pl.BlockSpec(memory_space=space) for space in spaces],
            out_specs=jax.tree.map(lambda _: pl.BlockSpec(memory_space=pltpu.VMEM), out_shape),
            compiler_params=pltpu.CompilerParams(vmem_limit_bytes=16 << 20),
            cost_estimate=pl.CostEstimate(flops=1000, bytes_accessed=1000, transcendentals=0),
            name=name,
        )(*args)

    return call


def total_kernel(place_ref, terms_ref, out_ref):
    total = terms_ref[0]
    for i in range(1, 32):
        total = total + terms_ref[i]
    lane = lax.broadcasted_iota(jnp.int32, (8, 128), 1)
    row = lax.broadcasted_iota(jnp.int32, (8, 128), 0)
    wanted = (lane == place_ref[0] * RQ + row).astype(F32)
    picked = lax.dot_general(
        wanted, total, (((1,), (1,)), ((), ())), preferred_element_type=F32, precision=lax.Precision.HIGHEST
    )
    out_ref[...] = picked[:RQ]


def dense_kernel(context_ref, token_ref, gain_ref, *refs):
    held, first_ref, terms_ref, scratch, sems = refs[:3], refs[3], refs[4], refs[5:8], refs[8]
    copies = [pltpu.make_async_copy(held[i], scratch[i], sems.at[i]) for i in range(3)]
    for copy in copies:
        copy.start()
    w_out_ref, inner_ref, outer_ref = scratch
    context = jnp.concatenate([context_ref[h] for h in range(8)], axis=1)
    copies[0].wait()
    attn = token_ref[...].astype(F32) + jnp.dot(context, w_out_ref[...], preferred_element_type=F32)
    first = layer_norm(attn, gain_ref[...]).astype(BF)
    first_ref[...] = first
    copies[1].wait()
    inner = jnp.dot(first, inner_ref[...], preferred_element_type=F32)
    active = (0.5 * inner * (1.0 + lax.erf(inner * (0.5**0.5)))).astype(BF)
    copies[2].wait()
    total = jnp.dot(active, outer_ref[...], preferred_element_type=F32)
    terms_ref[...] = total.astype(BF).reshape(8, 32, 1024)


def dense(context, tokens, gain, weights):
    return pl.pallas_call(
        dense_kernel,
        out_shape=(jax.ShapeDtypeStruct((NROW, 1024), BF), jax.ShapeDtypeStruct((8, 32, 1024), BF)),
        in_specs=[pl.BlockSpec(memory_space=pltpu.VMEM)] * 3 + [pl.BlockSpec(memory_space=pl.ANY)] * 3,
        out_specs=(pl.BlockSpec(memory_space=pltpu.VMEM), pl.BlockSpec(memory_space=pltpu.VMEM)),
        scratch_shapes=[pltpu.VMEM(w.shape, w.dtype) for w in weights] + [pltpu.SemaphoreType.DMA((3,))],
        compiler_params=pltpu.CompilerParams(vmem_limit_bytes=52 << 20),
        cost_estimate=pl.CostEstimate(flops=1000, bytes_accessed=1000, transcendentals=0),
        name="dense",
    )(context, tokens, gain, *weights)


def embed_kernel(place_ref, first_ref, terms_ref, gain_ref, w_project_ref, out_ref):
    start = pl.multiple_of(place_ref[0] * 32, 32)
    total = first_ref[pl.ds(start, 32), :].astype(F32)
    for h in range(8):
        total = total + terms_ref[h].astype(F32)
    second = layer_norm(total, gain_ref[...]).astype(BF)
    projected = jnp.dot(second, w_project_ref[...], preferred_element_type=F32)
    scale = lax.rsqrt(jnp.sum(projected * projected, axis=-1, keepdims=True) + 1e-06)
    embed = (projected * scale).astype(BF)
    for i in range(32):
        out_ref[i] = embed


def per_device(
    tokens,
    w_query,
    w_key,
    w_value,
    w_out,
    norm1_gain,
    w_inner,
    w_outer,
    norm2_gain,
    w_project,
    key_pages,
    value_pages,
    page_table,
    prompt_lengths,
    request_group,
    doc_vectors,
    doc_lengths,
    candidates,
):
    my_y = lax.axis_index("y")
    my_head = lax.axis_index(HEAD)
    token_rows = tokens.reshape(NROW, 1024)

    pages = jnp.concatenate([key_pages.reshape(128, 128), value_pages.reshape(128, 128)], axis=0)
    pages_q = spread(pages, "q", 4)

    w_out_all = lax.all_gather(w_out, HEAD, axis=0, tiled=True)

    query = jnp.dot(token_rows, w_query, preferred_element_type=F32).astype(BF) * BF(0.125)
    own_key = jnp.dot(token_rows, w_key, preferred_element_type=F32).astype(BF)
    own_value = jnp.dot(token_rows, w_value, preferred_element_type=F32).astype(BF)
    ids = jnp.concatenate([candidates // 64, candidates % 64, request_group[:, None]], axis=1)
    ids = jnp.pad(ids.astype(BF), ((0, 12), (0, 128 - 33)))
    rows = jnp.concatenate([query, own_key, own_value, ids], axis=0)
    rows = lax.all_gather(rows, "y", axis=0, tiled=True)
    pages_q, rows = lax.optimization_barrier((pages_q, rows))
    pages_q = pages_q.reshape(1024, 128)
    ahead_two = from_ahead(pages_q, 2)
    prompt = [pages_q, from_ahead(pages_q, 1), ahead_two, from_ahead(pages_q, -1)]

    doc_vectors, page_table, pages_q = lax.optimization_barrier((doc_vectors, page_table, pages_q))
    doc_rows = jnp.pad(doc_lengths.astype(BF), ((0, DPAD - DT - 1), (0, 124)))
    doc_block = jnp.concatenate([doc_vectors, doc_rows], axis=0)
    docs = lax.all_gather(doc_block, ("q", "r"), axis=0, tiled=True)

    rows = rows.reshape(4, XROW, 128)
    got = rows[:, 3 * NROW : 3 * NROW + RQ, :33].reshape(16, 33).astype(jnp.int32)
    groups = jnp.where(got[:, 32] // 4 == my_y, got[:, 32] % 4, -1)
    pick = jnp.where(got[:, :16] == my_head * 4 + my_y, got[:, 16:32], -1)

    table = lax.dynamic_slice(page_table, (my_y * 32,), (32,)).reshape(4, 8)
    lengths = lax.dynamic_slice(prompt_lengths, (my_y * 4,), (4,))
    page_ids = (my_y * 32 + jnp.arange(32, dtype=jnp.int32)).reshape(4, 8)
    slot = jnp.sum(
        jnp.where(table[:, None, :] == page_ids[:, :, None], jnp.arange(8, dtype=jnp.int32), 0), axis=-1
    )
    position = slot[:, :, None] * 64 + jnp.arange(64, dtype=jnp.int32)
    bias = jnp.where(position < lengths[:, None, None], 0.0, -1e30).astype(F32).reshape(4, 4, 128)
    ahead = (lax.axis_index("r") + jnp.arange(4, dtype=jnp.int32)) % 4
    turn = ahead[:, None] == jnp.arange(4, dtype=jnp.int32)
    bias = jnp.sum(jnp.where(turn[None, :, :, None], bias[:, None], 0.0), axis=2).reshape(4, 1, 512)

    mixed = attend(groups, rows, prompt, bias)
    back = lax.all_to_all(mixed, "y", 0, 0, tiled=True)
    context = jnp.sum(back.astype(F32), axis=0).astype(BF)
    context = lax.all_gather(context, HEAD, axis=0, tiled=False)
    first, terms = dense(context, token_rows, norm1_gain[None], [w_out_all, w_inner, w_outer])
    terms = lax.all_to_all(terms, HEAD, 0, 0, tiled=True)
    embed = vmem_call(embed_kernel, jax.ShapeDtypeStruct((32, 32, 128), BF), "embed", 1)(
        my_head.reshape(1), first, terms, norm2_gain[None], w_project
    )

    queries = lax.all_to_all(embed, HEAD + ("y",), 0, 0, tiled=True)
    own = lax.dynamic_slice(queries.reshape(8, 4, 32, 128), (0, my_y, 0, 0), (8, 1, 32, 128))
    embedded = own.reshape(RQ, QL, 128)

    docs = lax.optimization_barrier((docs, embed))[0].reshape(16, DPAD, 128)
    doc_len = docs[:, DT, :4].astype(jnp.int32)
    docs = docs[:, :DT].reshape(16 * DT, 128)
    doc_last = jnp.cumsum(doc_len, axis=1)
    doc_first = doc_last - doc_len
    need = jnp.any(
        pick.reshape(1, 256) == jnp.arange(64, dtype=jnp.int32)[:, None], axis=1
    ).astype(jnp.int32)
    pick_lanes = jnp.pad(pick.T, ((0, 0), (0, 112)), constant_values=-1)
    terms = match(
        need, doc_first.reshape(64), doc_last.reshape(64), queries.reshape(1024, 128), docs, pick_lanes
    )
    terms = lax.all_to_all(terms, HEAD + ("y",), 0, 0, tiled=True)
    scores = vmem_call(total_kernel, jax.ShapeDtypeStruct((RQ, NC), F32), "total", 1)(my_y.reshape(1), terms)
    return (embedded, scores)


def solution(mesh):
    fine = Mesh(mesh.devices.reshape(4, 2, 4, 4, 4), HEAD + SHARD)
    in_specs = (
        P(SHARD, None, None),
        P(None, HEAD),
        P(None, HEAD),
        P(None, HEAD),
        P(HEAD, None),
        P(),
        P(None, HEAD),
        P(HEAD, None),
        P(),
        P(),
        P(SHARD, None, HEAD),
        P(SHARD, None, HEAD),
        P(),
        P(),
        P(SHARD),
        P(HEAD + SHARD, None),
        P(HEAD + SHARD, None),
        P(SHARD, None),
    )
    out_specs = (P(SHARD, None, None), P(SHARD, None))
    return jax.shard_map(per_device, mesh=fine, in_specs=in_specs, out_specs=out_specs, check_vma=False)
```

```python
import jax
import jax.numpy as jnp
from jax import lax
from jax.experimental import pallas as pl
from jax.experimental.pallas import tpu as pltpu
from jax.sharding import Mesh, PartitionSpec as P

HEAD = ("x", "c")
SHARD = ("y", "q", "r")
RQ = 4
QL = 64
NC = 16
NROW = RQ * QL
DT = 256
DPAD = 272
XROW = 3 * NROW + 16
BF = jnp.bfloat16
F32 = jnp.float32


def layer_norm(values, norm_gain):
    row_mean = jnp.mean(values, axis=-1, keepdims=True)
    row_var = jnp.mean(jnp.square(values - row_mean), axis=-1, keepdims=True)
    return (values - row_mean) * lax.rsqrt(row_var + 1e-05) * norm_gain


def spread(block, axes, count):
    wide = jnp.broadcast_to(block[None], (count,) + block.shape)
    return lax.all_to_all(wide, axes, 0, 0, tiled=True).reshape((-1,) + block.shape[1:])


def from_ahead(block, step):
    return lax.ppermute(block, ("q", "r"), [((i + step) % 16, i) for i in range(16)])


def nt_dot(a, b):
    return lax.dot_general(a, b, (((1,), (1,)), ((), ())), preferred_element_type=F32)


def attend_kernel(group_ref, rows_ref, bias_ref, *refs):
    prompt_refs, out_ref, order_ref = refs[:4], refs[4], refs[5]
    low_half = lax.broadcasted_iota(jnp.int32, (QL, 128), 1) < 64
    out_ref[...] = jnp.zeros_like(out_ref)
    count = jnp.int32(0)
    for i in range(16):
        order_ref[count] = jnp.int32(i)
        count = count + (group_ref[i] >= 0).astype(jnp.int32)

    def one_request(i):
        src = i // RQ
        row = pl.multiple_of((i % RQ) * QL, QL)
        group = group_ref[i]
        query = rows_ref[src, pl.ds(row, QL), :]
        zero = jnp.zeros_like(query)
        both = jnp.concatenate(
            [jnp.where(low_half, query, zero), jnp.where(low_half, zero, query)], axis=0
        )
        own_key = rows_ref[src, pl.ds(pl.multiple_of(NROW + row, QL), QL), :]
        own_value = rows_ref[src, pl.ds(pl.multiple_of(2 * NROW + row, QL), QL), :]
        parts = [nt_dot(both, own_key)]
        values = [own_value]
        for piece in range(4):
            start = pl.multiple_of(group * 256, 256)
            key = prompt_refs[piece][pl.ds(start, 128), :]
            values.append(prompt_refs[piece][pl.ds(pl.multiple_of(start + 128, 128), 128), :])
            bias = bias_ref[group, :, piece * 128 : (piece + 1) * 128]
            parts.append(nt_dot(both, key) + bias)
        top = jnp.max(parts[0], axis=-1, keepdims=True)
        wide = jnp.maximum(jnp.maximum(parts[1], parts[2]), jnp.maximum(parts[3], parts[4]))
        top = jnp.maximum(top, jnp.max(wide, axis=-1, keepdims=True))
        weights = [jnp.exp(part - top) for part in parts]
        wide = (weights[1] + weights[2]) + (weights[3] + weights[4])
        total = jnp.sum(weights[0], axis=-1, keepdims=True) + jnp.sum(wide, axis=-1, keepdims=True)
        mixed = jnp.zeros((2 * QL, 128), F32)
        for weight, value in zip(weights, values):
            mixed = mixed + jnp.dot(weight.astype(BF), value, preferred_element_type=F32)
        mixed = mixed / total
        return jnp.where(low_half, mixed[:QL], mixed[QL:]).astype(BF)

    def two_requests(step, carry):
        i = order_ref[2 * step]
        k = order_ref[jnp.where(2 * step + 1 < count, 2 * step + 1, 2 * step)]
        results = [one_request(i), one_request(k)]
        for j, result in zip((i, k), results):
            out_ref[j // RQ, pl.ds(pl.multiple_of((j % RQ) * QL, QL), QL), :] = result
        return carry

    lax.fori_loop(0, (count + 1) // 2, two_requests, 0)


def attend(groups, rows, prompt, bias):
    return pl.pallas_call(
        attend_kernel,
        out_shape=jax.ShapeDtypeStruct((4, NROW, 128), BF),
        in_specs=[
            pl.BlockSpec(memory_space=pltpu.SMEM),
        ]
        + [pl.BlockSpec(memory_space=pltpu.VMEM)] * 6,
        out_specs=pl.BlockSpec(memory_space=pltpu.VMEM),
        scratch_shapes=[pltpu.SMEM((17,), jnp.int32)],
        compiler_params=pltpu.CompilerParams(vmem_limit_bytes=16 << 20),
        cost_estimate=pl.CostEstimate(flops=1000, bytes_accessed=1000, transcendentals=0),
        name="attend",
    )(groups, rows, bias, *prompt)


def match_kernel(need_ref, first_ref, last_ref, query_ref, docs_ref, pick_ref, out_ref, sims_ref, best_ref, term_ref):
    best_ref[...] = jnp.zeros_like(best_ref)
    token = lax.broadcasted_iota(jnp.int32, (DT, 128), 0)

    def one_holder(z, carry):
        base = z * 4
        any_need = need_ref[base] + need_ref[base + 1] + need_ref[base + 2] + need_ref[base + 3]

        @pl.when(any_need > 0)
        def _():
            vectors = docs_ref[pl.ds(pl.multiple_of(z * DT, DT), DT), :]
            sims_ref[...] = nt_dot(vectors, query_ref[...])

            def one_doc(k, inner):
                doc = base + k

                @pl.when(need_ref[doc] > 0)
                def _():
                    inside = (token >= first_ref[doc]) & (token < last_ref[doc])
                    tops = []
                    for col in range(8):
                        block = sims_ref[:, col * 128 : (col + 1) * 128]
                        tops.append(jnp.max(jnp.where(inside, block, -1e30), axis=0, keepdims=True))
                    best_ref[doc] = jnp.concatenate(tops, axis=0)

                return inner

            lax.fori_loop(0, 4, one_doc, 0)

        return carry

    lax.fori_loop(0, 16, one_holder, 0)
    lane = lax.broadcasted_iota(jnp.int32, (128, 128), 0)
    request = lax.broadcasted_iota(jnp.int32, (128, 128), 1)
    member = (lane // 32 == request // RQ).astype(F32)
    sums = jnp.dot(
        best_ref[...].reshape(512, 128), member, preferred_element_type=F32, precision=lax.Precision.HIGHEST
    ).reshape(64, 8, 128)
    head = lax.broadcasted_iota(jnp.int32, (64, 8, 128), 1)
    request = lax.broadcasted_iota(jnp.int32, (64, 8, 128), 2)
    per_doc = jnp.sum(jnp.where(head // 2 == request % RQ, sums, 0.0), axis=1)
    doc_row = lax.broadcasted_iota(jnp.int32, (64, 128), 0)
    for c in range(NC):
        hit = doc_row == pick_ref[c : c + 1, :]
        term_ref[c : c + 1, :] = jnp.sum(jnp.where(hit, per_doc, 0.0), axis=0, keepdims=True)
    for i in range(32):
        out_ref[i] = term_ref[...]


def match(need, first, last, queries, docs, pick):
    return pl.pallas_call(
        match_kernel,
        out_shape=jax.ShapeDtypeStruct((32, NC, 128), F32),
        in_specs=[pl.BlockSpec(memory_space=pltpu.SMEM)] * 3 + [pl.BlockSpec(memory_space=pltpu.VMEM)] * 3,
        out_specs=pl.BlockSpec(memory_space=pltpu.VMEM),
        scratch_shapes=[pltpu.VMEM((DT, 1024), F32), pltpu.VMEM((64, 8, 128), F32), pltpu.VMEM((NC, 128), F32)],
        compiler_params=pltpu.CompilerParams(vmem_limit_bytes=16 << 20),
        cost_estimate=pl.CostEstimate(flops=1000, bytes_accessed=1000, transcendentals=0),
        name="match",
    )(need, first, last, queries, docs, pick)


def vmem_call(body, out_shape, name, smem=0):
    def call(*args):
        spaces = [pltpu.SMEM] * smem + [pltpu.VMEM] * (len(args) - smem)
        return pl.pallas_call(
            body,
            out_shape=out_shape,
            in_specs=[pl.BlockSpec(memory_space=space) for space in spaces],
            out_specs=jax.tree.map(lambda _: pl.BlockSpec(memory_space=pltpu.VMEM), out_shape),
            compiler_params=pltpu.CompilerParams(vmem_limit_bytes=16 << 20),
            cost_estimate=pl.CostEstimate(flops=1000, bytes_accessed=1000, transcendentals=0),
            name=name,
        )(*args)

    return call


def total_kernel(place_ref, terms_ref, out_ref):
    total = terms_ref[0]
    for i in range(1, 32):
        total = total + terms_ref[i]
    lane = lax.broadcasted_iota(jnp.int32, (8, 128), 1)
    row = lax.broadcasted_iota(jnp.int32, (8, 128), 0)
    wanted = (lane == place_ref[0] * RQ + row).astype(F32)
    picked = lax.dot_general(
        wanted, total, (((1,), (1,)), ((), ())), preferred_element_type=F32, precision=lax.Precision.HIGHEST
    )
    out_ref[...] = picked[:RQ]


def dense_kernel(context_ref, token_ref, gain_ref, *refs):
    held, first_ref, terms_ref, scratch, sems = refs[:3], refs[3], refs[4], refs[5:8], refs[8]
    copies = [pltpu.make_async_copy(held[i], scratch[i], sems.at[i]) for i in range(3)]
    for copy in copies:
        copy.start()
    w_out_ref, inner_ref, outer_ref = scratch
    context = jnp.concatenate([context_ref[h] for h in range(8)], axis=1)
    copies[0].wait()
    attn = token_ref[...].astype(F32) + jnp.dot(context, w_out_ref[...], preferred_element_type=F32)
    first = layer_norm(attn, gain_ref[...]).astype(BF)
    first_ref[...] = first
    copies[1].wait()
    inner = jnp.dot(first, inner_ref[...], preferred_element_type=F32)
    active = (0.5 * inner * (1.0 + lax.erf(inner * (0.5**0.5)))).astype(BF)
    copies[2].wait()
    total = jnp.dot(active, outer_ref[...], preferred_element_type=F32)
    terms_ref[...] = total.astype(BF).reshape(8, 32, 1024)


def dense(context, tokens, gain, weights):
    return pl.pallas_call(
        dense_kernel,
        out_shape=(jax.ShapeDtypeStruct((NROW, 1024), BF), jax.ShapeDtypeStruct((8, 32, 1024), BF)),
        in_specs=[pl.BlockSpec(memory_space=pltpu.VMEM)] * 3 + [pl.BlockSpec(memory_space=pl.ANY)] * 3,
        out_specs=(pl.BlockSpec(memory_space=pltpu.VMEM), pl.BlockSpec(memory_space=pltpu.VMEM)),
        scratch_shapes=[pltpu.VMEM(w.shape, w.dtype) for w in weights] + [pltpu.SemaphoreType.DMA((3,))],
        compiler_params=pltpu.CompilerParams(vmem_limit_bytes=52 << 20),
        cost_estimate=pl.CostEstimate(flops=1000, bytes_accessed=1000, transcendentals=0),
        name="dense",
    )(context, tokens, gain, *weights)


def embed_kernel(place_ref, first_ref, terms_ref, gain_ref, w_project_ref, out_ref):
    start = pl.multiple_of(place_ref[0] * 32, 32)
    total = first_ref[pl.ds(start, 32), :].astype(F32)
    for h in range(8):
        total = total + terms_ref[h].astype(F32)
    second = layer_norm(total, gain_ref[...]).astype(BF)
    projected = jnp.dot(second, w_project_ref[...], preferred_element_type=F32)
    scale = lax.rsqrt(jnp.sum(projected * projected, axis=-1, keepdims=True) + 1e-06)
    embed = (projected * scale).astype(BF)
    for i in range(32):
        out_ref[i] = embed


def per_device(
    tokens,
    w_query,
    w_key,
    w_value,
    w_out,
    norm1_gain,
    w_inner,
    w_outer,
    norm2_gain,
    w_project,
    key_pages,
    value_pages,
    page_table,
    prompt_lengths,
    request_group,
    doc_vectors,
    doc_lengths,
    candidates,
):
    my_y = lax.axis_index("y")
    my_head = lax.axis_index(HEAD)
    token_rows = tokens.reshape(NROW, 1024)

    pages = jnp.concatenate([key_pages.reshape(128, 128), value_pages.reshape(128, 128)], axis=0)
    pages_q = spread(pages, "q", 4)

    w_out_all = lax.all_gather(w_out, HEAD, axis=0, tiled=True)

    query = jnp.dot(token_rows, w_query, preferred_element_type=F32).astype(BF) * BF(0.125)
    own_key = jnp.dot(token_rows, w_key, preferred_element_type=F32).astype(BF)
    own_value = jnp.dot(token_rows, w_value, preferred_element_type=F32).astype(BF)
    ids = jnp.concatenate([candidates // 64, candidates % 64, request_group[:, None]], axis=1)
    ids = jnp.pad(ids.astype(BF), ((0, 12), (0, 128 - 33)))
    rows = jnp.concatenate([query, own_key, own_value, ids], axis=0)
    rows = lax.all_gather(rows, "y", axis=0, tiled=True)
    pages_q, rows = lax.optimization_barrier((pages_q, rows))
    pages_q = pages_q.reshape(1024, 128)
    pairs = [((i + 2 if i % 2 == 0 else i - 2) % 16, i) for i in range(16)]
    ahead_two = lax.ppermute(pages_q, ("q", "r"), pairs)
    prompt = [pages_q, from_ahead(pages_q, 1), ahead_two, from_ahead(pages_q, -1)]

    doc_vectors, page_table, pages_q = lax.optimization_barrier((doc_vectors, page_table, pages_q))
    doc_rows = jnp.pad(doc_lengths.astype(BF), ((0, DPAD - DT - 1), (0, 124)))
    doc_block = jnp.concatenate([doc_vectors, doc_rows], axis=0)
    docs = lax.all_gather(doc_block, ("q", "r"), axis=0, tiled=True)

    rows = rows.reshape(4, XROW, 128)
    got = rows[:, 3 * NROW : 3 * NROW + RQ, :33].reshape(16, 33).astype(jnp.int32)
    groups = jnp.where(got[:, 32] // 4 == my_y, got[:, 32] % 4, -1)
    pick = jnp.where(got[:, :16] == my_head * 4 + my_y, got[:, 16:32], -1)

    table = lax.dynamic_slice(page_table, (my_y * 32,), (32,)).reshape(4, 8)
    lengths = lax.dynamic_slice(prompt_lengths, (my_y * 4,), (4,))
    page_ids = (my_y * 32 + jnp.arange(32, dtype=jnp.int32)).reshape(4, 8)
    slot = jnp.sum(
        jnp.where(table[:, None, :] == page_ids[:, :, None], jnp.arange(8, dtype=jnp.int32), 0), axis=-1
    )
    position = slot[:, :, None] * 64 + jnp.arange(64, dtype=jnp.int32)
    bias = jnp.where(position < lengths[:, None, None], 0.0, -1e30).astype(F32).reshape(4, 4, 128)
    ahead = (lax.axis_index("r") + jnp.arange(4, dtype=jnp.int32)) % 4
    turn = ahead[:, None] == jnp.arange(4, dtype=jnp.int32)
    bias = jnp.sum(jnp.where(turn[None, :, :, None], bias[:, None], 0.0), axis=2).reshape(4, 1, 512)

    mixed = attend(groups, rows, prompt, bias)
    back = lax.all_to_all(mixed, "y", 0, 0, tiled=True)
    context = jnp.sum(back.astype(F32), axis=0).astype(BF)
    context = lax.all_gather(context, HEAD, axis=0, tiled=False)
    first, terms = dense(context, token_rows, norm1_gain[None], [w_out_all, w_inner, w_outer])
    terms = lax.all_to_all(terms, HEAD, 0, 0, tiled=True)
    embed = vmem_call(embed_kernel, jax.ShapeDtypeStruct((32, 32, 128), BF), "embed", 1)(
        my_head.reshape(1), first, terms, norm2_gain[None], w_project
    )

    queries = lax.all_to_all(embed, HEAD + ("y",), 0, 0, tiled=True)
    own = lax.dynamic_slice(queries.reshape(8, 4, 32, 128), (0, my_y, 0, 0), (8, 1, 32, 128))
    embedded = own.reshape(RQ, QL, 128)

    docs = lax.optimization_barrier((docs, embed))[0].reshape(16, DPAD, 128)
    doc_len = docs[:, DT, :4].astype(jnp.int32)
    docs = docs[:, :DT].reshape(16 * DT, 128)
    doc_last = jnp.cumsum(doc_len, axis=1)
    doc_first = doc_last - doc_len
    need = jnp.any(
        pick.reshape(1, 256) == jnp.arange(64, dtype=jnp.int32)[:, None], axis=1
    ).astype(jnp.int32)
    pick_lanes = jnp.pad(pick.T, ((0, 0), (0, 112)), constant_values=-1)
    terms = match(
        need, doc_first.reshape(64), doc_last.reshape(64), queries.reshape(1024, 128), docs, pick_lanes
    )
    terms = lax.all_to_all(terms, HEAD + ("y",), 0, 0, tiled=True)
    scores = vmem_call(total_kernel, jax.ShapeDtypeStruct((RQ, NC), F32), "total", 1)(my_y.reshape(1), terms)
    return (embedded, scores)


def solution(mesh):
    fine = Mesh(mesh.devices.reshape(4, 2, 4, 4, 4), HEAD + SHARD)
    in_specs = (
        P(SHARD, None, None),
        P(None, HEAD),
        P(None, HEAD),
        P(None, HEAD),
        P(HEAD, None),
        P(),
        P(None, HEAD),
        P(HEAD, None),
        P(),
        P(),
        P(SHARD, None, HEAD),
        P(SHARD, None, HEAD),
        P(),
        P(),
        P(SHARD),
        P(HEAD + SHARD, None),
        P(HEAD + SHARD, None),
        P(SHARD, None),
    )
    out_specs = (P(SHARD, None, None), P(SHARD, None))
    return jax.shard_map(per_device, mesh=fine, in_specs=in_specs, out_specs=out_specs, check_vma=False)
```

```python
import jax
import jax.numpy as jnp
from jax import lax
from jax.experimental import pallas as pl
from jax.experimental.pallas import tpu as pltpu
from jax.sharding import Mesh, PartitionSpec as P

HEAD = ("x", "c")
SHARD = ("y", "q", "r")
RQ = 4
QL = 64
NC = 16
NROW = RQ * QL
DT = 256
DPAD = 272
XROW = 3 * NROW + 16
BF = jnp.bfloat16
F32 = jnp.float32


def layer_norm(values, norm_gain):
    row_mean = jnp.mean(values, axis=-1, keepdims=True)
    row_var = jnp.mean(jnp.square(values - row_mean), axis=-1, keepdims=True)
    return (values - row_mean) * lax.rsqrt(row_var + 1e-05) * norm_gain


def spread(block, axes, count):
    wide = jnp.broadcast_to(block[None], (count,) + block.shape)
    return lax.all_to_all(wide, axes, 0, 0, tiled=True).reshape((-1,) + block.shape[1:])


def from_ahead(block, step):
    return lax.ppermute(block, ("q", "r"), [((i + step) % 16, i) for i in range(16)])


def nt_dot(a, b):
    return lax.dot_general(a, b, (((1,), (1,)), ((), ())), preferred_element_type=F32)


def attend_kernel(group_ref, rows_ref, bias_ref, *refs):
    prompt_refs, out_ref, order_ref = refs[:4], refs[4], refs[5]
    low_half = lax.broadcasted_iota(jnp.int32, (QL, 128), 1) < 64
    out_ref[...] = jnp.zeros_like(out_ref)
    count = jnp.int32(0)
    for i in range(16):
        order_ref[count] = jnp.int32(i)
        count = count + (group_ref[i] >= 0).astype(jnp.int32)

    def one_request(i):
        src = i // RQ
        row = pl.multiple_of((i % RQ) * QL, QL)
        group = group_ref[i]
        query = rows_ref[src, pl.ds(row, QL), :]
        zero = jnp.zeros_like(query)
        both = jnp.concatenate(
            [jnp.where(low_half, query, zero), jnp.where(low_half, zero, query)], axis=0
        )
        own_key = rows_ref[src, pl.ds(pl.multiple_of(NROW + row, QL), QL), :]
        own_value = rows_ref[src, pl.ds(pl.multiple_of(2 * NROW + row, QL), QL), :]
        parts = [nt_dot(both, own_key)]
        values = [own_value]
        for piece in range(4):
            start = pl.multiple_of(group * 256, 256)
            key = prompt_refs[piece][pl.ds(start, 128), :]
            values.append(prompt_refs[piece][pl.ds(pl.multiple_of(start + 128, 128), 128), :])
            bias = bias_ref[group, :, piece * 128 : (piece + 1) * 128]
            parts.append(nt_dot(both, key) + bias)
        top = jnp.max(parts[0], axis=-1, keepdims=True)
        wide = jnp.maximum(jnp.maximum(parts[1], parts[2]), jnp.maximum(parts[3], parts[4]))
        top = jnp.maximum(top, jnp.max(wide, axis=-1, keepdims=True))
        weights = [jnp.exp(part - top) for part in parts]
        wide = (weights[1] + weights[2]) + (weights[3] + weights[4])
        total = jnp.sum(weights[0], axis=-1, keepdims=True) + jnp.sum(wide, axis=-1, keepdims=True)
        mixed = jnp.zeros((2 * QL, 128), F32)
        for weight, value in zip(weights, values):
            mixed = mixed + jnp.dot(weight.astype(BF), value, preferred_element_type=F32)
        mixed = mixed / total
        return jnp.where(low_half, mixed[:QL], mixed[QL:]).astype(BF)

    def two_requests(step, carry):
        i = order_ref[2 * step]
        k = order_ref[jnp.where(2 * step + 1 < count, 2 * step + 1, 2 * step)]
        results = [one_request(i), one_request(k)]
        for j, result in zip((i, k), results):
            out_ref[j // RQ, pl.ds(pl.multiple_of((j % RQ) * QL, QL), QL), :] = result
        return carry

    lax.fori_loop(0, (count + 1) // 2, two_requests, 0)


def attend(groups, rows, prompt, bias):
    return pl.pallas_call(
        attend_kernel,
        out_shape=jax.ShapeDtypeStruct((4, NROW, 128), BF),
        in_specs=[
            pl.BlockSpec(memory_space=pltpu.SMEM),
        ]
        + [pl.BlockSpec(memory_space=pltpu.VMEM)] * 6,
        out_specs=pl.BlockSpec(memory_space=pltpu.VMEM),
        scratch_shapes=[pltpu.SMEM((17,), jnp.int32)],
        compiler_params=pltpu.CompilerParams(vmem_limit_bytes=16 << 20),
        cost_estimate=pl.CostEstimate(flops=1000, bytes_accessed=1000, transcendentals=0),
        name="attend",
    )(groups, rows, bias, *prompt)


def match_kernel(need_ref, first_ref, last_ref, query_ref, docs_ref, pick_ref, out_ref, sims_ref, best_ref, term_ref):
    best_ref[...] = jnp.zeros_like(best_ref)
    token = lax.broadcasted_iota(jnp.int32, (DT, 128), 0)

    def one_holder(z, carry):
        base = z * 4
        any_need = need_ref[base] + need_ref[base + 1] + need_ref[base + 2] + need_ref[base + 3]

        @pl.when(any_need > 0)
        def _():
            vectors = docs_ref[pl.ds(pl.multiple_of(z * DT, DT), DT), :]
            sims_ref[...] = nt_dot(vectors, query_ref[...])

            def one_doc(k, inner):
                doc = base + k

                @pl.when(need_ref[doc] > 0)
                def _():
                    inside = (token >= first_ref[doc]) & (token < last_ref[doc])
                    tops = []
                    for col in range(8):
                        block = sims_ref[:, col * 128 : (col + 1) * 128]
                        tops.append(jnp.max(jnp.where(inside, block, -1e30), axis=0, keepdims=True))
                    best_ref[doc] = jnp.concatenate(tops, axis=0)

                return inner

            lax.fori_loop(0, 4, one_doc, 0)

        return carry

    lax.fori_loop(0, 16, one_holder, 0)
    lane = lax.broadcasted_iota(jnp.int32, (128, 128), 0)
    request = lax.broadcasted_iota(jnp.int32, (128, 128), 1)
    member = (lane // 32 == request // RQ).astype(F32)
    sums = jnp.dot(
        best_ref[...].reshape(512, 128), member, preferred_element_type=F32, precision=lax.Precision.HIGHEST
    ).reshape(64, 8, 128)
    head = lax.broadcasted_iota(jnp.int32, (64, 8, 128), 1)
    request = lax.broadcasted_iota(jnp.int32, (64, 8, 128), 2)
    per_doc = jnp.sum(jnp.where(head // 2 == request % RQ, sums, 0.0), axis=1)
    doc_row = lax.broadcasted_iota(jnp.int32, (64, 128), 0)
    for c in range(NC):
        hit = doc_row == pick_ref[c : c + 1, :]
        term_ref[c : c + 1, :] = jnp.sum(jnp.where(hit, per_doc, 0.0), axis=0, keepdims=True)
    for i in range(32):
        out_ref[i] = term_ref[...]


def match(need, first, last, queries, docs, pick):
    return pl.pallas_call(
        match_kernel,
        out_shape=jax.ShapeDtypeStruct((32, NC, 128), F32),
        in_specs=[pl.BlockSpec(memory_space=pltpu.SMEM)] * 3 + [pl.BlockSpec(memory_space=pltpu.VMEM)] * 3,
        out_specs=pl.BlockSpec(memory_space=pltpu.VMEM),
        scratch_shapes=[pltpu.VMEM((DT, 1024), F32), pltpu.VMEM((64, 8, 128), F32), pltpu.VMEM((NC, 128), F32)],
        compiler_params=pltpu.CompilerParams(vmem_limit_bytes=16 << 20),
        cost_estimate=pl.CostEstimate(flops=1000, bytes_accessed=1000, transcendentals=0),
        name="match",
    )(need, first, last, queries, docs, pick)


def vmem_call(body, out_shape, name, smem=0):
    def call(*args):
        spaces = [pltpu.SMEM] * smem + [pltpu.VMEM] * (len(args) - smem)
        return pl.pallas_call(
            body,
            out_shape=out_shape,
            in_specs=[pl.BlockSpec(memory_space=space) for space in spaces],
            out_specs=jax.tree.map(lambda _: pl.BlockSpec(memory_space=pltpu.VMEM), out_shape),
            compiler_params=pltpu.CompilerParams(vmem_limit_bytes=16 << 20),
            cost_estimate=pl.CostEstimate(flops=1000, bytes_accessed=1000, transcendentals=0),
            name=name,
        )(*args)

    return call


def total_kernel(place_ref, terms_ref, out_ref):
    total = terms_ref[0]
    for i in range(1, 32):
        total = total + terms_ref[i]
    lane = lax.broadcasted_iota(jnp.int32, (8, 128), 1)
    row = lax.broadcasted_iota(jnp.int32, (8, 128), 0)
    wanted = (lane == place_ref[0] * RQ + row).astype(F32)
    picked = lax.dot_general(
        wanted, total, (((1,), (1,)), ((), ())), preferred_element_type=F32, precision=lax.Precision.HIGHEST
    )
    out_ref[...] = picked[:RQ]


def dense_kernel(context_ref, token_ref, gain_ref, *refs):
    held, first_ref, terms_ref, scratch, sems = refs[:3], refs[3], refs[4], refs[5:8], refs[8]
    copies = [pltpu.make_async_copy(held[i], scratch[i], sems.at[i]) for i in range(3)]
    for copy in copies:
        copy.start()
    w_out_ref, inner_ref, outer_ref = scratch
    context = jnp.concatenate([context_ref[h] for h in range(8)], axis=1)
    copies[0].wait()
    attn = token_ref[...].astype(F32) + jnp.dot(context, w_out_ref[...], preferred_element_type=F32)
    first = layer_norm(attn, gain_ref[...]).astype(BF)
    first_ref[...] = first
    copies[1].wait()
    inner = jnp.dot(first, inner_ref[...], preferred_element_type=F32)
    active = (0.5 * inner * (1.0 + lax.erf(inner * (0.5**0.5)))).astype(BF)
    copies[2].wait()
    total = jnp.dot(active, outer_ref[...], preferred_element_type=F32)
    terms_ref[...] = total.astype(BF).reshape(8, 32, 1024)


def dense(context, tokens, gain, weights):
    return pl.pallas_call(
        dense_kernel,
        out_shape=(jax.ShapeDtypeStruct((NROW, 1024), BF), jax.ShapeDtypeStruct((8, 32, 1024), BF)),
        in_specs=[pl.BlockSpec(memory_space=pltpu.VMEM)] * 3 + [pl.BlockSpec(memory_space=pl.ANY)] * 3,
        out_specs=(pl.BlockSpec(memory_space=pltpu.VMEM), pl.BlockSpec(memory_space=pltpu.VMEM)),
        scratch_shapes=[pltpu.VMEM(w.shape, w.dtype) for w in weights] + [pltpu.SemaphoreType.DMA((3,))],
        compiler_params=pltpu.CompilerParams(vmem_limit_bytes=52 << 20),
        cost_estimate=pl.CostEstimate(flops=1000, bytes_accessed=1000, transcendentals=0),
        name="dense",
    )(context, tokens, gain, *weights)


def embed_kernel(place_ref, first_ref, terms_ref, gain_ref, w_project_ref, out_ref):
    start = pl.multiple_of(place_ref[0] * 32, 32)
    total = first_ref[pl.ds(start, 32), :].astype(F32)
    for h in range(8):
        total = total + terms_ref[h].astype(F32)
    second = layer_norm(total, gain_ref[...]).astype(BF)
    projected = jnp.dot(second, w_project_ref[...], preferred_element_type=F32)
    scale = lax.rsqrt(jnp.sum(projected * projected, axis=-1, keepdims=True) + 1e-06)
    embed = (projected * scale).astype(BF)
    for i in range(32):
        out_ref[i] = embed


def per_device(
    tokens,
    w_query,
    w_key,
    w_value,
    w_out,
    norm1_gain,
    w_inner,
    w_outer,
    norm2_gain,
    w_project,
    key_pages,
    value_pages,
    page_table,
    prompt_lengths,
    request_group,
    doc_vectors,
    doc_lengths,
    candidates,
):
    my_y = lax.axis_index("y")
    my_head = lax.axis_index(HEAD)
    token_rows = tokens.reshape(NROW, 1024)

    pages = jnp.concatenate([key_pages.reshape(128, 128), value_pages.reshape(128, 128)], axis=0)
    pages_q = spread(pages, "q", 4)

    w_out_all = lax.all_gather(w_out, HEAD, axis=0, tiled=True)

    query = jnp.dot(token_rows, w_query, preferred_element_type=F32).astype(BF) * BF(0.125)
    own_key = jnp.dot(token_rows, w_key, preferred_element_type=F32).astype(BF)
    own_value = jnp.dot(token_rows, w_value, preferred_element_type=F32).astype(BF)
    ids = jnp.pad(request_group.astype(BF)[:, None], ((0, 12), (0, 127)))
    rows = jnp.concatenate([query, own_key, own_value, ids], axis=0)
    rows = lax.all_gather(rows, "y", axis=0, tiled=True)
    pages_q, rows = lax.optimization_barrier((pages_q, rows))
    pages_q = pages_q.reshape(1024, 128)
    pairs = [((i + 2 if i % 2 == 0 else i - 2) % 16, i) for i in range(16)]
    ahead_two = lax.ppermute(pages_q, ("q", "r"), pairs)
    prompt = [pages_q, from_ahead(pages_q, 1), ahead_two, from_ahead(pages_q, -1)]

    doc_vectors, page_table, pages_q = lax.optimization_barrier((doc_vectors, page_table, pages_q))
    doc_rows = jnp.pad(doc_lengths.astype(BF), ((0, DPAD - DT - 1), (0, 124)))
    doc_block = jnp.concatenate([doc_vectors, doc_rows], axis=0)
    docs = lax.all_gather(doc_block, ("q", "r"), axis=0, tiled=True)

    rows = rows.reshape(4, XROW, 128)
    got = rows[:, 3 * NROW : 3 * NROW + RQ, 0].reshape(16).astype(jnp.int32)
    groups = jnp.where(got // 4 == my_y, got % 4, -1)

    table = lax.dynamic_slice(page_table, (my_y * 32,), (32,)).reshape(4, 8)
    lengths = lax.dynamic_slice(prompt_lengths, (my_y * 4,), (4,))
    page_ids = (my_y * 32 + jnp.arange(32, dtype=jnp.int32)).reshape(4, 8)
    slot = jnp.sum(
        jnp.where(table[:, None, :] == page_ids[:, :, None], jnp.arange(8, dtype=jnp.int32), 0), axis=-1
    )
    position = slot[:, :, None] * 64 + jnp.arange(64, dtype=jnp.int32)
    bias = jnp.where(position < lengths[:, None, None], 0.0, -1e30).astype(F32).reshape(4, 4, 128)
    ahead = (lax.axis_index("r") + jnp.arange(4, dtype=jnp.int32)) % 4
    turn = ahead[:, None] == jnp.arange(4, dtype=jnp.int32)
    bias = jnp.sum(jnp.where(turn[None, :, :, None], bias[:, None], 0.0), axis=2).reshape(4, 1, 512)

    mixed = attend(groups, rows, prompt, bias)
    back = lax.all_to_all(mixed, "y", 0, 0, tiled=True)
    context = jnp.sum(back.astype(F32), axis=0).astype(BF)
    context = lax.all_gather(context, HEAD, axis=0, tiled=False)
    first, terms = dense(context, token_rows, norm1_gain[None], [w_out_all, w_inner, w_outer])
    candidates, terms = lax.optimization_barrier((candidates, terms))
    asked = lax.all_gather(candidates, "y", axis=0, tiled=True)
    pick = jnp.where(asked // 64 == my_head * 4 + my_y, asked % 64, -1)
    terms = lax.all_to_all(terms, HEAD, 0, 0, tiled=True)
    embed = vmem_call(embed_kernel, jax.ShapeDtypeStruct((32, 32, 128), BF), "embed", 1)(
        my_head.reshape(1), first, terms, norm2_gain[None], w_project
    )

    queries = lax.all_to_all(embed, HEAD + ("y",), 0, 0, tiled=True)
    own = lax.dynamic_slice(queries.reshape(8, 4, 32, 128), (0, my_y, 0, 0), (8, 1, 32, 128))
    embedded = own.reshape(RQ, QL, 128)

    docs = lax.optimization_barrier((docs, embed))[0].reshape(16, DPAD, 128)
    doc_len = docs[:, DT, :4].astype(jnp.int32)
    docs = docs[:, :DT].reshape(16 * DT, 128)
    doc_last = jnp.cumsum(doc_len, axis=1)
    doc_first = doc_last - doc_len
    need = jnp.any(
        pick.reshape(1, 256) == jnp.arange(64, dtype=jnp.int32)[:, None], axis=1
    ).astype(jnp.int32)
    pick_lanes = jnp.pad(pick.T, ((0, 0), (0, 112)), constant_values=-1)
    terms = match(
        need, doc_first.reshape(64), doc_last.reshape(64), queries.reshape(1024, 128), docs, pick_lanes
    )
    terms = lax.all_to_all(terms, HEAD + ("y",), 0, 0, tiled=True)
    scores = vmem_call(total_kernel, jax.ShapeDtypeStruct((RQ, NC), F32), "total", 1)(my_y.reshape(1), terms)
    return (embedded, scores)


def solution(mesh):
    fine = Mesh(mesh.devices.reshape(4, 2, 4, 4, 4), HEAD + SHARD)
    in_specs = (
        P(SHARD, None, None),
        P(None, HEAD),
        P(None, HEAD),
        P(None, HEAD),
        P(HEAD, None),
        P(),
        P(None, HEAD),
        P(HEAD, None),
        P(),
        P(),
        P(SHARD, None, HEAD),
        P(SHARD, None, HEAD),
        P(),
        P(),
        P(SHARD),
        P(HEAD + SHARD, None),
        P(HEAD + SHARD, None),
        P(SHARD, None),
    )
    out_specs = (P(SHARD, None, None), P(SHARD, None))
    return jax.shard_map(per_device, mesh=fine, in_specs=in_specs, out_specs=out_specs, check_vma=False)
```

```python
import jax
import jax.numpy as jnp
from jax import lax
from jax.experimental import pallas as pl
from jax.experimental.pallas import tpu as pltpu
from jax.sharding import Mesh, PartitionSpec as P

HEAD = ("x", "c")
SHARD = ("y", "q", "r")
RQ = 4
QL = 64
NC = 16
NROW = RQ * QL
DT = 256
DPAD = 272
XROW = 3 * NROW + 16
BF = jnp.bfloat16
F32 = jnp.float32


def layer_norm(values, norm_gain):
    row_mean = jnp.mean(values, axis=-1, keepdims=True)
    row_var = jnp.mean(jnp.square(values - row_mean), axis=-1, keepdims=True)
    return (values - row_mean) * lax.rsqrt(row_var + 1e-05) * norm_gain


def spread(block, axes, count):
    wide = jnp.broadcast_to(block[None], (count,) + block.shape)
    return lax.all_to_all(wide, axes, 0, 0, tiled=True).reshape((-1,) + block.shape[1:])


def from_ahead(block, step):
    return lax.ppermute(block, ("q", "r"), [((i + step) % 16, i) for i in range(16)])


def nt_dot(a, b):
    return lax.dot_general(a, b, (((1,), (1,)), ((), ())), preferred_element_type=F32)


def attend_kernel(group_ref, rows_ref, bias_ref, *refs):
    prompt_refs, out_ref, order_ref = refs[:4], refs[4], refs[5]
    low_half = lax.broadcasted_iota(jnp.int32, (QL, 128), 1) < 64
    out_ref[...] = jnp.zeros_like(out_ref)
    count = jnp.int32(0)
    for i in range(16):
        order_ref[count] = jnp.int32(i)
        count = count + (group_ref[i] >= 0).astype(jnp.int32)

    def one_request(i):
        src = i // RQ
        row = pl.multiple_of((i % RQ) * QL, QL)
        group = group_ref[i]
        query = rows_ref[src, pl.ds(row, QL), :]
        zero = jnp.zeros_like(query)
        both = jnp.concatenate(
            [jnp.where(low_half, query, zero), jnp.where(low_half, zero, query)], axis=0
        )
        own_key = rows_ref[src, pl.ds(pl.multiple_of(NROW + row, QL), QL), :]
        own_value = rows_ref[src, pl.ds(pl.multiple_of(2 * NROW + row, QL), QL), :]
        parts = [nt_dot(both, own_key)]
        values = [own_value]
        for piece in range(4):
            start = pl.multiple_of(group * 256, 256)
            key = prompt_refs[piece][pl.ds(start, 128), :]
            values.append(prompt_refs[piece][pl.ds(pl.multiple_of(start + 128, 128), 128), :])
            bias = bias_ref[group, :, piece * 128 : (piece + 1) * 128]
            parts.append(nt_dot(both, key) + bias)
        top = jnp.max(parts[0], axis=-1, keepdims=True)
        wide = jnp.maximum(jnp.maximum(parts[1], parts[2]), jnp.maximum(parts[3], parts[4]))
        top = jnp.maximum(top, jnp.max(wide, axis=-1, keepdims=True))
        weights = [jnp.exp(part - top) for part in parts]
        wide = (weights[1] + weights[2]) + (weights[3] + weights[4])
        total = jnp.sum(weights[0], axis=-1, keepdims=True) + jnp.sum(wide, axis=-1, keepdims=True)
        mixed = jnp.zeros((2 * QL, 128), F32)
        for weight, value in zip(weights, values):
            mixed = mixed + jnp.dot(weight.astype(BF), value, preferred_element_type=F32)
        mixed = mixed / total
        return jnp.where(low_half, mixed[:QL], mixed[QL:]).astype(BF)

    def some_requests(step, carry):
        places = [4 * step + j for j in range(4)]
        picked = [order_ref[jnp.where(place < count, place, 4 * step)] for place in places]
        results = [one_request(i) for i in picked]
        for j, result in zip(picked, results):
            out_ref[j // RQ, pl.ds(pl.multiple_of((j % RQ) * QL, QL), QL), :] = result
        return carry

    lax.fori_loop(0, (count + 3) // 4, some_requests, 0)


def attend(groups, rows, prompt, bias):
    return pl.pallas_call(
        attend_kernel,
        out_shape=jax.ShapeDtypeStruct((4, NROW, 128), BF),
        in_specs=[
            pl.BlockSpec(memory_space=pltpu.SMEM),
        ]
        + [pl.BlockSpec(memory_space=pltpu.VMEM)] * 6,
        out_specs=pl.BlockSpec(memory_space=pltpu.VMEM),
        scratch_shapes=[pltpu.SMEM((17,), jnp.int32)],
        compiler_params=pltpu.CompilerParams(vmem_limit_bytes=16 << 20),
        cost_estimate=pl.CostEstimate(flops=1000, bytes_accessed=1000, transcendentals=0),
        name="attend",
    )(groups, rows, bias, *prompt)


def match_kernel(need_ref, first_ref, last_ref, query_ref, docs_ref, pick_ref, out_ref, sims_ref, best_ref, term_ref):
    best_ref[...] = jnp.zeros_like(best_ref)
    token = lax.broadcasted_iota(jnp.int32, (DT, 128), 0)

    def one_holder(z, carry):
        base = z * 4
        any_need = need_ref[base] + need_ref[base + 1] + need_ref[base + 2] + need_ref[base + 3]

        @pl.when(any_need > 0)
        def _():
            vectors = docs_ref[pl.ds(pl.multiple_of(z * DT, DT), DT), :]
            sims_ref[...] = nt_dot(vectors, query_ref[...])

            def one_doc(k, inner):
                doc = base + k

                @pl.when(need_ref[doc] > 0)
                def _():
                    inside = (token >= first_ref[doc]) & (token < last_ref[doc])
                    tops = []
                    for col in range(8):
                        block = sims_ref[:, col * 128 : (col + 1) * 128]
                        tops.append(jnp.max(jnp.where(inside, block, -1e30), axis=0, keepdims=True))
                    best_ref[doc] = jnp.concatenate(tops, axis=0)

                return inner

            lax.fori_loop(0, 4, one_doc, 0)

        return carry

    lax.fori_loop(0, 16, one_holder, 0)
    lane = lax.broadcasted_iota(jnp.int32, (128, 128), 0)
    request = lax.broadcasted_iota(jnp.int32, (128, 128), 1)
    member = (lane // 32 == request // RQ).astype(F32)
    sums = jnp.dot(
        best_ref[...].reshape(512, 128), member, preferred_element_type=F32, precision=lax.Precision.HIGHEST
    ).reshape(64, 8, 128)
    head = lax.broadcasted_iota(jnp.int32, (64, 8, 128), 1)
    request = lax.broadcasted_iota(jnp.int32, (64, 8, 128), 2)
    per_doc = jnp.sum(jnp.where(head // 2 == request % RQ, sums, 0.0), axis=1)
    doc_row = lax.broadcasted_iota(jnp.int32, (64, 128), 0)
    for c in range(NC):
        hit = doc_row == pick_ref[c : c + 1, :]
        term_ref[c : c + 1, :] = jnp.sum(jnp.where(hit, per_doc, 0.0), axis=0, keepdims=True)
    for i in range(32):
        out_ref[i] = term_ref[...]


def match(need, first, last, queries, docs, pick):
    return pl.pallas_call(
        match_kernel,
        out_shape=jax.ShapeDtypeStruct((32, NC, 128), F32),
        in_specs=[pl.BlockSpec(memory_space=pltpu.SMEM)] * 3 + [pl.BlockSpec(memory_space=pltpu.VMEM)] * 3,
        out_specs=pl.BlockSpec(memory_space=pltpu.VMEM),
        scratch_shapes=[pltpu.VMEM((DT, 1024), F32), pltpu.VMEM((64, 8, 128), F32), pltpu.VMEM((NC, 128), F32)],
        compiler_params=pltpu.CompilerParams(vmem_limit_bytes=16 << 20),
        cost_estimate=pl.CostEstimate(flops=1000, bytes_accessed=1000, transcendentals=0),
        name="match",
    )(need, first, last, queries, docs, pick)


def vmem_call(body, out_shape, name, smem=0):
    def call(*args):
        spaces = [pltpu.SMEM] * smem + [pltpu.VMEM] * (len(args) - smem)
        return pl.pallas_call(
            body,
            out_shape=out_shape,
            in_specs=[pl.BlockSpec(memory_space=space) for space in spaces],
            out_specs=jax.tree.map(lambda _: pl.BlockSpec(memory_space=pltpu.VMEM), out_shape),
            compiler_params=pltpu.CompilerParams(vmem_limit_bytes=16 << 20),
            cost_estimate=pl.CostEstimate(flops=1000, bytes_accessed=1000, transcendentals=0),
            name=name,
        )(*args)

    return call


def total_kernel(place_ref, terms_ref, out_ref):
    total = terms_ref[0]
    for i in range(1, 32):
        total = total + terms_ref[i]
    lane = lax.broadcasted_iota(jnp.int32, (8, 128), 1)
    row = lax.broadcasted_iota(jnp.int32, (8, 128), 0)
    wanted = (lane == place_ref[0] * RQ + row).astype(F32)
    picked = lax.dot_general(
        wanted, total, (((1,), (1,)), ((), ())), preferred_element_type=F32, precision=lax.Precision.HIGHEST
    )
    out_ref[...] = picked[:RQ]


def dense_kernel(context_ref, token_ref, gain_ref, *refs):
    held, first_ref, terms_ref, scratch, sems = refs[:3], refs[3], refs[4], refs[5:8], refs[8]
    copies = [pltpu.make_async_copy(held[i], scratch[i], sems.at[i]) for i in range(3)]
    for copy in copies:
        copy.start()
    w_out_ref, inner_ref, outer_ref = scratch
    context = jnp.concatenate([context_ref[h] for h in range(8)], axis=1)
    copies[0].wait()
    attn = token_ref[...].astype(F32) + jnp.dot(context, w_out_ref[...], preferred_element_type=F32)
    first = layer_norm(attn, gain_ref[...]).astype(BF)
    first_ref[...] = first
    copies[1].wait()
    inner = jnp.dot(first, inner_ref[...], preferred_element_type=F32)
    active = (0.5 * inner * (1.0 + lax.erf(inner * (0.5**0.5)))).astype(BF)
    copies[2].wait()
    total = jnp.dot(active, outer_ref[...], preferred_element_type=F32)
    terms_ref[...] = total.astype(BF).reshape(8, 32, 1024)


def dense(context, tokens, gain, weights):
    return pl.pallas_call(
        dense_kernel,
        out_shape=(jax.ShapeDtypeStruct((NROW, 1024), BF), jax.ShapeDtypeStruct((8, 32, 1024), BF)),
        in_specs=[pl.BlockSpec(memory_space=pltpu.VMEM)] * 3 + [pl.BlockSpec(memory_space=pl.ANY)] * 3,
        out_specs=(pl.BlockSpec(memory_space=pltpu.VMEM), pl.BlockSpec(memory_space=pltpu.VMEM)),
        scratch_shapes=[pltpu.VMEM(w.shape, w.dtype) for w in weights] + [pltpu.SemaphoreType.DMA((3,))],
        compiler_params=pltpu.CompilerParams(vmem_limit_bytes=52 << 20),
        cost_estimate=pl.CostEstimate(flops=1000, bytes_accessed=1000, transcendentals=0),
        name="dense",
    )(context, tokens, gain, *weights)


def embed_kernel(place_ref, first_ref, terms_ref, gain_ref, w_project_ref, out_ref):
    start = pl.multiple_of(place_ref[0] * 32, 32)
    total = first_ref[pl.ds(start, 32), :].astype(F32)
    for h in range(8):
        total = total + terms_ref[h].astype(F32)
    second = layer_norm(total, gain_ref[...]).astype(BF)
    projected = jnp.dot(second, w_project_ref[...], preferred_element_type=F32)
    scale = lax.rsqrt(jnp.sum(projected * projected, axis=-1, keepdims=True) + 1e-06)
    embed = (projected * scale).astype(BF)
    for i in range(32):
        out_ref[i] = embed


def per_device(
    tokens,
    w_query,
    w_key,
    w_value,
    w_out,
    norm1_gain,
    w_inner,
    w_outer,
    norm2_gain,
    w_project,
    key_pages,
    value_pages,
    page_table,
    prompt_lengths,
    request_group,
    doc_vectors,
    doc_lengths,
    candidates,
):
    my_y = lax.axis_index("y")
    my_head = lax.axis_index(HEAD)
    token_rows = tokens.reshape(NROW, 1024)

    pages = jnp.concatenate([key_pages.reshape(128, 128), value_pages.reshape(128, 128)], axis=0)
    pages_q = spread(pages, "q", 4)

    w_out_all = lax.all_gather(w_out, HEAD, axis=0, tiled=True)

    query = jnp.dot(token_rows, w_query, preferred_element_type=F32).astype(BF) * BF(0.125)
    own_key = jnp.dot(token_rows, w_key, preferred_element_type=F32).astype(BF)
    own_value = jnp.dot(token_rows, w_value, preferred_element_type=F32).astype(BF)
    ids = jnp.concatenate([candidates // 64, candidates % 64, request_group[:, None]], axis=1)
    ids = jnp.pad(ids.astype(BF), ((0, 12), (0, 128 - 33)))
    rows = jnp.concatenate([query, own_key, own_value, ids], axis=0)
    rows = lax.all_gather(rows, "y", axis=0, tiled=True)
    pages_q, rows = lax.optimization_barrier((pages_q, rows))
    pages_q = pages_q.reshape(1024, 128)
    ahead_two = from_ahead(pages_q, 2)
    prompt = [pages_q, from_ahead(pages_q, 1), ahead_two, from_ahead(pages_q, -1)]

    doc_vectors, page_table, pages_q = lax.optimization_barrier((doc_vectors, page_table, pages_q))
    doc_rows = jnp.pad(doc_lengths.astype(BF), ((0, DPAD - DT - 1), (0, 124)))
    doc_block = jnp.concatenate([doc_vectors, doc_rows], axis=0)
    docs = lax.all_gather(doc_block, ("q", "r"), axis=0, tiled=True)

    rows = rows.reshape(4, XROW, 128)
    got = rows[:, 3 * NROW : 3 * NROW + RQ, :33].reshape(16, 33).astype(jnp.int32)
    groups = jnp.where(got[:, 32] // 4 == my_y, got[:, 32] % 4, -1)
    pick = jnp.where(got[:, :16] == my_head * 4 + my_y, got[:, 16:32], -1)

    table = lax.dynamic_slice(page_table, (my_y * 32,), (32,)).reshape(4, 8)
    lengths = lax.dynamic_slice(prompt_lengths, (my_y * 4,), (4,))
    page_ids = (my_y * 32 + jnp.arange(32, dtype=jnp.int32)).reshape(4, 8)
    slot = jnp.sum(
        jnp.where(table[:, None, :] == page_ids[:, :, None], jnp.arange(8, dtype=jnp.int32), 0), axis=-1
    )
    position = slot[:, :, None] * 64 + jnp.arange(64, dtype=jnp.int32)
    bias = jnp.where(position < lengths[:, None, None], 0.0, -1e30).astype(F32).reshape(4, 4, 128)
    ahead = (lax.axis_index("r") + jnp.arange(4, dtype=jnp.int32)) % 4
    turn = ahead[:, None] == jnp.arange(4, dtype=jnp.int32)
    bias = jnp.sum(jnp.where(turn[None, :, :, None], bias[:, None], 0.0), axis=2).reshape(4, 1, 512)

    mixed = attend(groups, rows, prompt, bias)
    back = lax.all_to_all(mixed, "y", 0, 0, tiled=True)
    context = jnp.sum(back.astype(F32), axis=0).astype(BF)
    context = lax.all_gather(context, HEAD, axis=0, tiled=False)
    first, terms = dense(context, token_rows, norm1_gain[None], [w_out_all, w_inner, w_outer])
    terms = lax.all_to_all(terms, HEAD, 0, 0, tiled=True)
    embed = vmem_call(embed_kernel, jax.ShapeDtypeStruct((32, 32, 128), BF), "embed", 1)(
        my_head.reshape(1), first, terms, norm2_gain[None], w_project
    )

    queries = lax.all_to_all(embed, HEAD + ("y",), 0, 0, tiled=True)
    own = lax.dynamic_slice(queries.reshape(8, 4, 32, 128), (0, my_y, 0, 0), (8, 1, 32, 128))
    embedded = own.reshape(RQ, QL, 128)

    docs = lax.optimization_barrier((docs, embed))[0].reshape(16, DPAD, 128)
    doc_len = docs[:, DT, :4].astype(jnp.int32)
    docs = docs[:, :DT].reshape(16 * DT, 128)
    doc_last = jnp.cumsum(doc_len, axis=1)
    doc_first = doc_last - doc_len
    need = jnp.any(
        pick.reshape(1, 256) == jnp.arange(64, dtype=jnp.int32)[:, None], axis=1
    ).astype(jnp.int32)
    pick_lanes = jnp.pad(pick.T, ((0, 0), (0, 112)), constant_values=-1)
    terms = match(
        need, doc_first.reshape(64), doc_last.reshape(64), queries.reshape(1024, 128), docs, pick_lanes
    )
    terms = lax.all_to_all(terms, HEAD + ("y",), 0, 0, tiled=True)
    scores = vmem_call(total_kernel, jax.ShapeDtypeStruct((RQ, NC), F32), "total", 1)(my_y.reshape(1), terms)
    return (embedded, scores)


def solution(mesh):
    fine = Mesh(mesh.devices.reshape(4, 2, 4, 4, 4), HEAD + SHARD)
    in_specs = (
        P(SHARD, None, None),
        P(None, HEAD),
        P(None, HEAD),
        P(None, HEAD),
        P(HEAD, None),
        P(),
        P(None, HEAD),
        P(HEAD, None),
        P(),
        P(),
        P(SHARD, None, HEAD),
        P(SHARD, None, HEAD),
        P(),
        P(),
        P(SHARD),
        P(HEAD + SHARD, None),
        P(HEAD + SHARD, None),
        P(SHARD, None),
    )
    out_specs = (P(SHARD, None, None), P(SHARD, None))
    return jax.shard_map(per_device, mesh=fine, in_specs=in_specs, out_specs=out_specs, check_vma=False)
```

```python
import jax
import jax.numpy as jnp
from jax import lax
from jax.experimental import pallas as pl
from jax.experimental.pallas import tpu as pltpu
from jax.sharding import Mesh, PartitionSpec as P

HEAD = ("x", "c")
SHARD = ("y", "q", "r")
RQ = 4
QL = 64
NC = 16
NROW = RQ * QL
DT = 256
DPAD = 272
XROW = 3 * NROW + 16
BF = jnp.bfloat16
F32 = jnp.float32


def layer_norm(values, norm_gain):
    row_mean = jnp.mean(values, axis=-1, keepdims=True)
    row_var = jnp.mean(jnp.square(values - row_mean), axis=-1, keepdims=True)
    return (values - row_mean) * lax.rsqrt(row_var + 1e-05) * norm_gain


def spread(block, axes, count):
    wide = jnp.broadcast_to(block[None], (count,) + block.shape)
    return lax.all_to_all(wide, axes, 0, 0, tiled=True).reshape((-1,) + block.shape[1:])


def from_ahead(block, step):
    return lax.ppermute(block, ("q", "r"), [((i + step) % 16, i) for i in range(16)])


def nt_dot(a, b):
    return lax.dot_general(a, b, (((1,), (1,)), ((), ())), preferred_element_type=F32)


def attend_kernel(group_ref, rows_ref, bias_ref, *refs):
    prompt_refs, out_ref, order_ref = refs[:4], refs[4], refs[5]
    low_half = lax.broadcasted_iota(jnp.int32, (QL, 128), 1) < 64
    out_ref[...] = jnp.zeros_like(out_ref)
    count = jnp.int32(0)
    for i in range(16):
        order_ref[count] = jnp.int32(i)
        count = count + (group_ref[i] >= 0).astype(jnp.int32)

    def one_request(i):
        src = i // RQ
        row = pl.multiple_of((i % RQ) * QL, QL)
        group = group_ref[i]
        query = rows_ref[src, pl.ds(row, QL), :]
        zero = jnp.zeros_like(query)
        both = jnp.concatenate(
            [jnp.where(low_half, query, zero), jnp.where(low_half, zero, query)], axis=0
        )
        own_key = rows_ref[src, pl.ds(pl.multiple_of(NROW + row, QL), QL), :]
        own_value = rows_ref[src, pl.ds(pl.multiple_of(2 * NROW + row, QL), QL), :]
        parts = [nt_dot(both, own_key)]
        values = [own_value]
        for piece in range(4):
            start = pl.multiple_of(group * 256, 256)
            key = prompt_refs[piece][pl.ds(start, 128), :]
            values.append(prompt_refs[piece][pl.ds(pl.multiple_of(start + 128, 128), 128), :])
            bias = bias_ref[group, :, piece * 128 : (piece + 1) * 128]
            parts.append(nt_dot(both, key) + bias)
        top = jnp.max(parts[0], axis=-1, keepdims=True)
        wide = jnp.maximum(jnp.maximum(parts[1], parts[2]), jnp.maximum(parts[3], parts[4]))
        top = jnp.maximum(top, jnp.max(wide, axis=-1, keepdims=True))
        weights = [jnp.exp(part - top) for part in parts]
        wide = (weights[1] + weights[2]) + (weights[3] + weights[4])
        total = jnp.sum(weights[0], axis=-1, keepdims=True) + jnp.sum(wide, axis=-1, keepdims=True)
        mixed = jnp.zeros((2 * QL, 128), F32)
        for weight, value in zip(weights, values):
            mixed = mixed + jnp.dot(weight.astype(BF), value, preferred_element_type=F32)
        mixed = mixed / total
        return jnp.where(low_half, mixed[:QL], mixed[QL:]).astype(BF)

    def some_requests(step, carry):
        places = [4 * step + j for j in range(4)]
        picked = [order_ref[jnp.where(place < count, place, 4 * step)] for place in places]
        results = [one_request(i) for i in picked]
        for j, result in zip(picked, results):
            out_ref[j // RQ, pl.ds(pl.multiple_of((j % RQ) * QL, QL), QL), :] = result
        return carry

    lax.fori_loop(0, (count + 3) // 4, some_requests, 0)


def attend(groups, rows, prompt, bias):
    return pl.pallas_call(
        attend_kernel,
        out_shape=jax.ShapeDtypeStruct((4, NROW, 128), BF),
        in_specs=[
            pl.BlockSpec(memory_space=pltpu.SMEM),
        ]
        + [pl.BlockSpec(memory_space=pltpu.VMEM)] * 6,
        out_specs=pl.BlockSpec(memory_space=pltpu.VMEM),
        scratch_shapes=[pltpu.SMEM((17,), jnp.int32)],
        compiler_params=pltpu.CompilerParams(vmem_limit_bytes=16 << 20),
        cost_estimate=pl.CostEstimate(flops=1000, bytes_accessed=1000, transcendentals=0),
        name="attend",
    )(groups, rows, bias, *prompt)


def match_kernel(need_ref, first_ref, last_ref, query_ref, docs_ref, pick_ref, out_ref, sims_ref, best_ref, term_ref):
    best_ref[...] = jnp.zeros_like(best_ref)
    token = lax.broadcasted_iota(jnp.int32, (DT, 128), 0)

    def one_holder(z, carry):
        base = z * 4
        any_need = need_ref[base] + need_ref[base + 1] + need_ref[base + 2] + need_ref[base + 3]

        @pl.when(any_need > 0)
        def _():
            vectors = docs_ref[pl.ds(pl.multiple_of(z * DT, DT), DT), :]
            sims_ref[...] = nt_dot(vectors, query_ref[...])

            def one_doc(k, inner):
                doc = base + k

                @pl.when(need_ref[doc] > 0)
                def _():
                    inside = (token >= first_ref[doc]) & (token < last_ref[doc])
                    tops = []
                    for col in range(8):
                        block = sims_ref[:, col * 128 : (col + 1) * 128]
                        tops.append(jnp.max(jnp.where(inside, block, -1e30), axis=0, keepdims=True))
                    best_ref[doc] = jnp.concatenate(tops, axis=0)

                return inner

            lax.fori_loop(0, 4, one_doc, 0)

        return carry

    lax.fori_loop(0, 16, one_holder, 0)
    lane = lax.broadcasted_iota(jnp.int32, (128, 128), 0)
    request = lax.broadcasted_iota(jnp.int32, (128, 128), 1)
    member = (lane // 32 == request // RQ).astype(F32)
    sums = jnp.dot(
        best_ref[...].reshape(512, 128), member, preferred_element_type=F32, precision=lax.Precision.HIGHEST
    ).reshape(64, 8, 128)
    head = lax.broadcasted_iota(jnp.int32, (64, 8, 128), 1)
    request = lax.broadcasted_iota(jnp.int32, (64, 8, 128), 2)
    per_doc = jnp.sum(jnp.where(head // 2 == request % RQ, sums, 0.0), axis=1)
    doc_row = lax.broadcasted_iota(jnp.int32, (64, 128), 0)
    for c in range(NC):
        hit = doc_row == pick_ref[c : c + 1, :]
        term_ref[c : c + 1, :] = jnp.sum(jnp.where(hit, per_doc, 0.0), axis=0, keepdims=True)
    for i in range(32):
        out_ref[i] = term_ref[...]


def match(need, first, last, queries, docs, pick):
    return pl.pallas_call(
        match_kernel,
        out_shape=jax.ShapeDtypeStruct((32, NC, 128), F32),
        in_specs=[pl.BlockSpec(memory_space=pltpu.SMEM)] * 3 + [pl.BlockSpec(memory_space=pltpu.VMEM)] * 3,
        out_specs=pl.BlockSpec(memory_space=pltpu.VMEM),
        scratch_shapes=[pltpu.VMEM((DT, 1024), F32), pltpu.VMEM((64, 8, 128), F32), pltpu.VMEM((NC, 128), F32)],
        compiler_params=pltpu.CompilerParams(vmem_limit_bytes=16 << 20),
        cost_estimate=pl.CostEstimate(flops=1000, bytes_accessed=1000, transcendentals=0),
        name="match",
    )(need, first, last, queries, docs, pick)


def vmem_call(body, out_shape, name, smem=0):
    def call(*args):
        spaces = [pltpu.SMEM] * smem + [pltpu.VMEM] * (len(args) - smem)
        return pl.pallas_call(
            body,
            out_shape=out_shape,
            in_specs=[pl.BlockSpec(memory_space=space) for space in spaces],
            out_specs=jax.tree.map(lambda _: pl.BlockSpec(memory_space=pltpu.VMEM), out_shape),
            compiler_params=pltpu.CompilerParams(vmem_limit_bytes=16 << 20),
            cost_estimate=pl.CostEstimate(flops=1000, bytes_accessed=1000, transcendentals=0),
            name=name,
        )(*args)

    return call


def total_kernel(place_ref, terms_ref, out_ref):
    total = terms_ref[0]
    for i in range(1, 32):
        total = total + terms_ref[i]
    lane = lax.broadcasted_iota(jnp.int32, (8, 128), 1)
    row = lax.broadcasted_iota(jnp.int32, (8, 128), 0)
    wanted = (lane == place_ref[0] * RQ + row).astype(F32)
    picked = lax.dot_general(
        wanted, total, (((1,), (1,)), ((), ())), preferred_element_type=F32, precision=lax.Precision.HIGHEST
    )
    out_ref[...] = picked[:RQ]


def dense_kernel(context_ref, token_ref, gain_ref, *refs):
    held, first_ref, terms_ref, scratch, sems = refs[:3], refs[3], refs[4], refs[5:8], refs[8]
    copies = [pltpu.make_async_copy(held[i], scratch[i], sems.at[i]) for i in range(3)]
    for copy in copies:
        copy.start()
    w_out_ref, inner_ref, outer_ref = scratch
    context = jnp.concatenate([context_ref[h] for h in range(8)], axis=1)
    copies[0].wait()
    attn = token_ref[...].astype(F32) + jnp.dot(context, w_out_ref[...], preferred_element_type=F32)
    first = layer_norm(attn, gain_ref[...]).astype(BF)
    first_ref[...] = first
    copies[1].wait()
    inner = jnp.dot(first, inner_ref[...], preferred_element_type=F32)
    active = (0.5 * inner * (1.0 + lax.erf(inner * (0.5**0.5)))).astype(BF)
    copies[2].wait()
    total = jnp.dot(active, outer_ref[...], preferred_element_type=F32)
    terms_ref[...] = total.astype(BF).reshape(8, 32, 1024)


def dense(context, tokens, gain, weights):
    return pl.pallas_call(
        dense_kernel,
        out_shape=(jax.ShapeDtypeStruct((NROW, 1024), BF), jax.ShapeDtypeStruct((8, 32, 1024), BF)),
        in_specs=[pl.BlockSpec(memory_space=pltpu.VMEM)] * 3 + [pl.BlockSpec(memory_space=pl.ANY)] * 3,
        out_specs=(pl.BlockSpec(memory_space=pltpu.VMEM), pl.BlockSpec(memory_space=pltpu.VMEM)),
        scratch_shapes=[pltpu.VMEM(w.shape, w.dtype) for w in weights] + [pltpu.SemaphoreType.DMA((3,))],
        compiler_params=pltpu.CompilerParams(vmem_limit_bytes=52 << 20),
        cost_estimate=pl.CostEstimate(flops=1000, bytes_accessed=1000, transcendentals=0),
        name="dense",
    )(context, tokens, gain, *weights)


def embed_kernel(place_ref, first_ref, terms_ref, gain_ref, w_project_ref, out_ref):
    start = pl.multiple_of(place_ref[0] * 32, 32)
    total = first_ref[pl.ds(start, 32), :].astype(F32)
    for h in range(8):
        total = total + terms_ref[h].astype(F32)
    second = layer_norm(total, gain_ref[...]).astype(BF)
    projected = jnp.dot(second, w_project_ref[...], preferred_element_type=F32)
    scale = lax.rsqrt(jnp.sum(projected * projected, axis=-1, keepdims=True) + 1e-06)
    embed = (projected * scale).astype(BF)
    for i in range(32):
        out_ref[i] = embed


def per_device(
    tokens,
    w_query,
    w_key,
    w_value,
    w_out,
    norm1_gain,
    w_inner,
    w_outer,
    norm2_gain,
    w_project,
    key_pages,
    value_pages,
    page_table,
    prompt_lengths,
    request_group,
    doc_vectors,
    doc_lengths,
    candidates,
):
    my_y = lax.axis_index("y")
    my_head = lax.axis_index(HEAD)
    token_rows = tokens.reshape(NROW, 1024)

    pages = jnp.concatenate([key_pages.reshape(128, 128), value_pages.reshape(128, 128)], axis=0)
    pages_q = spread(pages, "q", 4)

    w_out_all = lax.all_gather(w_out, HEAD, axis=0, tiled=True)

    query = jnp.dot(token_rows, w_query, preferred_element_type=F32).astype(BF) * BF(0.125)
    own_key = jnp.dot(token_rows, w_key, preferred_element_type=F32).astype(BF)
    own_value = jnp.dot(token_rows, w_value, preferred_element_type=F32).astype(BF)
    ids = jnp.concatenate([candidates // 64, candidates % 64, request_group[:, None]], axis=1)
    ids = jnp.pad(ids.astype(BF), ((0, 12), (0, 128 - 33)))
    rows = jnp.concatenate([query, own_key, own_value, ids], axis=0)
    rows = lax.all_gather(rows, "y", axis=0, tiled=True)
    pages_q, rows = lax.optimization_barrier((pages_q, rows))
    pages_q = pages_q.reshape(1024, 128)
    pairs = [((i + 2 if i % 2 == 0 else i - 2) % 16, i) for i in range(16)]
    ahead_two = lax.ppermute(pages_q, ("q", "r"), pairs)
    prompt = [pages_q, from_ahead(pages_q, 1), ahead_two, from_ahead(pages_q, -1)]

    doc_vectors, page_table, pages_q = lax.optimization_barrier((doc_vectors, page_table, pages_q))
    doc_rows = jnp.pad(doc_lengths.astype(BF), ((0, DPAD - DT - 1), (0, 124)))
    doc_block = jnp.concatenate([doc_vectors, doc_rows], axis=0)
    docs = lax.all_gather(doc_block, ("q", "r"), axis=0, tiled=True)

    rows = rows.reshape(4, XROW, 128)
    got = rows[:, 3 * NROW : 3 * NROW + RQ, :33].reshape(16, 33).astype(jnp.int32)
    groups = jnp.where(got[:, 32] // 4 == my_y, got[:, 32] % 4, -1)
    pick = jnp.where(got[:, :16] == my_head * 4 + my_y, got[:, 16:32], -1)

    table = lax.dynamic_slice(page_table, (my_y * 32,), (32,)).reshape(4, 8)
    lengths = lax.dynamic_slice(prompt_lengths, (my_y * 4,), (4,))
    page_ids = (my_y * 32 + jnp.arange(32, dtype=jnp.int32)).reshape(4, 8)
    slot = jnp.sum(
        jnp.where(table[:, None, :] == page_ids[:, :, None], jnp.arange(8, dtype=jnp.int32), 0), axis=-1
    )
    position = slot[:, :, None] * 64 + jnp.arange(64, dtype=jnp.int32)
    bias = jnp.where(position < lengths[:, None, None], 0.0, -1e30).astype(F32).reshape(4, 4, 128)
    ahead = (lax.axis_index("r") + jnp.arange(4, dtype=jnp.int32)) % 4
    turn = ahead[:, None] == jnp.arange(4, dtype=jnp.int32)
    bias = jnp.sum(jnp.where(turn[None, :, :, None], bias[:, None], 0.0), axis=2).reshape(4, 1, 512)

    mixed = attend(groups, rows, prompt, bias)
    back = lax.all_to_all(mixed, "y", 0, 0, tiled=True)
    context = jnp.sum(back.astype(F32), axis=0).astype(BF)
    context = lax.all_gather(context, HEAD, axis=0, tiled=False)
    first, terms = dense(context, token_rows, norm1_gain[None], [w_out_all, w_inner, w_outer])
    terms = lax.all_to_all(terms, HEAD, 0, 0, tiled=True)
    embed = vmem_call(embed_kernel, jax.ShapeDtypeStruct((32, 32, 128), BF), "embed", 1)(
        my_head.reshape(1), first, terms, norm2_gain[None], w_project
    )

    queries = lax.all_to_all(embed, HEAD + ("y",), 0, 0, tiled=True)
    own = lax.dynamic_slice(queries.reshape(8, 4, 32, 128), (0, my_y, 0, 0), (8, 1, 32, 128))
    embedded = own.reshape(RQ, QL, 128)

    docs = lax.optimization_barrier((docs, embed))[0].reshape(16, DPAD, 128)
    doc_len = docs[:, DT, :4].astype(jnp.int32)
    docs = docs[:, :DT].reshape(16 * DT, 128)
    doc_last = jnp.cumsum(doc_len, axis=1)
    doc_first = doc_last - doc_len
    need = jnp.any(
        pick.reshape(1, 256) == jnp.arange(64, dtype=jnp.int32)[:, None], axis=1
    ).astype(jnp.int32)
    pick_lanes = jnp.pad(pick.T, ((0, 0), (0, 112)), constant_values=-1)
    terms = match(
        need, doc_first.reshape(64), doc_last.reshape(64), queries.reshape(1024, 128), docs, pick_lanes
    )
    terms = lax.all_to_all(terms, HEAD + ("y",), 0, 0, tiled=True)
    scores = vmem_call(total_kernel, jax.ShapeDtypeStruct((RQ, NC), F32), "total", 1)(my_y.reshape(1), terms)
    return (embedded, scores)


def solution(mesh):
    fine = Mesh(mesh.devices.reshape(4, 2, 4, 4, 4), HEAD + SHARD)
    in_specs = (
        P(SHARD, None, None),
        P(None, HEAD),
        P(None, HEAD),
        P(None, HEAD),
        P(HEAD, None),
        P(),
        P(None, HEAD),
        P(HEAD, None),
        P(),
        P(),
        P(SHARD, None, HEAD),
        P(SHARD, None, HEAD),
        P(),
        P(),
        P(SHARD),
        P(HEAD + SHARD, None),
        P(HEAD + SHARD, None),
        P(SHARD, None),
    )
    out_specs = (P(SHARD, None, None), P(SHARD, None))
    return jax.shard_map(per_device, mesh=fine, in_specs=in_specs, out_specs=out_specs, check_vma=False)
```
